32 devices in a mesh: seq: 2 (over x), mp: 16 (over z, y, core).
Axes of the slice: x: 2, y: 2, z: 4, core: 2. Of those that a mesh axis runs over, the one named last changes fastest.
Arguments:
- tokens: bfloat16 [512, 4, 1536], P('seq'), may hold values from -6 to 6
- target: bfloat16 [512, 4, 1536], P(('seq', 'mp')), may hold values from -6 to 6
- lengths: int32 [4], replicated, may hold values from 128 to 512, as said below
- routes: int32 [512, 4, 6], P(('seq', 'mp')), may hold values from 0 to 15, all different within a row; in each aligned block of 64 rows (0 to 63, 64 to 127, ..., all dimensions but the last counted through in order) at most 48 rows name the same one
- route_weight: float32 [512, 4, 6], P(('seq', 'mp')), may hold values from 0.1 to 0.4
- in_gain: bfloat16 [1536], P(('seq', 'mp')), may hold values from 0.5 to 1.5
- gate_proj: bfloat16 [1536, 3072], P(None, 'mp'), may hold values from -0.15625 to 0.15625
- value_proj: bfloat16 [1536, 3072], P(None, 'mp'), may hold values from -0.15625 to 0.15625
- state_proj: bfloat16 [1536, 256], P(('seq', 'mp')), may hold values from -0.078125 to 0.078125
- step_proj: bfloat16 [1536, 48], P(None, 'mp'), may hold values from -0.15625 to 0.15625
- conv_value: float32 [4, 3072], P(None, 'mp'), may hold values from -3 to 3
- conv_value_bias: float32 [3072], P('mp'), may hold values from -3 to 3
- conv_state: bfloat16 [256, 4], P(('seq', 'mp')), may hold values from -3 to 3
- conv_state_bias: bfloat16 [256], P(('seq', 'mp')), may hold values from -3 to 3
- step_bias: float32 [48], P('mp'), may hold values from -4 to -1
- decay_log: float32 [48], P('mp'), may hold values from -8 to -1
- skip_gain: float32 [48], P('mp'), may hold values from 0.5 to 2
- mixer_gain: float32 [3072], P('mp'), may hold values from 0.5 to 1.5
- out_proj: bfloat16 [3072, 1536], P('mp'), may hold values from -0.109375 to 0.109375
- ffn_gain: bfloat16 [1536], P(('seq', 'mp')), may hold values from 0.5 to 1.5
- shared_gate: bfloat16 [1536, 1024], P(('seq', 'mp')), may hold values from -0.15625 to 0.15625
- shared_up: bfloat16 [1536, 1024], P(('seq', 'mp')), may hold values from -0.15625 to 0.15625
- shared_down: bfloat16 [1024, 1536], P(('seq', 'mp')), may hold values from -0.1875 to 0.1875
- expert_gate: bfloat16 [16, 1536, 512], P('mp'), may hold values from -0.15625 to 0.15625
- routed_up_weights: bfloat16 [16, 1536, 512], P('mp'), may hold values from -0.15625 to 0.15625
- expert_down: bfloat16 [16, 512, 1536], P('mp'), may hold values from -0.25 to 0.25
Outputs:
- block_out: bfloat16 [512, 4, 1536], P(('seq', 'mp'))
- tokens_grad: float32 [512, 4, 1536], P(('seq', 'mp'))
- in_gain_grad: float32 [1536], P(('seq', 'mp'))
- gate_proj_grad: float32 [1536, 3072], P(None, 'mp')
- value_proj_grad: float32 [1536, 3072], P(None, 'mp')
- state_proj_grad: float32 [1536, 256], P(('seq', 'mp'))
- step_proj_grad: float32 [1536, 48], P(None, 'mp')
- conv_value_grad: float32 [4, 3072], P(None, 'mp')
- conv_value_bias_grad: float32 [3072], P('mp')
- conv_state_grad: float32 [256, 4], P(('seq', 'mp'))
- conv_state_bias_grad: float32 [256], P(('seq', 'mp'))
- step_bias_grad: float32 [48], P('mp')
- decay_log_grad: float32 [48], P('mp')
- skip_gain_grad: float32 [48], P('mp')
- mixer_gain_grad: float32 [3072], P('mp')
- out_proj_grad: float32 [3072, 1536], P('mp')
- ffn_gain_grad: float32 [1536], P(('seq', 'mp'))
- shared_gate_grad: float32 [1536, 1024], P(('seq', 'mp'))
- shared_up_grad: float32 [1536, 1024], P(('seq', 'mp'))
- shared_down_grad: float32 [1024, 1536], P(('seq', 'mp'))
- expert_gate_grad: float32 [16, 1536, 512], P('mp')
- expert_up_grad: float32 [16, 1536, 512], P('mp')
- expert_down_grad: float32 [16, 512, 1536], P('mp')
The draws below stay inside these ranges and needn't reach their ends.
Inputs may be any that keep to these rules, and one draw needn't show every extreme that they name: `routes`: each row names 6 different experts. In each aligned block of 64 rows (the rows of one device), no expert is named by more than 48 rows, a bound that some block reaches. `lengths`: some sequence has all 512 slots true.
All inputs are finite; a program needn't handle non-finite values.
Results may differ from the reference program's by a relative error of at most 0.018.
The reference program's roundings to bfloat16 on the way count: a program that leaves them out, or rounds other values in their place, can miss the bound.
Values may be sent and summed in bfloat16 or wider, within the bound.
No kernel may reach another device: no remote copies, remote signals or barrier semaphores. Data moves between devices by JAX's collectives and lax.ppermute only.
A program may use at most 192 MiB of HBM per device.

```python
import math
import jax
import jax.numpy as jnp
import numpy as np
from jax import lax

D = 1536
HEADS = 48
HEAD_DIM = 64
STATE = 128
CONV = 4
EXPERT_FF = 512
SHARED_FF = 1024
TOPK = 6
NSEQ = 4
SLOT_DEV = 256
INNER = 3072
EXPERTS = 16
SLOTS = 512
ROWS_MP = 64
CAP = 48


def draw_lengths(key, part):
    base_lengths = jax.random.randint(key, (NSEQ,), SLOTS // 4, SLOTS + 1)
    longest = jax.random.randint(jax.random.fold_in(key, 7), (), 0, NSEQ)
    return jnp.where(jnp.arange(NSEQ) == longest, SLOTS, base_lengths).astype(jnp.int32)


def levels(key, extent, cuts, least, largest):
    level, own = 1.0, jax.random.fold_in(key, 6)
    for axis_at, shards_of in cuts:
        steps = jnp.exp(jax.random.uniform(jax.random.fold_in(own, axis_at), (shards_of,), jnp.float32, least / len(cuts), largest / len(cuts)))
        level = level * jnp.repeat(steps, extent[axis_at] // shards_of).reshape([-1 if axis == axis_at else 1 for axis in range(len(extent))])
    return level


def deal_out(stream_key, own, number, rows, count, top, bound, skew):
    sequence = jax.random.permutation(stream_key, count)
    crowded, common = shares(count, rows * top, bound, skew, True), shares(count, rows * top, bound, skew, False)
    places = jnp.arange(count)

    def named(tallies, turn):
        used = int((tallies > 0).sum())
        fixed = max(1, used // 4)
        shifted = fixed + (places - fixed + turn * (used - fixed)) % max(1, count - fixed)
        return jnp.zeros((count,), jnp.int32).at[sequence[jnp.where(places < fixed, places, shifted)]].set(jnp.asarray(tallies, jnp.int32))

    tallies = jnp.where(number % 4 == 0, named(crowded, number // 4), named(common, number - number // 4 - 1))
    mixed = jax.random.permutation(jax.random.fold_in(own, 3), count)
    source_of, taker = mixed[0:count // 2 * 2:2], mixed[1:count // 2 * 2:2]
    margin = jnp.minimum(tallies[source_of] - 1, bound - tallies[taker]) // 2
    margin = jnp.where((source_of == sequence[0]) | (taker == sequence[0]) | (tallies[taker] == 0), 0, jnp.maximum(margin, 0))
    shifted = jax.random.randint(jax.random.fold_in(own, 4), (count // 2,), 0, 1 << 20) % (margin + 1)
    tallies = tallies.at[source_of].add(-shifted).at[taker].add(shifted)
    labels = jnp.searchsorted(jnp.cumsum(tallies), jnp.arange(rows * top), side="right").astype(jnp.int32)
    listing = labels.reshape(top, rows).T
    listing = listing[jax.random.permutation(jax.random.fold_in(own, 1), rows)]
    turn = jax.random.randint(jax.random.fold_in(own, 2), (rows, 1), 0, top)
    return jnp.take_along_axis(listing, (jnp.arange(top)[None, :] + turn) % top, axis=1)


def shares(number_of, total, limit, skew, full):
    loads = [(1 << 20) // math.isqrt(rank ** skew) + 1 for rank in range(1, number_of + 1)]
    largest = limit if full else min(limit, max(-(-total // number_of), total * loads[0] // sum(loads)))
    least = 1 if total - largest >= number_of - 1 else 0
    holding, spare = [largest] + [least] * (number_of - 1), total - largest - least * (number_of - 1)
    while spare > 0:
        free = [i for i in range(1, number_of) if holding[i] < largest] or [i for i in range(1, number_of) if holding[i] < limit]
        pool, budget = sum([loads[i] for i in free]), spare
        for i in free:
            more = min(limit - holding[i], max(1, budget * loads[i] // pool), spare)
            holding[i] = holding[i] + more
            spare = spare - more
    return np.array(holding)


def bell_draw(rng, extent, spread, most, cuts=(), held_as=jnp.bfloat16):
    drawn = jax.random.normal(rng, extent, jnp.float32) * spread
    if len(cuts) > 0:
        drawn = levels(rng, extent, cuts, -0.22, 0.18) * drawn
    return jnp.clip(drawn, min=-most, max=most).astype(held_as)


def setup_inputs(seed: int = 0) -> dict:
    arg_keys = jax.random.split(jax.random.key(seed), 27)
    tokens = bell_draw(arg_keys[0], (SLOTS, NSEQ, D), 1.0, 6.0, ((0, 2),))
    target = bell_draw(arg_keys[1], (SLOTS, NSEQ, D), 1.0, 6.0, ((0, 32),))
    lengths = draw_lengths(jax.random.fold_in(arg_keys[26], 71), 0)
    routes_keys = jax.random.split(jax.random.fold_in(arg_keys[3], 1), SLOTS * NSEQ // ROWS_MP)
    routes_turns = jax.random.permutation(jax.random.fold_in(arg_keys[3], 3), SLOTS * NSEQ // ROWS_MP)
    routes = jax.vmap(lambda own, number: deal_out(jax.random.fold_in(arg_keys[3], 2), own, number, ROWS_MP, EXPERTS, TOPK, CAP, 2))(routes_keys, routes_turns).reshape((SLOTS, NSEQ, TOPK))
    route_weight = jnp.clip(0.1 + 0.3 * jax.random.uniform(arg_keys[4], (SLOTS, NSEQ, TOPK), jnp.float32) ** levels(arg_keys[4], (SLOTS, NSEQ, TOPK), ((0, 32),), -0.2, 0.2), 0.1, 0.4)
    in_gain = jnp.clip(1.0 + 0.1 * jax.random.normal(arg_keys[5], (D,), jnp.float32), 0.5, 1.5).astype(jnp.bfloat16)
    gate_proj = bell_draw(arg_keys[6], (D, INNER), D ** -0.5, 0.15625, ((1, 16),))
    value_proj = bell_draw(arg_keys[7], (D, INNER), D ** -0.5, 0.15625, ((1, 16),))
    state_proj = bell_draw(arg_keys[8], (D, 2 * STATE), (4 * D) ** -0.5, 0.078125, ((0, 32),))
    step_proj = bell_draw(arg_keys[9], (D, HEADS), D ** -0.5, 0.15625, ((1, 16),))
    conv_value = bell_draw(arg_keys[10], (CONV, INNER), 0.5, 3.0, ((1, 16),), jnp.float32)
    conv_value_bias = bell_draw(arg_keys[11], (INNER,), 0.5, 3.0, ((0, 16),), jnp.float32)
    conv_state = bell_draw(arg_keys[12], (2 * STATE, CONV), 0.5, 3.0, ((0, 32),))
    conv_state_bias = bell_draw(arg_keys[13], (2 * STATE,), 0.5, 3.0, ((0, 32),))
    step_bias = jnp.clip(-4.0 + 3.0 * jax.random.uniform(arg_keys[14], (HEADS,), jnp.float32) ** levels(arg_keys[14], (HEADS,), ((0, 16),), -0.2, 0.2), -4.0, -1.0)
    decay_log = jnp.clip(-8.0 + 7.0 * jax.random.uniform(arg_keys[15], (HEADS,), jnp.float32) ** levels(arg_keys[15], (HEADS,), ((0, 16),), -0.2, 0.2), -8.0, -1.0)
    skip_gain = jnp.clip(0.5 + 1.5 * jax.random.uniform(arg_keys[16], (HEADS,), jnp.float32) ** levels(arg_keys[16], (HEADS,), ((0, 16),), -0.2, 0.2), 0.5, 2.0)
    mixer_gain = jnp.clip(1.0 + 0.1 * jax.random.normal(arg_keys[17], (INNER,), jnp.float32), 0.5, 1.5)
    out_proj = bell_draw(arg_keys[18], (INNER, D), INNER ** -0.5, 0.109375, ((0, 16),))
    ffn_gain = jnp.clip(1.0 + 0.1 * jax.random.normal(arg_keys[19], (D,), jnp.float32), 0.5, 1.5).astype(jnp.bfloat16)
    shared_gate = bell_draw(arg_keys[20], (D, SHARED_FF), D ** -0.5, 0.15625, ((0, 32),))
    shared_up = bell_draw(arg_keys[21], (D, SHARED_FF), D ** -0.5, 0.15625, ((0, 32),))
    shared_down = bell_draw(arg_keys[22], (SHARED_FF, D), SHARED_FF ** -0.5, 0.1875, ((0, 32),))
    expert_gate = bell_draw(arg_keys[23], (EXPERTS, D, EXPERT_FF), D ** -0.5, 0.15625, ((0, 16),))
    routed_up_weights = bell_draw(arg_keys[24], (EXPERTS, D, EXPERT_FF), D ** -0.5, 0.15625, ((0, 16),))
    expert_down = bell_draw(arg_keys[25], (EXPERTS, EXPERT_FF, D), EXPERT_FF ** -0.5, 0.25, ((0, 16),))
    return dict(tokens=tokens, target=target, lengths=lengths, routes=routes, route_weight=route_weight, in_gain=in_gain, gate_proj=gate_proj, value_proj=value_proj, state_proj=state_proj, step_proj=step_proj, conv_value=conv_value, conv_value_bias=conv_value_bias, conv_state=conv_state, conv_state_bias=conv_state_bias, step_bias=step_bias, decay_log=decay_log, skip_gain=skip_gain, mixer_gain=mixer_gain, out_proj=out_proj, ffn_gain=ffn_gain, shared_gate=shared_gate, shared_up=shared_up, shared_down=shared_down, expert_gate=expert_gate, routed_up_weights=routed_up_weights, expert_down=expert_down)


epsilon = 1e-05
highest = lax.Precision.HIGHEST

@jax.custom_vjp
def low(v):
    return lax.optimization_barrier(v.astype(jnp.bfloat16)).astype(jnp.float32)

@jax.custom_vjp
def low_back(v):
    return v

def low_keep(v):
    return (low(v), None)

def low_pass(kept, grad):
    return (grad,)

def back_keep(v):
    return (v, None)

def back_low(kept, grad):
    return (low(grad),)
low.defvjp(low_keep, low_pass)
low_back.defvjp(back_keep, back_low)

def project(left_side, matrix):
    return jnp.dot(left_side, matrix, precision=highest, preferred_element_type=jnp.float32)

def rms_scale(values, gain):
    return values * lax.rsqrt(lax.optimization_barrier(jnp.mean(values * values, axis=-1, keepdims=True)) + epsilon) * gain

def conv_decay(extended, conv_weight, conv_bias, step_raw, step_bias, decay_log, inner_width, state_width):
    length = step_raw.shape[0]
    preact = conv_bias + conv_weight[0] * extended[0:length]
    for offset in range(1, conv_weight.shape[0]):
        preact = preact + conv_weight[offset] * extended[offset:offset + length]
    activated = jax.nn.silu(preact)
    head_count = step_raw.shape[-1]
    values = activated[..., :inner_width].reshape(length, activated.shape[1], head_count, inner_width // head_count)
    input_matrix_b = activated[..., inner_width:inner_width + state_width]
    c_matrix = activated[..., inner_width + state_width:]
    step_size = jax.nn.softplus(step_raw + step_bias)
    log_decay = -jnp.exp(decay_log) * step_size
    return (values, input_matrix_b, c_matrix, step_size, log_decay)

def ssd_output(values, input_matrix_b, c_matrix, step_size, log_decay, entering, skip_gain):
    cumulative = jnp.cumsum(log_decay, axis=0)
    length = cumulative.shape[0]
    causal = (jnp.arange(length)[:, None] >= jnp.arange(length)[None, :])[:, :, None, None]
    log_gap = jnp.where(causal, cumulative[:, None] - cumulative[None, :], 0.0)
    decay_mask = jnp.where(causal, jnp.exp(log_gap), 0.0)
    intersection = jnp.einsum('tbn,sbn->tsb', c_matrix, input_matrix_b, precision=highest)
    weighted = decay_mask * intersection[..., None]
    scaled = values * step_size[..., None]
    within = jnp.einsum('tsbh,sbhp->tbhp', weighted, scaled, precision=highest)
    carried = jnp.exp(cumulative)[..., None] * jnp.einsum('tbn,bhpn->tbhp', c_matrix, entering, precision=highest)
    return within + carried + skip_gain[:, None] * values

def state_update(values, input_matrix_b, step_size, log_decay):
    cumulative = jnp.cumsum(log_decay, axis=0)
    decay_total = jnp.exp(cumulative[-1])
    tail_weight = jnp.exp(cumulative[-1] - cumulative) * step_size
    local_state = jnp.einsum('sbh,sbhp,sbn->bhpn', tail_weight, values, input_matrix_b, precision=highest)
    return (decay_total, local_state)

def forward(routes, route_weight, tokens, in_gain, gate_proj, value_proj, state_proj, step_proj, conv_value, conv_value_bias, conv_state, conv_state_bias, step_bias, decay_log, skip_gain, mixer_gain, out_proj, ffn_gain, shared_gate, shared_up, shared_down, expert_gate, routed_up_weights, expert_down):
    normed = low(rms_scale(tokens, in_gain))
    gate_raw = low_back(project(normed, gate_proj))
    value_raw = low_back(project(normed, value_proj))
    state_raw = low_back(project(normed, state_proj))
    step_raw = low_back(project(normed, step_proj))
    conv_input = jnp.concatenate([value_raw, state_raw], axis=-1)
    padding = jnp.zeros((CONV - 1,) + conv_input.shape[1:], jnp.float32)
    extended = jnp.concatenate([padding, conv_input], axis=0)
    conv_weight = jnp.concatenate([conv_value, conv_state.T], axis=1)
    conv_bias = jnp.concatenate([conv_value_bias, conv_state_bias])
    values, input_matrix_b, c_matrix, step_size, log_decay = conv_decay(extended, conv_weight, conv_bias, step_raw, step_bias, decay_log, INNER, STATE)
    block_count = SLOTS // SLOT_DEV

    def blocks(source_array):
        return source_array.reshape((block_count, SLOT_DEV) + source_array.shape[1:])

    def advance(carry_state, pieces):
        block_values, block_b, block_c, block_step, block_decay = pieces
        result = ssd_output(block_values, block_b, block_c, block_step, block_decay, carry_state, skip_gain)
        decay_total, local_state = state_update(block_values, block_b, block_step, block_decay)
        return (decay_total[..., None, None] * carry_state + local_state, result)
    start_state = jnp.zeros((NSEQ, HEADS, HEAD_DIM, STATE), jnp.float32)
    _, outputs = lax.scan(jax.checkpoint(advance), start_state, (blocks(values), blocks(input_matrix_b), blocks(c_matrix), blocks(step_size), blocks(log_decay)))
    mixer_values = outputs.reshape(SLOTS, NSEQ, INNER)
    gated_out = mixer_values * jax.nn.silu(gate_raw)
    square_sum = lax.optimization_barrier(jnp.sum(gated_out * gated_out, axis=-1))
    pre_mix = low_back(project(low(gated_out * mixer_gain), out_proj))
    hidden = tokens + pre_mix * lax.rsqrt(square_sum / INNER + epsilon)[..., None]
    ffn_input = low(rms_scale(hidden, ffn_gain))
    shared_gate_val = low_back(project(ffn_input, shared_gate))
    shared_up_val = low_back(project(ffn_input, shared_up))
    shared_act = low(jax.nn.silu(shared_gate_val) * shared_up_val)
    shared_out = low_back(project(shared_act, shared_down))
    chosen = routes[..., None] == jnp.arange(EXPERTS)
    coefficient = lax.optimization_barrier(jnp.sum(jnp.where(chosen, route_weight[..., None], 0.0), axis=-2))

    def expert_step(running, pieces):
        gate_weight, up_weight, down_weight, share_weight = pieces
        copied = low_back(ffn_input)
        gate_activation = low_back(project(copied, gate_weight))
        up_val = low_back(project(copied, up_weight))
        act_val = low(jax.nn.silu(gate_activation) * up_val)
        result = low_back(low(project(act_val, down_weight)))
        return (running + share_weight[..., None] * result, None)
    routed, _ = lax.scan(jax.checkpoint(expert_step), jnp.zeros_like(tokens), (expert_gate, routed_up_weights, expert_down, jnp.moveaxis(coefficient, -1, 0)))
    return hidden + shared_out + routed

def reference(tokens, target, lengths, routes, route_weight, in_gain, gate_proj, value_proj, state_proj, step_proj, conv_value, conv_value_bias, conv_state, conv_state_bias, step_bias, decay_log, skip_gain, mixer_gain, out_proj, ffn_gain, shared_gate, shared_up, shared_down, expert_gate, routed_up_weights, expert_down):
    params = tuple((member.astype(jnp.float32) for member in (tokens, in_gain, gate_proj, value_proj, state_proj, step_proj, conv_value, conv_value_bias, conv_state, conv_state_bias, step_bias, decay_log, skip_gain, mixer_gain, out_proj, ffn_gain, shared_gate, shared_up, shared_down, expert_gate, routed_up_weights, expert_down)))
    weights_float = route_weight.astype(jnp.float32)

    def run_block(*floats):
        return forward(routes, weights_float, *floats)
    output, pullback = jax.vjp(run_block, *params)
    valid_mask = (jnp.arange(SLOTS)[:, None] < lengths[None, :]).astype(jnp.float32)
    cotangent = (output - target.astype(jnp.float32)) * valid_mask[..., None]
    gradients = pullback(cotangent)
    return (output.astype(jnp.bfloat16), gradients[0], gradients[1], gradients[2], gradients[3], gradients[4], gradients[5], gradients[6], gradients[7], gradients[8], gradients[9], gradients[10], gradients[11], gradients[12], gradients[13], gradients[14], gradients[15], gradients[16], gradients[17], gradients[18], gradients[19], gradients[20], gradients[21])
```

```python
import jax
import jax.numpy as jnp
from jax import lax
from jax.sharding import PartitionSpec as P

STATE = 128
INNER = 3072


epsilon = 1e-05
highest = lax.Precision.HIGHEST


def shifted(block, axis, distance):
    devices = range(lax.axis_size(axis))
    route = [(i - distance, i) for i in devices if i - distance in devices]
    return lax.ppermute(block, axis, route)


def entering_2(value, axis, join, neutral, backward):
    count, mine = (lax.axis_size(axis), lax.axis_index(axis))
    pieces = jax.tree.map(lambda part: lax.all_gather(part, axis), value)
    if backward:
        pieces = jax.tree.map(lambda part: part[::-1], pieces)
        mine = count - 1 - mine
    running = jax.tree.map(
        lambda part, zero: jnp.full_like(part, 0) + jnp.asarray(zero, part.dtype), value, neutral
    )

    def hop(position, running):
        longer = join(running, jax.tree.map(lambda part: part[position], pieces))
        return jax.tree.map(lambda new, old: jnp.where(position < mine, new, old), longer, running)

    return lax.fori_loop(0, count - 1, hop, running)


def rms_scale(values, gain):
    return values * lax.rsqrt(jnp.mean(values * values, axis=-1, keepdims=True) + epsilon) * gain


def silu_slope(values):
    sigmoid_val = jax.nn.sigmoid(values)
    return sigmoid_val * (1.0 + values * (1.0 - sigmoid_val))


def conv_decay(
    extended, conv_weight, conv_bias, step_raw, step_bias, decay_log, inner_width, state_width
):
    length = step_raw.shape[0]
    preact = conv_bias + conv_weight[0] * extended[0:length]
    for offset in range(1, conv_weight.shape[0]):
        preact = preact + conv_weight[offset] * extended[offset : offset + length]
    activated = jax.nn.silu(preact)
    head_count = step_raw.shape[-1]
    values = activated[..., :inner_width].reshape(
        length, activated.shape[1], head_count, inner_width // head_count
    )
    input_matrix_b = activated[..., inner_width : inner_width + state_width]
    c_matrix = activated[..., inner_width + state_width :]
    step_size = jax.nn.softplus(step_raw + step_bias)
    log_decay = -jnp.exp(decay_log) * step_size
    return (values, input_matrix_b, c_matrix, step_size, log_decay)


def ssd_output(values, input_matrix_b, c_matrix, step_size, log_decay, entering, skip_gain):
    cumulative = jnp.cumsum(log_decay, axis=0)
    length = cumulative.shape[0]
    causal = (jnp.arange(length)[:, None] >= jnp.arange(length)[None, :])[:, :, None, None]
    log_gap = jnp.where(causal, cumulative[:, None] - cumulative[None, :], 0.0)
    decay_mask = jnp.where(causal, jnp.exp(log_gap), 0.0)
    intersection = jnp.einsum("tbn,sbn->tsb", c_matrix, input_matrix_b, precision=highest)
    weighted = decay_mask * intersection[..., None]
    scaled = values * step_size[..., None]
    within = jnp.einsum("tsbh,sbhp->tbhp", weighted, scaled, precision=highest)
    carried = jnp.exp(cumulative)[..., None] * jnp.einsum(
        "tbn,bhpn->tbhp", c_matrix, entering, precision=highest
    )
    return within + carried + skip_gain[:, None] * values


def state_update(values, input_matrix_b, step_size, log_decay):
    cumulative = jnp.cumsum(log_decay, axis=0)
    decay_total = jnp.exp(cumulative[-1])
    tail_weight = jnp.exp(cumulative[-1] - cumulative) * step_size
    local_state = jnp.einsum(
        "sbh,sbhp,sbn->bhpn", tail_weight, values, input_matrix_b, precision=highest
    )
    return (decay_total, local_state)


def chain_combine(earlier, latter):
    return (earlier[0] * latter[0], latter[0][..., None, None] * earlier[1] + latter[1])


def bits(value):
    return value.astype(jnp.bfloat16)


def wide(value):
    return value.astype(jnp.float32)


def rounded(value):
    return lax.reduce_precision(value, 8, 7)


def mp_permute(value, target):
    count = lax.axis_size("mp")
    return lax.ppermute(value, "mp", [(i, target(i)) for i in range(count)])


def across_core(value):
    return mp_permute(value, lambda i: i ^ 1)


def across_pair(value):
    return mp_permute(value, lambda i: i ^ 2)


def ring_step(value, distance=1):
    count = lax.axis_size("mp")
    return mp_permute(value, lambda i: (i + 4 * distance) % count)


def coordinates():
    mine = lax.axis_index("mp")
    return mine // 4, (mine // 2) % 2, mine % 2


def pick(value, index, axis=0):
    return lax.dynamic_index_in_dim(value, index, axis, keepdims=False)


def gather_relative(block):
    ring = lax.axis_size("mp") // 4
    held, pairs = block, []
    for step in range(ring):
        pairs.append(jnp.stack([held, across_pair(held)]))
        if step < ring - 1:
            held = ring_step(held)
    own = jnp.stack(pairs)
    return own, across_core(own)


def relative_owner():
    ring = lax.axis_size("mp") // 4
    deep, pair, core = coordinates()
    cores = jnp.arange(2)[:, None, None]
    steps = jnp.arange(ring)[None, :, None]
    pairs = jnp.arange(2)[None, None, :]
    return ((deep - steps) % ring) * 4 + (pair ^ pairs) * 2 + (core ^ cores)


def scatter_relative(own, partner, kept=jnp.bfloat16):
    ring = lax.axis_size("mp") // 4
    half = (wide(own) + wide(across_core(partner))).astype(kept)
    order = list(range(1, ring)) + [0]
    received = {step: across_pair(half[step, 1]) for step in order}
    moving = None
    for step in range(1, ring):
        total = wide(half[step, 0]) + wide(received[step])
        if moving is not None:
            total = total + wide(moving)
        moving = ring_step(total.astype(kept))
    return wide(half[0, 0]) + wide(received[0]) + wide(moving)


def to_relative(value):
    ring = lax.axis_size("mp") // 4
    order = relative_owner()
    both = value[order.reshape(-1)].reshape((2, ring, 2) + value.shape[1:])
    return both[0], both[1]


def from_relative(own, partner):
    count = lax.axis_size("mp")
    order = relative_owner().reshape(-1)
    place = jnp.zeros((count,), jnp.int32).at[order].set(jnp.arange(count, dtype=jnp.int32))
    both = jnp.stack([own, partner])
    return both.reshape((count,) + both.shape[3:])[place]


def gather_small(block):
    ring = lax.axis_size("mp") // 4
    deep, pair, core = coordinates()
    both = [block, across_core(block)]
    rows = jnp.stack(both)
    rows = jnp.stack([rows, across_pair(rows)])
    turned = [rows] + [ring_step(rows, step) for step in range(1, ring)]
    every = jnp.stack(turned)
    count = lax.axis_size("mp")
    flat = every.reshape((count,) + block.shape)
    position = jnp.arange(count)
    steps = (deep - position // 4) % ring
    place = steps * 4 + (pair ^ ((position // 2) % 2)) * 2 + (core ^ (position % 2))
    return flat[place]


def seq_gather(value):
    if lax.axis_size("seq") != 2:
        return lax.all_gather(value, "seq")
    other = lax.ppermute(value, "seq", [(0, 1), (1, 0)])
    first = lax.axis_index("seq") == 0
    return jnp.stack([jnp.where(first, value, other), jnp.where(first, other, value)])


def seq_scatter(value):
    if lax.axis_size("seq") != 2:
        return lax.psum_scatter(wide(value), "seq", scatter_dimension=0, tiled=False)
    mine = lax.axis_index("seq")
    other = lax.ppermute(bits(pick(value, 1 - mine)), "seq", [(0, 1), (1, 0)])
    return wide(pick(value, mine)) + wide(other)


def seq_sum(value):
    if lax.axis_size("seq") != 2:
        return lax.psum(wide(value), "seq")
    low = bits(value)
    return wide(low) + wide(lax.ppermute(low, "seq", [(0, 1), (1, 0)]))


def seq_entering(decay, state, backward):
    if lax.axis_size("seq") == 2:
        route = [(1, 0)] if backward else [(0, 1)]
        return lax.ppermute(state, "seq", route)
    return entering_2(
        (decay, state),
        "seq",
        chain_combine,
        (jnp.ones_like(decay), jnp.zeros_like(state)),
        backward,
    )[1]


def mp_exchange(value):
    return lax.all_to_all(value, "mp", split_axis=0, concat_axis=0, tiled=True)


def body(
    tokens,
    target,
    lengths,
    routes,
    route_weight,
    in_gain,
    gate_proj,
    value_proj,
    state_proj,
    step_proj,
    conv_value,
    conv_value_bias,
    conv_state,
    conv_state_bias,
    step_bias,
    decay_log,
    skip_gain,
    mixer_gain,
    out_proj,
    ffn_gain,
    shared_gate,
    shared_up,
    shared_down,
    expert_gate,
    routed_up_weights,
    expert_down,
):
    mp_count = lax.axis_size("mp")
    slot_count, seq_count, model_width = tokens.shape
    seq_devices = lax.axis_size("seq")
    shared_expert_rows = slot_count // mp_count
    inner_width = gate_proj.shape[1]
    row_count = shared_expert_rows * seq_count
    window = conv_value.shape[0]
    gain_rows = in_gain.shape[0]
    state_rows = conv_state.shape[0]
    state_width = state_proj.shape[1]
    expert_count = expert_gate.shape[0] * mp_count

    packed = jnp.concatenate(
        [
            state_proj.reshape(-1),
            in_gain,
            ffn_gain,
            conv_state.reshape(-1),
            conv_state_bias,
        ]
    )
    route_rows = route_weight.reshape(row_count, -1)
    chosen = routes.reshape(row_count, -1, 1) == jnp.arange(expert_count, dtype=jnp.int32)
    coefficient = jnp.sum(jnp.where(chosen, route_rows[..., None], 0.0), axis=1)
    coefficient_high = rounded(coefficient)
    coefficient_low = coefficient - coefficient_high
    both_packed = seq_gather(packed)
    small = gather_small(
        jnp.concatenate(
            [
                both_packed.reshape(-1),
                bits(coefficient_high).reshape(-1),
                bits(coefficient_low).reshape(-1),
            ]
        )
    )
    width = packed.shape[0]
    weights_small = small[:, : seq_devices * width].reshape(mp_count, seq_devices, width)
    weights_small = jnp.moveaxis(weights_small, 1, 0).reshape(seq_devices * mp_count, width)
    cut = [gain_rows * state_width]
    for part in (gain_rows, gain_rows, conv_state.size):
        cut.append(cut[-1] + part)
    state_whole = weights_small[:, : cut[0]].reshape(-1, state_width)
    gain_first = weights_small[:, cut[0] : cut[1]].reshape(-1)
    gain_second = weights_small[:, cut[1] : cut[2]].reshape(-1)
    conv_state_whole = weights_small[:, cut[2] : cut[3]].reshape(-1, window)
    conv_bias_whole = weights_small[:, cut[3] :].reshape(-1)
    share = small[:, seq_devices * width :].reshape(mp_count, 2, row_count, expert_count)
    share = lax.dynamic_index_in_dim(share, lax.axis_index("mp"), 3, keepdims=False)
    share = wide(share[:, 0]) + wide(share[:, 1])
    share_own, share_partner = to_relative(share)

    columns = shared_gate.shape[1] // (seq_devices * mp_count)
    hidden_own = seq_devices * columns
    pair_cut = jnp.stack([shared_gate, shared_up]).reshape(2, gain_rows, seq_devices, mp_count, columns)
    pair_moved = mp_exchange(pair_cut.transpose(3, 0, 1, 2, 4).reshape(mp_count, -1))
    pair_all = seq_gather(pair_moved).reshape(
        seq_devices, mp_count, 2, gain_rows, hidden_own
    )
    pair_all = pair_all.transpose(2, 0, 1, 3, 4).reshape(2, model_width, hidden_own)
    gate_shared, up_shared = pair_all[0], pair_all[1]
    down_shared = seq_gather(shared_down).reshape(hidden_own, model_width)
    gate_weight, up_weight, down_weight = expert_gate[0], routed_up_weights[0], expert_down[0]

    inputs = tokens.astype(jnp.float32)
    normed = rms_scale(inputs, gain_first.astype(jnp.float32)).astype(jnp.bfloat16)
    gate_raw = jnp.dot(normed, gate_proj, preferred_element_type=jnp.float32)
    value_raw = jnp.dot(normed, value_proj, preferred_element_type=jnp.float32)
    state_raw = jnp.dot(normed, state_whole, preferred_element_type=jnp.float32)
    step_raw = jnp.dot(normed, step_proj, preferred_element_type=jnp.float32)
    conv_input = jnp.concatenate([value_raw, state_raw], axis=-1)
    edge_rows = shifted(conv_input[slot_count - window + 1 :], "seq", 1)
    extended = jnp.concatenate([edge_rows, conv_input], axis=0)
    conv_weight = jnp.concatenate([conv_value, conv_state_whole.astype(jnp.float32).T], axis=1)
    conv_bias = jnp.concatenate([conv_value_bias, conv_bias_whole.astype(jnp.float32)])

    def first_piece(ext_values, weight_values, bias_values, step_values, bias_step, decay_values):
        return conv_decay(
            ext_values,
            weight_values,
            bias_values,
            step_values,
            bias_step,
            decay_values,
            inner_width,
            STATE,
        )

    mixer_inputs, first_back = jax.vjp(
        first_piece, extended, conv_weight, conv_bias, step_raw, step_bias, decay_log
    )
    values, input_matrix_b, c_matrix, step_size, log_decay = mixer_inputs
    local_out, state_back = jax.vjp(state_update, values, input_matrix_b, step_size, log_decay)
    decay_total, local_state = local_out
    entering = seq_entering(decay_total, local_state, False)

    def second_piece(
        in_values,
        in_bmatrix,
        in_cmatrix,
        in_step,
        in_decay,
        in_state,
        in_skip,
        in_gate,
        in_gain_mix,
    ):
        result = ssd_output(in_values, in_bmatrix, in_cmatrix, in_step, in_decay, in_state, in_skip)
        gated_part = result.reshape(in_gate.shape) * jax.nn.silu(in_gate)
        return (gated_part, gated_part * in_gain_mix)

    gated_pair, second_back = jax.vjp(
        second_piece,
        values,
        input_matrix_b,
        c_matrix,
        step_size,
        log_decay,
        entering,
        skip_gain,
        gate_raw,
        mixer_gain,
    )
    gated_out, scaled = gated_pair
    scaled_low = scaled.astype(jnp.bfloat16)
    mix_part = jnp.dot(scaled_low, out_proj, preferred_element_type=jnp.float32)
    squares = jnp.sum(gated_out * gated_out, axis=-1)
    square_sum = jnp.sum(mp_exchange(squares.reshape(mp_count, row_count)), axis=0)
    mix_send = bits(mix_part).reshape(mp_count, row_count, model_width)
    pre_mix = scatter_relative(*to_relative(mix_send))
    inv_norm = lax.rsqrt(square_sum / INNER + epsilon)[:, None]
    start_row = lax.axis_index("mp") * shared_expert_rows
    own_inputs = lax.dynamic_slice_in_dim(inputs, start_row, shared_expert_rows, 0).reshape(
        row_count, model_width
    )
    hidden = own_inputs + pre_mix * inv_norm
    ffn_input = rms_scale(hidden, wide(gain_second)).astype(jnp.bfloat16)

    def dot(left, right):
        return jnp.dot(left, right, preferred_element_type=jnp.float32)

    def dot_t(left, right):
        return lax.dot_general(
            left, right, (((1,), (1,)), ((), ())), preferred_element_type=jnp.float32
        )

    def t_dot(left, right):
        return lax.dot_general(
            left, right, (((0,), (0,)), ((), ())), preferred_element_type=jnp.float32
        )

    rows_own, rows_partner = gather_relative(ffn_input)
    all_rows = jnp.stack([rows_own, rows_partner]).reshape(-1, model_width)
    shares = jnp.stack([share_own, share_partner]).reshape(-1, 1)
    gate_activation = dot(all_rows, gate_weight)
    up_val = dot(all_rows, up_weight)
    act_val = bits(jax.nn.silu(gate_activation) * up_val)
    shared_gate_val = dot(all_rows, gate_shared)
    shared_up_val = dot(all_rows, up_shared)
    shared_act = bits(jax.nn.silu(shared_gate_val) * shared_up_val)
    partial_out = shares * wide(bits(dot(act_val, down_weight))) + dot(shared_act, down_shared)

    def halves(value):
        cut_value = bits(value).reshape((2,) + rows_own.shape)
        return cut_value[0], cut_value[1]

    output = hidden + scatter_relative(*halves(partial_out))
    block_out = output.astype(jnp.bfloat16).reshape(shared_expert_rows, seq_count, model_width)
    position = (
        lax.axis_index("seq") * slot_count
        + start_row
        + jnp.arange(shared_expert_rows, dtype=jnp.int32)
    )
    valid_mask = (position[:, None] < lengths[None, :]).astype(jnp.float32).reshape(row_count, 1)
    grad_out = (output - target.astype(jnp.float32).reshape(row_count, model_width)) * valid_mask
    grad_own, grad_partner = gather_relative(bits(grad_out))
    all_grads = jnp.stack([grad_own, grad_partner]).reshape(-1, model_width)
    route_grads = bits(shares * wide(all_grads))
    activation_gradient = dot_t(route_grads, down_weight)
    egate_grad = bits(activation_gradient * up_val * silu_slope(gate_activation))
    expert_up_gradient = bits(activation_gradient * jax.nn.silu(gate_activation))
    shact_grad = dot_t(all_grads, down_shared)
    sgate_grad = bits(shact_grad * shared_up_val * silu_slope(shared_gate_val))
    sup_grad = bits(shact_grad * jax.nn.silu(shared_gate_val))
    partial_rows = (
        dot_t(egate_grad, gate_weight)
        + dot_t(expert_up_gradient, up_weight)
        + dot_t(sgate_grad, gate_shared)
        + dot_t(sup_grad, up_shared)
    )
    ffn_input_grad = scatter_relative(*halves(partial_rows))
    expert_down_grad = seq_sum(t_dot(act_val, route_grads))[None]
    expert_gate_grad = seq_sum(t_dot(all_rows, egate_grad))[None]
    expert_up_grad = seq_sum(t_dot(all_rows, expert_up_gradient))[None]
    shared_down_grad = seq_scatter(
        t_dot(shared_act, all_grads).reshape(seq_devices, columns, model_width)
    )
    pair_grad = jnp.stack([t_dot(all_rows, sgate_grad), t_dot(all_rows, sup_grad)])
    pair_grad = pair_grad.reshape(2, seq_devices, mp_count, gain_rows, hidden_own)
    pair_grad = seq_scatter(pair_grad.transpose(1, 2, 0, 3, 4))
    pair_grad = wide(mp_exchange(bits(pair_grad).reshape(mp_count, -1)))
    pair_grad = pair_grad.reshape(mp_count, 2, gain_rows, seq_devices, columns)
    pair_grad = pair_grad.transpose(1, 2, 3, 0, 4).reshape(2, gain_rows, -1)
    shared_gate_grad, shared_up_grad = pair_grad[0], pair_grad[1]

    _, second_norm_back = jax.vjp(rms_scale, hidden, wide(gain_second))
    hidden_part, ffn_gain_grad = second_norm_back(ffn_input_grad)
    hidden_grad_share = grad_out + hidden_part
    sum_grad_share = (
        jnp.sum(hidden_grad_share * pre_mix, axis=-1, keepdims=True)
        * (-0.5 / INNER)
        * inv_norm
        * inv_norm
        * inv_norm
    )
    sum_high = rounded(sum_grad_share)
    sum_low = sum_grad_share - sum_high
    mix_grad_send = jnp.concatenate(
        [
            bits(hidden_grad_share * inv_norm),
            bits(sum_high),
            bits(sum_low),
            jnp.zeros((row_count, 126), jnp.bfloat16),
        ],
        axis=-1,
    )
    mix_all = from_relative(*gather_relative(mix_grad_send))
    mix_all = mix_all.reshape(slot_count, seq_count, -1)
    mix_grad_all = mix_all[..., :model_width]
    sum_grad = wide(mix_all[..., model_width]) + wide(mix_all[..., model_width + 1])
    out_proj_grad = jnp.einsum(
        "sbc,sbd->cd", scaled_low, mix_grad_all, preferred_element_type=jnp.float32
    )
    scaled_grad = jnp.einsum(
        "sbd,cd->sbc", mix_grad_all, out_proj, preferred_element_type=jnp.float32
    )
    gated_grad = 2.0 * gated_out * sum_grad[..., None]
    (
        out_values_grad,
        out_bmatrix_grad,
        out_cmatrix_grad,
        out_step_grad,
        out_decay_grad,
        entering_grad,
        skip_gain_grad,
        gate_raw_grad,
        mixer_gain_grad,
    ) = second_back((gated_grad, scaled_grad))
    exit_grad = seq_entering(decay_total, entering_grad, True)
    total_grad = jnp.sum(entering * exit_grad, axis=(-2, -1))
    tail_values_grad, tail_bmatrix_grad, tail_step_grad, tail_decay_grad = state_back(
        (total_grad, exit_grad)
    )
    ext_grad, conv_weight_grad, conv_bias_grad, step_raw_grad, step_bias_grad, decay_log_grad = (
        first_back(
            (
                out_values_grad + tail_values_grad,
                out_bmatrix_grad + tail_bmatrix_grad,
                out_cmatrix_grad,
                out_step_grad + tail_step_grad,
                out_decay_grad + tail_decay_grad,
            )
        )
    )
    edge_grad = shifted(ext_grad[: window - 1], "seq", -1)
    conv_grad = ext_grad[window - 1 :] + jnp.concatenate(
        [jnp.zeros((slot_count - window + 1,) + ext_grad.shape[1:], jnp.float32), edge_grad], axis=0
    )
    conv_grad_low = conv_grad.astype(jnp.bfloat16)
    value_grad = conv_grad_low[..., :inner_width]
    state_grad = conv_grad_low[..., inner_width:]
    gate_grad = gate_raw_grad.astype(jnp.bfloat16)
    step_grad = step_raw_grad.astype(jnp.bfloat16)
    partial_value = jnp.einsum(
        "sbc,dc->sbd", gate_grad, gate_proj, preferred_element_type=jnp.float32
    )
    partial_value = partial_value + jnp.einsum(
        "sbc,dc->sbd", value_grad, value_proj, preferred_element_type=jnp.float32
    )
    partial_value = partial_value + jnp.einsum(
        "sbc,dc->sbd", state_grad, state_whole, preferred_element_type=jnp.float32
    )
    partial_value = partial_value + jnp.einsum(
        "sbh,dh->sbd", step_grad, step_proj, preferred_element_type=jnp.float32
    )
    gate_proj_grad = jnp.einsum(
        "sbd,sbc->dc", normed, gate_grad, preferred_element_type=jnp.float32
    )
    value_proj_grad = jnp.einsum(
        "sbd,sbc->dc", normed, value_grad, preferred_element_type=jnp.float32
    )
    state_proj_grad = jnp.einsum(
        "sbd,sbc->dc", normed, state_grad, preferred_element_type=jnp.float32
    )
    step_proj_grad = jnp.einsum(
        "sbd,sbh->dh", normed, step_grad, preferred_element_type=jnp.float32
    )
    conv_value_grad = conv_weight_grad[:, :inner_width]
    conv_state_grad = conv_weight_grad[:, inner_width:].T
    conv_value_bias_grad = conv_bias_grad[:inner_width]
    conv_state_bias_grad = conv_bias_grad[inner_width:]
    whole_width = lax.rsqrt(jnp.mean(inputs * inputs, axis=-1, keepdims=True) + epsilon)
    in_gain_grad = jnp.sum(partial_value * inputs * whole_width, axis=(0, 1))

    def by_owner(value):
        parts = value.reshape((seq_devices, mp_count, -1))
        return jnp.moveaxis(parts, 1, 0).reshape(mp_count, -1)

    extra = jnp.concatenate(
        [
            by_owner(state_proj_grad),
            by_owner(in_gain_grad),
            by_owner(ffn_gain_grad),
        ],
        axis=-1,
    )
    extra_rows = -(-extra.shape[1] // (8 * model_width)) * 8
    extra_size = extra.shape[1]
    extra = jnp.pad(extra, ((0, 0), (0, extra_rows * model_width - extra_size)))
    last_send = jnp.concatenate(
        [
            bits(partial_value).reshape(mp_count, row_count, model_width),
            bits(extra).reshape(mp_count, extra_rows, model_width),
        ],
        axis=1,
    )
    last_sum = scatter_relative(*to_relative(last_send))
    normed_grad = last_sum[:row_count]
    extra_sum = last_sum[row_count:].reshape(-1)[:extra_size]
    _, first_norm_back = jax.vjp(rms_scale, own_inputs, wide(gain_first))
    tokens_grad = (first_norm_back(normed_grad)[0] + hidden_grad_share).reshape(
        shared_expert_rows, seq_count, model_width
    )
    sizes = [gain_rows * state_width, gain_rows, gain_rows]
    parts, at = [], 0
    for size in sizes:
        parts.append(extra_sum[at : at + seq_devices * size].reshape(seq_devices, size))
        at += seq_devices * size
    extra_own = seq_scatter(jnp.concatenate(parts, axis=-1))
    state_proj_out = extra_own[: sizes[0]].reshape(gain_rows, state_width)
    at = sizes[0]
    in_gain_out = extra_own[at : at + gain_rows]
    at += gain_rows
    ffn_gain_out = extra_own[at : at + gain_rows]
    conv_small = jnp.concatenate(
        [
            conv_state_grad.reshape(seq_devices, mp_count, -1),
            conv_state_bias_grad.reshape(seq_devices, mp_count, -1),
        ],
        axis=-1,
    )
    conv_small = jnp.moveaxis(conv_small, 1, 0).reshape(mp_count, -1)
    conv_small = jnp.sum(mp_exchange(conv_small), axis=0)
    exact = (
        step_proj_grad,
        conv_value_grad,
        conv_value_bias_grad,
        step_bias_grad,
        decay_log_grad,
        skip_gain_grad,
        mixer_gain_grad,
        conv_small.reshape(seq_devices, -1),
    )
    flat = jnp.concatenate([part.reshape(-1) for part in exact])
    if seq_devices == 2:
        flat = flat + lax.ppermute(flat, "seq", [(0, 1), (1, 0)])
    else:
        flat = lax.psum(flat, "seq")
    exact_out, at = [], 0
    for part in exact:
        exact_out.append(flat[at : at + part.size].reshape(part.shape))
        at += part.size
    conv_own = pick(exact_out[7], lax.axis_index("seq"))
    conv_state_out = conv_own[: state_rows * window].reshape(state_rows, window)
    conv_state_bias_out = conv_own[state_rows * window :]
    return (
        block_out,
        tokens_grad,
        in_gain_out,
        seq_sum(gate_proj_grad),
        seq_sum(value_proj_grad),
        state_proj_out,
        exact_out[0],
        exact_out[1],
        exact_out[2],
        conv_state_out,
        conv_state_bias_out,
        exact_out[3],
        exact_out[4],
        exact_out[5],
        exact_out[6],
        seq_sum(out_proj_grad),
        ffn_gain_out,
        shared_gate_grad,
        shared_up_grad,
        shared_down_grad,
        expert_gate_grad,
        expert_up_grad,
        expert_down_grad,
    )


def solution(mesh):
    placed = (
        P("seq", None, None),
        P(("seq", "mp"), None, None),
        P(),
        P(("seq", "mp"), None, None),
        P(("seq", "mp"), None, None),
        P(("seq", "mp")),
        P(None, "mp"),
        P(None, "mp"),
        P(("seq", "mp"), None),
        P(None, "mp"),
        P(None, "mp"),
        P("mp"),
        P(("seq", "mp"), None),
        P(("seq", "mp")),
        P("mp"),
        P("mp"),
        P("mp"),
        P("mp"),
        P("mp", None),
        P(("seq", "mp")),
        P(("seq", "mp"), None),
        P(("seq", "mp"), None),
        P(("seq", "mp"), None),
        P("mp", None, None),
        P("mp", None, None),
        P("mp", None, None),
    )
    return jax.shard_map(
        body,
        mesh=mesh,
        in_specs=placed,
        out_specs=(
            P(("seq", "mp"), None, None),
            P(("seq", "mp"), None, None),
            P(("seq", "mp")),
            P(None, "mp"),
            P(None, "mp"),
            P(("seq", "mp"), None),
            P(None, "mp"),
            P(None, "mp"),
            P("mp"),
            P(("seq", "mp"), None),
            P(("seq", "mp")),
            P("mp"),
            P("mp"),
            P("mp"),
            P("mp"),
            P("mp", None),
            P(("seq", "mp")),
            P(("seq", "mp"), None),
            P(("seq", "mp"), None),
            P(("seq", "mp"), None),
            P("mp", None, None),
            P("mp", None, None),
            P("mp", None, None),
        ),
        check_vma=False,
    )
```

```python
import jax
import jax.numpy as jnp
from jax import lax
from jax.experimental import pallas as pl
from jax.experimental.pallas import tpu as pltpu
from jax.sharding import PartitionSpec as P

STATE = 128
INNER = 3072


epsilon = 1e-05
highest = lax.Precision.HIGHEST


def shifted(block, axis, distance):
    devices = range(lax.axis_size(axis))
    route = [(i - distance, i) for i in devices if i - distance in devices]
    return lax.ppermute(block, axis, route)


def entering_2(value, axis, join, neutral, backward):
    count, mine = (lax.axis_size(axis), lax.axis_index(axis))
    pieces = jax.tree.map(lambda part: lax.all_gather(part, axis), value)
    if backward:
        pieces = jax.tree.map(lambda part: part[::-1], pieces)
        mine = count - 1 - mine
    running = jax.tree.map(
        lambda part, zero: jnp.full_like(part, 0) + jnp.asarray(zero, part.dtype), value, neutral
    )

    def hop(position, running):
        longer = join(running, jax.tree.map(lambda part: part[position], pieces))
        return jax.tree.map(lambda new, old: jnp.where(position < mine, new, old), longer, running)

    return lax.fori_loop(0, count - 1, hop, running)


def rms_scale(values, gain):
    return values * lax.rsqrt(jnp.mean(values * values, axis=-1, keepdims=True) + epsilon) * gain


def silu_slope(values):
    sigmoid_val = jax.nn.sigmoid(values)
    return sigmoid_val * (1.0 + values * (1.0 - sigmoid_val))


def chain_combine(earlier, latter):
    return (earlier[0] * latter[0], latter[0][..., None, None] * earlier[1] + latter[1])


def bits(value):
    return value.astype(jnp.bfloat16)


def wide(value):
    return value.astype(jnp.float32)


def rounded(value):
    return lax.reduce_precision(value, 8, 7)


def mp_permute(value, target):
    count = lax.axis_size("mp")
    return lax.ppermute(value, "mp", [(i, target(i)) for i in range(count)])


def across_core(value):
    return mp_permute(value, lambda i: i ^ 1)


def across_pair(value):
    return mp_permute(value, lambda i: i ^ 2)


def ring_step(value, distance=1):
    count = lax.axis_size("mp")
    return mp_permute(value, lambda i: (i + 4 * distance) % count)


def coordinates():
    mine = lax.axis_index("mp")
    return mine // 4, (mine // 2) % 2, mine % 2


def pick(value, index, axis=0):
    return lax.dynamic_index_in_dim(value, index, axis, keepdims=False)


def gather_relative(block):
    ring = lax.axis_size("mp") // 4
    held, pairs = block, []
    for step in range(ring):
        pairs.append(jnp.stack([held, across_pair(held)]))
        if step < ring - 1:
            held = ring_step(held)
    own = jnp.stack(pairs)
    return own, across_core(own)


def relative_owner():
    ring = lax.axis_size("mp") // 4
    deep, pair, core = coordinates()
    cores = jnp.arange(2)[:, None, None]
    steps = jnp.arange(ring)[None, :, None]
    pairs = jnp.arange(2)[None, None, :]
    return ((deep - steps) % ring) * 4 + (pair ^ pairs) * 2 + (core ^ cores)


def scatter_relative(own, partner, kept=jnp.bfloat16):
    ring = lax.axis_size("mp") // 4
    half = (wide(own) + wide(across_core(partner))).astype(kept)
    order = list(range(1, ring)) + [0]
    received = {step: across_pair(half[step, 1]) for step in order}
    moving = None
    for step in range(1, ring):
        total = wide(half[step, 0]) + wide(received[step])
        if moving is not None:
            total = total + wide(moving)
        moving = ring_step(total.astype(kept))
    return wide(half[0, 0]) + wide(received[0]) + wide(moving)


def to_relative(value):
    ring = lax.axis_size("mp") // 4
    order = relative_owner()
    both = value[order.reshape(-1)].reshape((2, ring, 2) + value.shape[1:])
    return both[0], both[1]


def from_relative(own, partner):
    count = lax.axis_size("mp")
    order = relative_owner().reshape(-1)
    place = jnp.zeros((count,), jnp.int32).at[order].set(jnp.arange(count, dtype=jnp.int32))
    both = jnp.stack([own, partner])
    return both.reshape((count,) + both.shape[3:])[place]


def gather_small(block):
    ring = lax.axis_size("mp") // 4
    deep, pair, core = coordinates()
    both = [block, across_core(block)]
    rows = jnp.stack(both)
    rows = jnp.stack([rows, across_pair(rows)])
    turned = [rows] + [ring_step(rows, step) for step in range(1, ring)]
    every = jnp.stack(turned)
    count = lax.axis_size("mp")
    flat = every.reshape((count,) + block.shape)
    position = jnp.arange(count)
    steps = (deep - position // 4) % ring
    place = steps * 4 + (pair ^ ((position // 2) % 2)) * 2 + (core ^ (position % 2))
    return flat[place]


def seq_gather(value):
    if lax.axis_size("seq") != 2:
        return lax.all_gather(value, "seq")
    other = lax.ppermute(value, "seq", [(0, 1), (1, 0)])
    first = lax.axis_index("seq") == 0
    return jnp.stack([jnp.where(first, value, other), jnp.where(first, other, value)])


def seq_scatter(value):
    if lax.axis_size("seq") != 2:
        return lax.psum_scatter(wide(value), "seq", scatter_dimension=0, tiled=False)
    mine = lax.axis_index("seq")
    other = lax.ppermute(bits(pick(value, 1 - mine)), "seq", [(0, 1), (1, 0)])
    return wide(pick(value, mine)) + wide(other)


def seq_sum(value):
    if lax.axis_size("seq") != 2:
        return lax.psum(wide(value), "seq")
    low = bits(value)
    return wide(low) + wide(lax.ppermute(low, "seq", [(0, 1), (1, 0)]))


def seq_entering(decay, state, backward):
    if lax.axis_size("seq") == 2:
        route = [(1, 0)] if backward else [(0, 1)]
        return lax.ppermute(state, "seq", route)
    return entering_2(
        (decay, state),
        "seq",
        chain_combine,
        (jnp.ones_like(decay), jnp.zeros_like(state)),
        backward,
    )[1]


def mp_exchange(value):
    return lax.all_to_all(value, "mp", split_axis=0, concat_axis=0, tiled=True)


EDGE = 16
TRANSPOSED = (((1,), (1,)), ((), ()))
ROWS_SUMMED = (((0,), (0,)), ((), ()))
PLAIN = (((1,), (0,)), ((), ()))


def product(left, right, dims=PLAIN):
    return lax.dot_general(left, right, dims, preferred_element_type=jnp.float32)


def halves_of(value):
    high = value.astype(jnp.bfloat16)
    return high, (value - high.astype(jnp.float32)).astype(jnp.bfloat16)


def fine(left, right, dims=PLAIN):
    left_high, left_low = halves_of(left)
    right_high, right_low = halves_of(right)
    small = product(left_high, right_low, dims) + product(left_low, right_high, dims)
    return product(left_high, right_high, dims) + small


def exact_right(left, right, dims=PLAIN):
    high, low = halves_of(left)
    return product(high, right, dims) + product(low, right, dims)


def exact_left(left, right, dims=PLAIN):
    high = right.astype(jnp.bfloat16)
    rest = right - high.astype(jnp.float32)
    middle = rest.astype(jnp.bfloat16)
    last = (rest - middle.astype(jnp.float32)).astype(jnp.bfloat16)
    return product(left, high, dims) + (product(left, middle, dims) + product(left, last, dims))


def softplus(value):
    return jnp.maximum(value, 0.0) + jnp.log1p(jnp.exp(-jnp.abs(value)))


def spread(value, heads, width):
    channel = width // heads
    lane = lax.broadcasted_iota(jnp.int32, (value.shape[0], width), 1)
    result = jnp.broadcast_to(value[:, heads - 1 : heads], (value.shape[0], width))
    for head in range(heads - 2, -1, -1):
        result = jnp.where(lane < (head + 1) * channel, value[:, head : head + 1], result)
    return result


def only_head(value, head, heads):
    channel = value.shape[1] // heads
    lane = lax.broadcasted_iota(jnp.int32, value.shape, 1)
    inside = (lane >= head * channel) & (lane < (head + 1) * channel)
    return jnp.where(inside, value, 0.0)


def head_sum_matrix(width, heads):
    channel = width // heads
    row = lax.broadcasted_iota(jnp.int32, (width, 128), 0) // channel
    lane = lax.broadcasted_iota(jnp.int32, (width, 128), 1)
    return (row == lane).astype(jnp.float32).astype(jnp.bfloat16)


def not_before(length, reverse=False):
    row = lax.broadcasted_iota(jnp.int32, (length, length), 0)
    lane = lax.broadcasted_iota(jnp.int32, (length, length), 1)
    return (row <= lane) if reverse else (row >= lane)


def ones_of(mask):
    return mask.astype(jnp.float32).astype(jnp.bfloat16)


def whole(shape):
    return pl.BlockSpec(shape, lambda b, *_: (0,) * len(shape))


def each(shape):
    return pl.BlockSpec((1,) + shape, lambda b, *_: (b,) + (0,) * len(shape))


def f32(*shape):
    return jax.ShapeDtypeStruct(shape, jnp.float32)


def bf16(*shape):
    return jax.ShapeDtypeStruct(shape, jnp.bfloat16)


def call(kernel, grid, in_specs, out_specs, out_shape, scratch=(), prefetch=0):
    return pl.pallas_call(
        kernel,
        grid_spec=pltpu.PrefetchScalarGridSpec(
            num_scalar_prefetch=prefetch,
            grid=grid,
            in_specs=in_specs,
            out_specs=out_specs,
            scratch_shapes=list(scratch),
        ),
        out_shape=out_shape,
        compiler_params=pltpu.CompilerParams(vmem_limit_bytes=56 * 1024 * 1024),
    )


def mixer_input(
    x, edge, gain, gate_w, value_w, state_w, step_w, value_taps, state_taps,
    value_bias, state_bias, step_shift, decay_rate, heads,
):
    count, length, model = x.shape
    inner, double = value_w.shape[1], state_w.shape[1]
    window = value_taps.shape[0]

    def kernel(
        x_ref, edge_ref, gain_ref, gate_ref, value_ref, state_ref, step_ref, vt_ref, st_ref,
        vb_ref, sb_ref, shift_ref, rate_ref,
        normed_out, gate_out, ev_out, es_out, pv_out, ps_out, step_out, decay_out, local_out,
    ):
        def norm(value):
            value = value.astype(jnp.float32)
            scale = lax.rsqrt(jnp.mean(value * value, axis=-1, keepdims=True) + epsilon)
            return (value * scale * gain_ref[...]).astype(jnp.bfloat16)

        normed = norm(x_ref[0])
        normed_out[0] = normed
        ev_out[0, EDGE:] = product(normed, value_ref[...])
        es_out[0, EDGE:] = product(normed, state_ref[...])
        step_raw = product(normed, step_ref[...])
        step_out[0] = step_raw
        gate_out[0] = product(normed, gate_ref[...])
        edge_normed = norm(edge_ref[0])
        ev_out[0, :EDGE] = product(edge_normed, value_ref[...])
        es_out[0, :EDGE] = product(edge_normed, state_ref[...])
        first = EDGE - window + 1
        pre_value = jnp.broadcast_to(vb_ref[...], (length, inner))
        pre_state = jnp.broadcast_to(sb_ref[...], (length, double))
        for tap in range(window):
            pre_value = pre_value + vt_ref[tap : tap + 1] * ev_out[0, first + tap : first + tap + length]
            pre_state = pre_state + st_ref[tap : tap + 1] * es_out[0, first + tap : first + tap + length]
        pv_out[0] = pre_value
        ps_out[0] = pre_state
        values = jax.nn.silu(pre_value)
        b_matrix = jax.nn.silu(pre_state[:, : double // 2])
        step = softplus(step_raw + shift_ref[...])
        decay = exact_left(ones_of(not_before(length)), -jnp.exp(rate_ref[...]) * step)
        decay_out[0] = decay
        tail = jnp.exp(decay[length - 1 : length] - decay) * step
        local_out[0] = fine(values * spread(tail, heads, inner), b_matrix, ROWS_SUMMED)

    return call(
        kernel,
        (count,),
        [
            each((length, model)), each((EDGE, model)), whole(gain.shape), whole(gate_w.shape),
            whole(value_w.shape), whole(state_w.shape), whole(step_w.shape), whole(value_taps.shape),
            whole(state_taps.shape), whole(value_bias.shape), whole(state_bias.shape),
            whole(step_shift.shape), whole(decay_rate.shape),
        ],
        [
            each((length, model)), each((length, inner)), each((length + EDGE, inner)),
            each((length + EDGE, double)), each((length, inner)), each((length, double)),
            each((length, 128)), each((length, 128)), each((inner, double // 2)),
        ],
        [
            bf16(count, length, model), f32(count, length, inner), f32(count, length + EDGE, inner),
            f32(count, length + EDGE, double), f32(count, length, inner), f32(count, length, double),
            f32(count, length, 128), f32(count, length, 128), f32(count, inner, double // 2),
        ],
    )(
        x, edge, gain, gate_w, value_w, state_w, step_w, value_taps, state_taps,
        value_bias, state_bias, step_shift, decay_rate,
    )


def decay_masks(decay, heads):
    length = decay.shape[0]
    causal = not_before(length)
    turned = decay.T
    return [
        jnp.exp(jnp.where(causal, decay[:, head : head + 1] - turned[head : head + 1], -1e30))
        for head in range(heads)
    ]


def mixer_within(pre_value, pre_state, step_raw, decay_sum, step_shift, skip, heads):
    count, length, inner = pre_value.shape
    double = pre_state.shape[2]

    def kernel(pv_ref, ps_ref, step_ref, decay_ref, shift_ref, skip_ref, within_out):
        values = jax.nn.silu(pv_ref[0])
        both = jax.nn.silu(ps_ref[0])
        b_matrix, c_matrix = both[:, : double // 2], both[:, double // 2 :]
        scaled = values * spread(softplus(step_ref[0] + shift_ref[...]), heads, inner)
        crossed = fine(c_matrix, b_matrix, TRANSPOSED)
        result = spread(skip_ref[...], heads, inner) * values
        for head, mask in enumerate(decay_masks(decay_ref[0], heads)):
            result = result + fine(crossed * mask, only_head(scaled, head, heads))
        within_out[0] = result

    return call(
        kernel,
        (count,),
        [
            each((length, inner)), each((length, double)), each((length, 128)), each((length, 128)),
            whole(step_shift.shape), whole(skip.shape),
        ],
        each((length, inner)),
        f32(count, length, inner),
    )(pre_value, pre_state, step_raw, decay_sum, step_shift, skip)


def mixer_output(order, within, pre_state, decay_sum, entering, gate_raw, gain, out_w, heads, owners):
    count, length, inner = within.shape
    double, model = pre_state.shape[2], out_w.shape[1]
    rows = length // owners
    half = owners // 2

    def kernel(
        order_ref, within_ref, ps_ref, decay_ref, state_ref, gate_ref, gain_ref, out_ref,
        ssm_out, scaled_out, square_out, own_out, partner_out, mixed,
    ):
        c_matrix = jax.nn.silu(ps_ref[0, :, double // 2 :])
        carried = fine(c_matrix, state_ref[0], TRANSPOSED)
        ssm = within_ref[0] + spread(jnp.exp(decay_ref[0]), heads, inner) * carried
        ssm_out[0] = ssm
        gated = ssm * jax.nn.silu(gate_ref[0])
        scaled = (gated * gain_ref[...]).astype(jnp.bfloat16)
        scaled_out[0] = scaled
        square_out[0] = exact_left(jnp.ones((8, inner), jnp.bfloat16), gated * gated, TRANSPOSED)
        mixed[...] = product(scaled, out_ref[...]).astype(jnp.bfloat16)
        for place in range(owners):
            start = pl.multiple_of(order_ref[place] * rows, rows)
            target = own_out if place < half else partner_out
            target[place % half] = mixed[pl.ds(start, rows)]

    blocks = pl.BlockSpec((half, rows, model), lambda b, *_: (0, b, 0))
    return call(
        kernel,
        (count,),
        [
            each((length, inner)), each((length, double)), each((length, 128)),
            each((inner, double // 2)), each((length, inner)), whole(gain.shape), whole(out_w.shape),
        ],
        [each((length, inner)), each((length, inner)), each((8, length)), blocks, blocks],
        [
            f32(count, length, inner), bf16(count, length, inner), f32(count, 8, length),
            bf16(half, count * rows, model), bf16(half, count * rows, model),
        ],
        [pltpu.VMEM((length, model), jnp.bfloat16)],
        1,
    )(order, within, pre_state, decay_sum, entering, gate_raw, gain, out_w)


def mixer_output_back(order, blocks, gate_raw, ssm, pre_state, decay_sum, gain, out_w, heads):
    count, length, inner = ssm.shape
    double, model = pre_state.shape[2], out_w.shape[1]
    owners, _, wide_model = blocks.shape
    rows = length // owners

    def kernel(
        order_ref, blocks_ref, gate_ref, ssm_ref, ps_ref, decay_ref, gain_ref, out_ref,
        mix_out, ssm_grad_out, gate_grad_out, state_out, gain_out, sums,
    ):
        for place in range(owners):
            start = pl.multiple_of(order_ref[place] * rows, rows)
            mix_out[0, pl.ds(start, rows)] = blocks_ref[place, :, :model]
            sums[pl.ds(start, rows)] = blocks_ref[place, :, model:].astype(jnp.float32)
        sum_grad = sums[:, 0:1] + sums[:, 1:2]
        scaled_grad = product(mix_out[0], out_ref[...], TRANSPOSED)
        gate, value = gate_ref[0], ssm_ref[0]
        opened = jax.nn.silu(gate)
        gated = value * opened

        @pl.when(pl.program_id(0) == 0)
        def _():
            gain_out[...] = jnp.zeros_like(gain_out)

        gain_out[...] += jnp.sum(scaled_grad * gated, axis=0, keepdims=True)
        gated_grad = scaled_grad * gain_ref[...] + 2.0 * gated * sum_grad
        ssm_grad = gated_grad * opened
        ssm_grad_out[0] = ssm_grad
        gate_grad_out[0] = (gated_grad * value * silu_slope(gate)).astype(jnp.bfloat16)
        c_matrix = jax.nn.silu(ps_ref[0, :, double // 2 :])
        carried_grad = spread(jnp.exp(decay_ref[0]), heads, inner) * ssm_grad
        state_out[0] = fine(carried_grad, c_matrix, ROWS_SUMMED)

    return call(
        kernel,
        (count,),
        [
            pl.BlockSpec((owners, rows, wide_model), lambda b, *_: (0, b, 0)),
            each((length, inner)), each((length, inner)), each((length, double)), each((length, 128)),
            whole(gain.shape), whole(out_w.shape),
        ],
        [
            each((length, model)), each((length, inner)), each((length, inner)),
            each((inner, double // 2)), whole((8, inner)),
        ],
        [
            bf16(count, length, model), f32(count, length, inner), bf16(count, length, inner),
            f32(count, inner, double // 2), f32(8, inner),
        ],
        [pltpu.VMEM((length, wide_model - model), jnp.float32)],
        1,
    )(order, blocks, gate_raw, ssm, pre_state, decay_sum, gain, out_w)


def mixer_within_back(pre_value, pre_state, step_raw, decay_sum, step_shift, ssm_grad, entering, heads):
    count, length, inner = pre_value.shape
    double = pre_state.shape[2]

    def kernel(pv_ref, ps_ref, step_ref, decay_ref, shift_ref, grad_ref, state_ref, scaled_out, both_out):
        values = jax.nn.silu(pv_ref[0])
        both = jax.nn.silu(ps_ref[0])
        b_matrix, c_matrix = both[:, : double // 2], both[:, double // 2 :]
        scaled = values * spread(softplus(step_ref[0] + shift_ref[...]), heads, inner)
        crossed = fine(c_matrix, b_matrix, TRANSPOSED)
        grad = grad_ref[0]
        decay = decay_ref[0]
        scaled_grad = jnp.zeros((length, inner), jnp.float32)
        crossed_grad = jnp.zeros((length, length), jnp.float32)
        for head, mask in enumerate(decay_masks(decay, heads)):
            head_grad = only_head(grad, head, heads)
            scaled_grad = scaled_grad + fine(crossed * mask, head_grad, ROWS_SUMMED)
            crossed_grad = crossed_grad + fine(head_grad, scaled, TRANSPOSED) * mask
        scaled_out[0] = scaled_grad
        both_out[0, :, : double // 2] = fine(crossed_grad, c_matrix, ROWS_SUMMED)
        carried_grad = spread(jnp.exp(decay), heads, inner) * grad
        both_out[0, :, double // 2 :] = fine(crossed_grad, b_matrix) + fine(carried_grad, state_ref[0])

    return call(
        kernel,
        (count,),
        [
            each((length, inner)), each((length, double)), each((length, 128)), each((length, 128)),
            whole(step_shift.shape), each((length, inner)), each((inner, double // 2)),
        ],
        [each((length, inner)), each((length, double))],
        [f32(count, length, inner), f32(count, length, double)],
    )(pre_value, pre_state, step_raw, decay_sum, step_shift, ssm_grad, entering)


def mixer_input_back(
    pre_value, pre_state, ext_value, ext_state, step_raw, decay_sum, ssm, ssm_grad, scaled_grad,
    state_part, entering, exit_grad, value_taps, state_taps, step_shift, decay_rate, skip, heads,
):
    count, length, inner = pre_value.shape
    double = pre_state.shape[2]
    window = value_taps.shape[0]

    def kernel(
        pv_ref, ps_ref, ev_ref, es_ref, step_ref, decay_ref, ssm_ref, grad_ref, scaled_ref, part_ref,
        state_ref, exit_ref, vt_ref, st_ref, shift_ref, rate_ref, skip_ref,
        value_out, state_out, edge_v_out, edge_s_out, step_out, taps_v_out, taps_s_out, head_out,
        room_v, room_s,
    ):
        pre_v, pre_s = pv_ref[0], ps_ref[0]
        values = jax.nn.silu(pre_v)
        b_matrix = jax.nn.silu(pre_s[:, : double // 2])
        grad, scaled = grad_ref[0], scaled_ref[0]
        step_pre = step_ref[0] + shift_ref[...]
        step = softplus(step_pre)
        rate = jnp.exp(rate_ref[...])
        decay = decay_ref[0]
        last = decay[length - 1 : length]
        remain = jnp.exp(last - decay)
        remain_wide = spread(remain, heads, inner)
        step_wide = spread(step, heads, inner)
        tail_wide = remain_wide * step_wide
        skip_wide = spread(skip_ref[...], heads, inner)
        leaving = exit_ref[0]
        passed = fine(b_matrix, leaving, TRANSPOSED)
        value_grad = scaled * step_wide + tail_wide * passed + skip_wide * grad
        b_grad = part_ref[0, :, : double // 2] + fine(tail_wide * values, leaving)
        summing = head_sum_matrix(inner, heads)
        crossing = values * passed
        left_part = exact_right(crossing * tail_wide, summing)
        decay_grad = (
            exact_right(grad * (ssm_ref[0] - skip_wide * values) - values * step_wide * scaled, summing)
            - left_part
        )
        total_grad = jnp.sum(left_part, axis=0, keepdims=True)
        state_dot = exact_left(jnp.ones((8, double // 2), jnp.bfloat16), leaving * state_ref[0], TRANSPOSED)
        total_grad = total_grad + jnp.exp(last) * exact_right(state_dot, summing)[:1]
        row = lax.broadcasted_iota(jnp.int32, decay_grad.shape, 0)
        decay_grad = decay_grad + jnp.where(row == length - 1, total_grad, 0.0)
        log_grad = exact_left(ones_of(not_before(length, True)), decay_grad)
        step_size_grad = exact_right(scaled * values + crossing * remain_wide, summing) - rate * log_grad
        step_raw_grad = step_size_grad * jax.nn.sigmoid(step_pre)
        step_out[0] = step_raw_grad.astype(jnp.bfloat16)
        skip_grad = exact_right(grad * values, summing)

        @pl.when(pl.program_id(0) == 0)
        def _():
            taps_v_out[...] = jnp.zeros_like(taps_v_out)
            taps_s_out[...] = jnp.zeros_like(taps_s_out)
            head_out[...] = jnp.zeros_like(head_out)
            for room in (room_v, room_s):
                room[:EDGE] = jnp.zeros((EDGE, room.shape[1]), jnp.float32)
                room[EDGE + length :] = jnp.zeros((EDGE, room.shape[1]), jnp.float32)

        head_out[0:1] += jnp.sum(step_raw_grad, axis=0, keepdims=True)
        head_out[1:2] += jnp.sum(-rate * step * log_grad, axis=0, keepdims=True)
        head_out[2:3] += jnp.sum(skip_grad, axis=0, keepdims=True)
        room_v[EDGE : EDGE + length] = value_grad * silu_slope(pre_v)
        room_s[EDGE : EDGE + length, : double // 2] = b_grad * silu_slope(pre_s[:, : double // 2])
        room_s[EDGE : EDGE + length, double // 2 :] = part_ref[0, :, double // 2 :] * silu_slope(
            pre_s[:, double // 2 :]
        )
        first = EDGE - window + 1
        for room, ext, taps, taps_out, out, edge_out in (
            (room_v, ev_ref, vt_ref, taps_v_out, value_out, edge_v_out),
            (room_s, es_ref, st_ref, taps_s_out, state_out, edge_s_out),
        ):
            pre_grad = room[EDGE : EDGE + length]
            taps_out[window : window + 1] += jnp.sum(pre_grad, axis=0, keepdims=True)
            inside = jnp.zeros(pre_grad.shape, jnp.float32)
            before = jnp.zeros((EDGE, pre_grad.shape[1]), jnp.float32)
            for tap in range(window):
                moved = ext[0, first + tap : first + tap + length]
                taps_out[tap : tap + 1] += jnp.sum(pre_grad * moved, axis=0, keepdims=True)
                ahead = window - 1 - tap
                weight = taps[tap : tap + 1]
                inside = inside + weight * room[EDGE + ahead : EDGE + ahead + length]
                before = before + weight * room[ahead : ahead + EDGE]
            out[0] = inside
            edge_out[0] = before

    return call(
        kernel,
        (count,),
        [
            each((length, inner)), each((length, double)), each((length + EDGE, inner)),
            each((length + EDGE, double)), each((length, 128)), each((length, 128)),
            each((length, inner)), each((length, inner)), each((length, inner)), each((length, double)),
            each((inner, double // 2)), each((inner, double // 2)), whole(value_taps.shape),
            whole(state_taps.shape), whole(step_shift.shape), whole(decay_rate.shape), whole(skip.shape),
        ],
        [
            each((length, inner)), each((length, double)), each((EDGE, inner)), each((EDGE, double)),
            each((length, 128)), whole((8, inner)), whole((8, double)), whole((8, 128)),
        ],
        [
            f32(count, length, inner), f32(count, length, double), f32(count, EDGE, inner),
            f32(count, EDGE, double), bf16(count, length, 128), f32(8, inner), f32(8, double), f32(8, 128),
        ],
        [
            pltpu.VMEM((length + 2 * EDGE, inner), jnp.float32),
            pltpu.VMEM((length + 2 * EDGE, double), jnp.float32),
        ],
    )(
        pre_value, pre_state, ext_value, ext_state, step_raw, decay_sum, ssm, ssm_grad, scaled_grad,
        state_part, entering, exit_grad, value_taps, state_taps, step_shift, decay_rate, skip,
    )


def mixer_project_back(
    order, value_local, state_local, edge_value, edge_state, gate_grad, step_grad, x,
    gate_w, value_w, state_w, step_w, owners,
):
    count, length, inner = value_local.shape
    double, model = state_local.shape[2], x.shape[2]
    rows = length // owners
    half = owners // 2

    def kernel(
        order_ref, value_ref, state_ref, ev_ref, es_ref, gate_grad_ref, step_grad_ref, x_ref,
        gate_ref, vw_ref, sw_ref, step_ref,
        own_out, partner_out, value_out, state_out, gain_out, mixed,
    ):
        body_rows = length - EDGE
        for part, edge, out in ((value_ref, ev_ref, value_out), (state_ref, es_ref, state_out)):
            out[0, :body_rows] = part[0, :body_rows].astype(jnp.bfloat16)
            out[0, body_rows:] = (part[0, body_rows:] + edge[0]).astype(jnp.bfloat16)
        grad = product(gate_grad_ref[0], gate_ref[...], TRANSPOSED)
        grad = grad + product(value_out[0], vw_ref[...], TRANSPOSED)
        grad = grad + product(state_out[0], sw_ref[...], TRANSPOSED)
        grad = grad + product(step_grad_ref[0], step_ref[...], TRANSPOSED)
        value = x_ref[0].astype(jnp.float32)
        scale = lax.rsqrt(jnp.mean(value * value, axis=-1, keepdims=True) + epsilon)

        @pl.when(pl.program_id(0) == 0)
        def _():
            gain_out[...] = jnp.zeros_like(gain_out)

        gain_out[...] += jnp.sum(grad * value * scale, axis=0, keepdims=True)
        mixed[...] = grad.astype(jnp.bfloat16)
        for place in range(owners):
            start = pl.multiple_of(order_ref[place] * rows, rows)
            target = own_out if place < half else partner_out
            target[place % half] = mixed[pl.ds(start, rows)]

    blocks = pl.BlockSpec((half, rows, model), lambda b, *_: (0, b, 0))
    return call(
        kernel,
        (count,),
        [
            each((length, inner)), each((length, double)), each((EDGE, inner)), each((EDGE, double)),
            each((length, inner)), each((length, 128)), each((length, model)), whole(gate_w.shape),
            whole(value_w.shape), whole(state_w.shape), whole(step_w.shape),
        ],
        [blocks, blocks, each((length, inner)), each((length, double)), whole((8, model))],
        [
            bf16(half, count * rows, model), bf16(half, count * rows, model), bf16(count, length, inner),
            bf16(count, length, double), f32(8, model),
        ],
        [pltpu.VMEM((length, model), jnp.bfloat16)],
        1,
    )(
        order, value_local, state_local, edge_value, edge_state, gate_grad, step_grad, x,
        gate_w, value_w, state_w, step_w,
    )


def body(
    tokens,
    target,
    lengths,
    routes,
    route_weight,
    in_gain,
    gate_proj,
    value_proj,
    state_proj,
    step_proj,
    conv_value,
    conv_value_bias,
    conv_state,
    conv_state_bias,
    step_bias,
    decay_log,
    skip_gain,
    mixer_gain,
    out_proj,
    ffn_gain,
    shared_gate,
    shared_up,
    shared_down,
    expert_gate,
    routed_up_weights,
    expert_down,
):
    mp_count = lax.axis_size("mp")
    slot_count, seq_count, model_width = tokens.shape
    seq_devices = lax.axis_size("seq")
    shared_expert_rows = slot_count // mp_count
    inner_width = gate_proj.shape[1]
    row_count = shared_expert_rows * seq_count
    window = conv_value.shape[0]
    gain_rows = in_gain.shape[0]
    state_rows = conv_state.shape[0]
    state_width = state_proj.shape[1]
    expert_count = expert_gate.shape[0] * mp_count

    packed = jnp.concatenate(
        [
            state_proj.reshape(-1),
            in_gain,
            ffn_gain,
            conv_state.reshape(-1),
            conv_state_bias,
        ]
    )
    route_rows = route_weight.transpose(1, 0, 2).reshape(row_count, -1)
    chosen = routes.transpose(1, 0, 2).reshape(row_count, -1, 1) == jnp.arange(expert_count, dtype=jnp.int32)
    coefficient = jnp.sum(jnp.where(chosen, route_rows[..., None], 0.0), axis=1)
    coefficient_high = rounded(coefficient)
    coefficient_low = coefficient - coefficient_high
    both_packed = seq_gather(packed)
    small = gather_small(
        jnp.concatenate(
            [
                both_packed.reshape(-1),
                bits(coefficient_high).reshape(-1),
                bits(coefficient_low).reshape(-1),
            ]
        )
    )
    width = packed.shape[0]
    weights_small = small[:, : seq_devices * width].reshape(mp_count, seq_devices, width)
    weights_small = jnp.moveaxis(weights_small, 1, 0).reshape(seq_devices * mp_count, width)
    cut = [gain_rows * state_width]
    for part in (gain_rows, gain_rows, conv_state.size):
        cut.append(cut[-1] + part)
    state_whole = weights_small[:, : cut[0]].reshape(-1, state_width)
    gain_first = weights_small[:, cut[0] : cut[1]].reshape(-1)
    gain_second = weights_small[:, cut[1] : cut[2]].reshape(-1)
    conv_state_whole = weights_small[:, cut[2] : cut[3]].reshape(-1, window)
    conv_bias_whole = weights_small[:, cut[3] :].reshape(-1)
    share = small[:, seq_devices * width :].reshape(mp_count, 2, row_count, expert_count)
    share = lax.dynamic_index_in_dim(share, lax.axis_index("mp"), 3, keepdims=False)
    share = wide(share[:, 0]) + wide(share[:, 1])
    share_own, share_partner = to_relative(share)

    columns = shared_gate.shape[1] // (seq_devices * mp_count)
    hidden_own = seq_devices * columns
    pair_cut = jnp.stack([shared_gate, shared_up]).reshape(2, gain_rows, seq_devices, mp_count, columns)
    pair_moved = mp_exchange(pair_cut.transpose(3, 0, 1, 2, 4).reshape(mp_count, -1))
    pair_all = seq_gather(pair_moved).reshape(
        seq_devices, mp_count, 2, gain_rows, hidden_own
    )
    pair_all = pair_all.transpose(2, 0, 1, 3, 4).reshape(2, model_width, hidden_own)
    gate_shared, up_shared = pair_all[0], pair_all[1]
    down_shared = seq_gather(shared_down).reshape(hidden_own, model_width)
    gate_weight, up_weight, down_weight = expert_gate[0], routed_up_weights[0], expert_down[0]

    order = relative_owner().reshape(-1).astype(jnp.int32)
    head_count = step_proj.shape[1]
    start_row = lax.axis_index("mp") * shared_expert_rows
    sequences = tokens.transpose(1, 0, 2)
    own_inputs = wide(
        lax.dynamic_slice_in_dim(sequences, start_row, shared_expert_rows, 1)
    ).reshape(row_count, model_width)
    edge_rows = shifted(tokens[slot_count - window + 1 :].transpose(1, 0, 2), "seq", 1)
    edge_rows = jnp.pad(edge_rows, ((0, 0), (EDGE - window + 1, 0), (0, 0)))
    lane_pad = ((0, 0), (0, 128 - head_count))
    step_weight = jnp.pad(step_proj, lane_pad)
    step_shift = jnp.pad(step_bias[None], lane_pad)
    decay_rate = jnp.pad(decay_log[None], lane_pad)
    skip_row = jnp.pad(skip_gain[None], lane_pad)
    state_taps = wide(conv_state_whole).T
    mixer = mixer_input(
        sequences,
        edge_rows,
        wide(gain_first)[None],
        gate_proj,
        value_proj,
        state_whole,
        step_weight,
        conv_value,
        state_taps,
        conv_value_bias[None],
        wide(conv_bias_whole)[None],
        step_shift,
        decay_rate,
        head_count,
    )
    normed, gate_raw, ext_value, ext_state, pre_value, pre_state, step_raw, decay_sum, local_state = mixer
    decay_total = jnp.exp(decay_sum[:, slot_count - 1, :head_count])
    state_shape = (seq_count, head_count, inner_width // head_count, STATE)

    def entering_of(state, backward):
        moved = seq_entering(decay_total, state.reshape(state_shape), backward)
        return moved.reshape(state.shape)

    entering = entering_of(local_state, False)
    within = mixer_within(pre_value, pre_state, step_raw, decay_sum, step_shift, skip_row, head_count)
    ssm, scaled_low, squares, mix_own, mix_partner = mixer_output(
        order,
        within,
        pre_state,
        decay_sum,
        entering,
        gate_raw,
        mixer_gain[None],
        out_proj,
        head_count,
        mp_count,
    )
    squares = squares[:, 0].reshape(seq_count, mp_count, shared_expert_rows).transpose(1, 0, 2)
    square_sum = jnp.sum(mp_exchange(squares.reshape(mp_count, row_count)), axis=0)
    ring = mp_count // 4
    pre_mix = scatter_relative(
        mix_own.reshape(ring, 2, row_count, model_width),
        mix_partner.reshape(ring, 2, row_count, model_width),
    )
    inv_norm = lax.rsqrt(square_sum / INNER + epsilon)[:, None]
    hidden = own_inputs + pre_mix * inv_norm
    ffn_input = rms_scale(hidden, wide(gain_second)).astype(jnp.bfloat16)

    def dot(left, right):
        return jnp.dot(left, right, preferred_element_type=jnp.float32)

    def dot_t(left, right):
        return lax.dot_general(
            left, right, (((1,), (1,)), ((), ())), preferred_element_type=jnp.float32
        )

    def t_dot(left, right):
        return lax.dot_general(
            left, right, (((0,), (0,)), ((), ())), preferred_element_type=jnp.float32
        )

    rows_own, rows_partner = gather_relative(ffn_input)
    all_rows = jnp.stack([rows_own, rows_partner]).reshape(-1, model_width)
    shares = jnp.stack([share_own, share_partner]).reshape(-1, 1)
    gate_activation = dot(all_rows, gate_weight)
    up_val = dot(all_rows, up_weight)
    act_val = bits(jax.nn.silu(gate_activation) * up_val)
    shared_gate_val = dot(all_rows, gate_shared)
    shared_up_val = dot(all_rows, up_shared)
    shared_act = bits(jax.nn.silu(shared_gate_val) * shared_up_val)
    partial_out = shares * wide(bits(dot(act_val, down_weight))) + dot(shared_act, down_shared)

    def halves(value):
        cut_value = bits(value).reshape((2,) + rows_own.shape)
        return cut_value[0], cut_value[1]

    output = hidden + scatter_relative(*halves(partial_out))

    def slots_first(value):
        return value.reshape(seq_count, shared_expert_rows, model_width).transpose(1, 0, 2)

    block_out = slots_first(output.astype(jnp.bfloat16))
    position = (
        lax.axis_index("seq") * slot_count
        + start_row
        + jnp.arange(shared_expert_rows, dtype=jnp.int32)
    )
    valid_mask = (position[None, :] < lengths[:, None]).astype(jnp.float32).reshape(row_count, 1)
    grad_out = (output - wide(target).transpose(1, 0, 2).reshape(row_count, model_width)) * valid_mask
    grad_own, grad_partner = gather_relative(bits(grad_out))
    all_grads = jnp.stack([grad_own, grad_partner]).reshape(-1, model_width)
    route_grads = bits(shares * wide(all_grads))
    activation_gradient = dot_t(route_grads, down_weight)
    egate_grad = bits(activation_gradient * up_val * silu_slope(gate_activation))
    expert_up_gradient = bits(activation_gradient * jax.nn.silu(gate_activation))
    shact_grad = dot_t(all_grads, down_shared)
    sgate_grad = bits(shact_grad * shared_up_val * silu_slope(shared_gate_val))
    sup_grad = bits(shact_grad * jax.nn.silu(shared_gate_val))
    partial_rows = (
        dot_t(egate_grad, gate_weight)
        + dot_t(expert_up_gradient, up_weight)
        + dot_t(sgate_grad, gate_shared)
        + dot_t(sup_grad, up_shared)
    )
    ffn_input_grad = scatter_relative(*halves(partial_rows))
    expert_down_grad = seq_sum(t_dot(act_val, route_grads))[None]
    expert_gate_grad = seq_sum(t_dot(all_rows, egate_grad))[None]
    expert_up_grad = seq_sum(t_dot(all_rows, expert_up_gradient))[None]
    shared_down_grad = seq_scatter(
        t_dot(shared_act, all_grads).reshape(seq_devices, columns, model_width)
    )
    pair_grad = jnp.stack([t_dot(all_rows, sgate_grad), t_dot(all_rows, sup_grad)])
    pair_grad = pair_grad.reshape(2, seq_devices, mp_count, gain_rows, hidden_own)
    pair_grad = seq_scatter(pair_grad.transpose(1, 2, 0, 3, 4))
    pair_grad = wide(mp_exchange(bits(pair_grad).reshape(mp_count, -1)))
    pair_grad = pair_grad.reshape(mp_count, 2, gain_rows, seq_devices, columns)
    pair_grad = pair_grad.transpose(1, 2, 3, 0, 4).reshape(2, gain_rows, -1)
    shared_gate_grad, shared_up_grad = pair_grad[0], pair_grad[1]

    _, second_norm_back = jax.vjp(rms_scale, hidden, wide(gain_second))
    hidden_part, ffn_gain_grad = second_norm_back(ffn_input_grad)
    hidden_grad_share = grad_out + hidden_part
    sum_grad_share = (
        jnp.sum(hidden_grad_share * pre_mix, axis=-1, keepdims=True)
        * (-0.5 / INNER)
        * inv_norm
        * inv_norm
        * inv_norm
    )
    sum_high = rounded(sum_grad_share)
    sum_low = sum_grad_share - sum_high
    mix_grad_send = jnp.concatenate(
        [
            bits(hidden_grad_share * inv_norm),
            bits(sum_high),
            bits(sum_low),
            jnp.zeros((row_count, 126), jnp.bfloat16),
        ],
        axis=-1,
    )
    mix_blocks = jnp.stack(gather_relative(mix_grad_send)).reshape(mp_count, row_count, -1)
    mix_grad_all, ssm_grad, gate_grad, entering_grad, mixer_gain_grad = mixer_output_back(
        order,
        mix_blocks,
        gate_raw,
        ssm,
        pre_state,
        decay_sum,
        mixer_gain[None],
        out_proj,
        head_count,
    )
    exit_grad = entering_of(entering_grad, True)
    scaled_value_grad, state_part_grad = mixer_within_back(
        pre_value, pre_state, step_raw, decay_sum, step_shift, ssm_grad, entering, head_count
    )
    value_local, state_local, edge_value, edge_state, step_grad, taps_value, taps_state, head_grads = (
        mixer_input_back(
            pre_value,
            pre_state,
            ext_value,
            ext_state,
            step_raw,
            decay_sum,
            ssm,
            ssm_grad,
            scaled_value_grad,
            state_part_grad,
            entering,
            exit_grad,
            conv_value,
            state_taps,
            step_shift,
            decay_rate,
            skip_row,
            head_count,
        )
    )
    edges = shifted(jnp.concatenate([edge_value, edge_state], axis=-1), "seq", -1)
    last_own, last_partner, value_grad, state_grad, in_gain_grad = mixer_project_back(
        order,
        value_local,
        state_local,
        edges[..., :inner_width],
        edges[..., inner_width:],
        gate_grad,
        step_grad,
        sequences,
        gate_proj,
        value_proj,
        state_whole,
        step_weight,
        mp_count,
    )

    def by_rows(value):
        return value.reshape(slot_count * seq_count, -1)

    out_proj_grad = t_dot(by_rows(scaled_low), by_rows(mix_grad_all))
    gate_proj_grad = t_dot(by_rows(normed), by_rows(gate_grad))
    value_proj_grad = t_dot(by_rows(normed), by_rows(value_grad))
    state_proj_grad = t_dot(by_rows(normed), by_rows(state_grad))
    step_proj_grad = t_dot(by_rows(normed), by_rows(step_grad))[:, :head_count]
    conv_value_grad = taps_value[:window]
    conv_state_grad = taps_state[:window].T
    conv_value_bias_grad = taps_value[window]
    conv_state_bias_grad = taps_state[window]
    step_bias_grad = head_grads[0, :head_count]
    decay_log_grad = head_grads[1, :head_count]
    skip_gain_grad = head_grads[2, :head_count]
    mixer_gain_grad = mixer_gain_grad[0]
    in_gain_grad = in_gain_grad[0]

    def by_owner(value):
        parts = value.reshape((seq_devices, mp_count, -1))
        return jnp.moveaxis(parts, 1, 0).reshape(mp_count, -1)

    extra = jnp.concatenate(
        [
            by_owner(state_proj_grad),
            by_owner(in_gain_grad),
            by_owner(ffn_gain_grad),
        ],
        axis=-1,
    )
    extra_rows = -(-extra.shape[1] // (8 * model_width)) * 8
    extra_size = extra.shape[1]
    extra = jnp.pad(extra, ((0, 0), (0, extra_rows * model_width - extra_size)))
    extra_own, extra_partner = to_relative(bits(extra).reshape(mp_count, extra_rows, model_width))
    normed_grad = scatter_relative(
        last_own.reshape(ring, 2, row_count, model_width),
        last_partner.reshape(ring, 2, row_count, model_width),
    )
    extra_sum = scatter_relative(extra_own, extra_partner).reshape(-1)[:extra_size]
    _, first_norm_back = jax.vjp(rms_scale, own_inputs, wide(gain_first))
    tokens_grad = slots_first(first_norm_back(normed_grad)[0] + hidden_grad_share)
    sizes = [gain_rows * state_width, gain_rows, gain_rows]
    parts, at = [], 0
    for size in sizes:
        parts.append(extra_sum[at : at + seq_devices * size].reshape(seq_devices, size))
        at += seq_devices * size
    extra_own = seq_scatter(jnp.concatenate(parts, axis=-1))
    state_proj_out = extra_own[: sizes[0]].reshape(gain_rows, state_width)
    at = sizes[0]
    in_gain_out = extra_own[at : at + gain_rows]
    at += gain_rows
    ffn_gain_out = extra_own[at : at + gain_rows]
    conv_small = jnp.concatenate(
        [
            conv_state_grad.reshape(seq_devices, mp_count, -1),
            conv_state_bias_grad.reshape(seq_devices, mp_count, -1),
        ],
        axis=-1,
    )
    conv_small = jnp.moveaxis(conv_small, 1, 0).reshape(mp_count, -1)
    conv_small = jnp.sum(mp_exchange(conv_small), axis=0)
    exact = (
        step_proj_grad,
        conv_value_grad,
        conv_value_bias_grad,
        step_bias_grad,
        decay_log_grad,
        skip_gain_grad,
        mixer_gain_grad,
        conv_small.reshape(seq_devices, -1),
    )
    flat = jnp.concatenate([part.reshape(-1) for part in exact])
    if seq_devices == 2:
        flat = flat + lax.ppermute(flat, "seq", [(0, 1), (1, 0)])
    else:
        flat = lax.psum(flat, "seq")
    exact_out, at = [], 0
    for part in exact:
        exact_out.append(flat[at : at + part.size].reshape(part.shape))
        at += part.size
    conv_own = pick(exact_out[7], lax.axis_index("seq"))
    conv_state_out = conv_own[: state_rows * window].reshape(state_rows, window)
    conv_state_bias_out = conv_own[state_rows * window :]
    return (
        block_out,
        tokens_grad,
        in_gain_out,
        seq_sum(gate_proj_grad),
        seq_sum(value_proj_grad),
        state_proj_out,
        exact_out[0],
        exact_out[1],
        exact_out[2],
        conv_state_out,
        conv_state_bias_out,
        exact_out[3],
        exact_out[4],
        exact_out[5],
        exact_out[6],
        seq_sum(out_proj_grad),
        ffn_gain_out,
        shared_gate_grad,
        shared_up_grad,
        shared_down_grad,
        expert_gate_grad,
        expert_up_grad,
        expert_down_grad,
    )


def solution(mesh):
    placed = (
        P("seq", None, None),
        P(("seq", "mp"), None, None),
        P(),
        P(("seq", "mp"), None, None),
        P(("seq", "mp"), None, None),
        P(("seq", "mp")),
        P(None, "mp"),
        P(None, "mp"),
        P(("seq", "mp"), None),
        P(None, "mp"),
        P(None, "mp"),
        P("mp"),
        P(("seq", "mp"), None),
        P(("seq", "mp")),
        P("mp"),
        P("mp"),
        P("mp"),
        P("mp"),
        P("mp", None),
        P(("seq", "mp")),
        P(("seq", "mp"), None),
        P(("seq", "mp"), None),
        P(("seq", "mp"), None),
        P("mp", None, None),
        P("mp", None, None),
        P("mp", None, None),
    )
    return jax.shard_map(
        body,
        mesh=mesh,
        in_specs=placed,
        out_specs=(
            P(("seq", "mp"), None, None),
            P(("seq", "mp"), None, None),
            P(("seq", "mp")),
            P(None, "mp"),
            P(None, "mp"),
            P(("seq", "mp"), None),
            P(None, "mp"),
            P(None, "mp"),
            P("mp"),
            P(("seq", "mp"), None),
            P(("seq", "mp")),
            P("mp"),
            P("mp"),
            P("mp"),
            P("mp"),
            P("mp", None),
            P(("seq", "mp")),
            P(("seq", "mp"), None),
            P(("seq", "mp"), None),
            P(("seq", "mp"), None),
            P("mp", None, None),
            P("mp", None, None),
            P("mp", None, None),
        ),
        check_vma=False,
    )
```

```python
import jax
import jax.numpy as jnp
from jax import lax
from jax.experimental import pallas as pl
from jax.experimental.pallas import tpu as pltpu
from jax.sharding import PartitionSpec as P

STATE = 128
INNER = 3072


epsilon = 1e-05
highest = lax.Precision.HIGHEST


def shifted(block, axis, distance):
    devices = range(lax.axis_size(axis))
    route = [(i - distance, i) for i in devices if i - distance in devices]
    return lax.ppermute(block, axis, route)


def entering_2(value, axis, join, neutral, backward):
    count, mine = (lax.axis_size(axis), lax.axis_index(axis))
    pieces = jax.tree.map(lambda part: lax.all_gather(part, axis), value)
    if backward:
        pieces = jax.tree.map(lambda part: part[::-1], pieces)
        mine = count - 1 - mine
    running = jax.tree.map(
        lambda part, zero: jnp.full_like(part, 0) + jnp.asarray(zero, part.dtype), value, neutral
    )

    def hop(position, running):
        longer = join(running, jax.tree.map(lambda part: part[position], pieces))
        return jax.tree.map(lambda new, old: jnp.where(position < mine, new, old), longer, running)

    return lax.fori_loop(0, count - 1, hop, running)


def rms_scale(values, gain):
    return values * lax.rsqrt(jnp.mean(values * values, axis=-1, keepdims=True) + epsilon) * gain


def silu_slope(values):
    sigmoid_val = jax.nn.sigmoid(values)
    return sigmoid_val * (1.0 + values * (1.0 - sigmoid_val))


def chain_combine(earlier, latter):
    return (earlier[0] * latter[0], latter[0][..., None, None] * earlier[1] + latter[1])


def bits(value):
    return value.astype(jnp.bfloat16)


def wide(value):
    return value.astype(jnp.float32)


def rounded(value):
    return lax.reduce_precision(value, 8, 7)


def mp_permute(value, target):
    count = lax.axis_size("mp")
    return lax.ppermute(value, "mp", [(i, target(i)) for i in range(count)])


def across_core(value):
    return mp_permute(value, lambda i: i ^ 1)


def across_pair(value):
    return mp_permute(value, lambda i: i ^ 2)


def ring_step(value, distance=1):
    count = lax.axis_size("mp")
    return mp_permute(value, lambda i: (i + 4 * distance) % count)


def coordinates():
    mine = lax.axis_index("mp")
    return mine // 4, (mine // 2) % 2, mine % 2


def pick(value, index, axis=0):
    return lax.dynamic_index_in_dim(value, index, axis, keepdims=False)


def relative_owner():
    ring = lax.axis_size("mp") // 4
    deep, pair, core = coordinates()
    cores = jnp.arange(2)[:, None, None]
    steps = jnp.array(distances())[None, :, None]
    pairs = jnp.arange(2)[None, None, :]
    return ((deep - steps) % ring) * 4 + (pair ^ pairs) * 2 + (core ^ cores)


def gather_small(block):
    count = lax.axis_size("mp")
    every = jnp.stack([block] + [ring_step(block, step) for step in distances()[1:]])
    every = jnp.stack([every, across_pair(every)], axis=1)
    every = jnp.stack([every, across_core(every)])
    order = relative_owner().reshape(-1)
    place = jnp.zeros((count,), jnp.int32).at[order].set(jnp.arange(count, dtype=jnp.int32))
    return every.reshape((count,) + block.shape)[place]


def seq_gather(value):
    if lax.axis_size("seq") != 2:
        return lax.all_gather(value, "seq")
    other = lax.ppermute(value, "seq", [(0, 1), (1, 0)])
    first = lax.axis_index("seq") == 0
    return jnp.stack([jnp.where(first, value, other), jnp.where(first, other, value)])


def seq_scatter(value):
    if lax.axis_size("seq") != 2:
        return lax.psum_scatter(wide(value), "seq", scatter_dimension=0, tiled=False)
    mine = lax.axis_index("seq")
    other = lax.ppermute(bits(pick(value, 1 - mine)), "seq", [(0, 1), (1, 0)])
    return wide(pick(value, mine)) + wide(other)


def seq_sum(value):
    if lax.axis_size("seq") != 2:
        return lax.psum(wide(value), "seq")
    low = bits(value)
    return wide(low) + wide(lax.ppermute(low, "seq", [(0, 1), (1, 0)]))


def seq_entering(decay, state, backward):
    if lax.axis_size("seq") == 2:
        route = [(1, 0)] if backward else [(0, 1)]
        return lax.ppermute(state, "seq", route)
    return entering_2(
        (decay, state),
        "seq",
        chain_combine,
        (jnp.ones_like(decay), jnp.zeros_like(state)),
        backward,
    )[1]


def mp_exchange(value):
    return lax.all_to_all(value, "mp", split_axis=0, concat_axis=0, tiled=True)


EDGE = 16
TRANSPOSED = (((1,), (1,)), ((), ()))
ROWS_SUMMED = (((0,), (0,)), ((), ()))
PLAIN = (((1,), (0,)), ((), ()))


def product(left, right, dims=PLAIN):
    return lax.dot_general(left, right, dims, preferred_element_type=jnp.float32)


def halves_of(value):
    high = value.astype(jnp.bfloat16)
    return high, (value - high.astype(jnp.float32)).astype(jnp.bfloat16)


def fine(left, right, dims=PLAIN):
    left_high, left_low = halves_of(left)
    right_high, right_low = halves_of(right)
    small = product(left_high, right_low, dims) + product(left_low, right_high, dims)
    return product(left_high, right_high, dims) + small


def exact_right(left, right, dims=PLAIN):
    high, low = halves_of(left)
    return product(high, right, dims) + product(low, right, dims)


def exact_left(left, right, dims=PLAIN):
    high = right.astype(jnp.bfloat16)
    rest = right - high.astype(jnp.float32)
    middle = rest.astype(jnp.bfloat16)
    last = (rest - middle.astype(jnp.float32)).astype(jnp.bfloat16)
    return product(left, high, dims) + (product(left, middle, dims) + product(left, last, dims))


def softplus(value):
    return jnp.maximum(value, 0.0) + jnp.log1p(jnp.exp(-jnp.abs(value)))


def spread(value, heads, width):
    channel = width // heads
    lane = lax.broadcasted_iota(jnp.int32, (value.shape[0], width), 1)
    result = jnp.broadcast_to(value[:, heads - 1 : heads], (value.shape[0], width))
    for head in range(heads - 2, -1, -1):
        result = jnp.where(lane < (head + 1) * channel, value[:, head : head + 1], result)
    return result


def only_head(value, head, heads):
    channel = value.shape[1] // heads
    lane = lax.broadcasted_iota(jnp.int32, value.shape, 1)
    inside = (lane >= head * channel) & (lane < (head + 1) * channel)
    return jnp.where(inside, value, 0.0)


def head_sum_matrix(width, heads):
    channel = width // heads
    row = lax.broadcasted_iota(jnp.int32, (width, 128), 0) // channel
    lane = lax.broadcasted_iota(jnp.int32, (width, 128), 1)
    return (row == lane).astype(jnp.float32).astype(jnp.bfloat16)


def not_before(length, reverse=False):
    row = lax.broadcasted_iota(jnp.int32, (length, length), 0)
    lane = lax.broadcasted_iota(jnp.int32, (length, length), 1)
    return (row <= lane) if reverse else (row >= lane)


def ones_of(mask):
    return mask.astype(jnp.float32).astype(jnp.bfloat16)


def whole(shape):
    return pl.BlockSpec(shape, lambda b, *_: (0,) * len(shape))


def each(shape):
    return pl.BlockSpec((1,) + shape, lambda b, *_: (b,) + (0,) * len(shape))


def f32(*shape):
    return jax.ShapeDtypeStruct(shape, jnp.float32)


def bf16(*shape):
    return jax.ShapeDtypeStruct(shape, jnp.bfloat16)


def call(kernel, grid, in_specs, out_specs, out_shape, scratch=(), prefetch=0, micros=2):
    return pl.pallas_call(
        kernel,
        grid_spec=pltpu.PrefetchScalarGridSpec(
            num_scalar_prefetch=prefetch,
            grid=grid,
            in_specs=in_specs,
            out_specs=out_specs,
            scratch_shapes=list(scratch),
        ),
        out_shape=out_shape,
        compiler_params=pltpu.CompilerParams(vmem_limit_bytes=56 * 1024 * 1024),
        cost_estimate=pl.CostEstimate(
            flops=int(micros * 9e+07), bytes_accessed=int(micros * 2.5e+05), transcendentals=0
        ),
    )


def mixer_input(
    x, edge, gain, gate_w, value_w, state_w, step_w, value_taps, state_taps,
    value_bias, state_bias, step_shift, decay_rate, heads,
):
    count, length, model = x.shape
    inner, double = value_w.shape[1], state_w.shape[1]
    window = value_taps.shape[0]

    def kernel(
        x_ref, edge_ref, gain_ref, gate_ref, value_ref, state_ref, step_ref, vt_ref, st_ref,
        vb_ref, sb_ref, shift_ref, rate_ref,
        normed_out, gate_out, ev_out, es_out, pv_out, ps_out, step_out, decay_out, local_out,
    ):
        def norm(value):
            value = value.astype(jnp.float32)
            scale = lax.rsqrt(jnp.mean(value * value, axis=-1, keepdims=True) + epsilon)
            return (value * scale * gain_ref[...]).astype(jnp.bfloat16)

        normed = norm(x_ref[0])
        normed_out[0] = normed
        ev_out[0, EDGE:] = product(normed, value_ref[...])
        es_out[0, EDGE:] = product(normed, state_ref[...])
        step_raw = product(normed, step_ref[...])
        step_out[0] = step_raw
        gate_out[0] = product(normed, gate_ref[...])
        edge_normed = norm(edge_ref[0])
        ev_out[0, :EDGE] = product(edge_normed, value_ref[...])
        es_out[0, :EDGE] = product(edge_normed, state_ref[...])
        first = EDGE - window + 1
        pre_value = jnp.broadcast_to(vb_ref[...], (length, inner))
        pre_state = jnp.broadcast_to(sb_ref[...], (length, double))
        for tap in range(window):
            pre_value = pre_value + vt_ref[tap : tap + 1] * ev_out[0, first + tap : first + tap + length]
            pre_state = pre_state + st_ref[tap : tap + 1] * es_out[0, first + tap : first + tap + length]
        pv_out[0] = pre_value
        ps_out[0] = pre_state
        values = jax.nn.silu(pre_value)
        b_matrix = jax.nn.silu(pre_state[:, : double // 2])
        step = softplus(step_raw + shift_ref[...])
        decay = exact_left(ones_of(not_before(length)), -jnp.exp(rate_ref[...]) * step)
        decay_out[0] = decay
        tail = jnp.exp(decay[length - 1 : length] - decay) * step
        local_out[0] = fine(values * spread(tail, heads, inner), b_matrix, ROWS_SUMMED)

    return call(
        kernel,
        (count,),
        [
            each((length, model)), each((EDGE, model)), whole(gain.shape), whole(gate_w.shape),
            whole(value_w.shape), whole(state_w.shape), whole(step_w.shape), whole(value_taps.shape),
            whole(state_taps.shape), whole(value_bias.shape), whole(state_bias.shape),
            whole(step_shift.shape), whole(decay_rate.shape),
        ],
        [
            each((length, model)), each((length, inner)), each((length + EDGE, inner)),
            each((length + EDGE, double)), each((length, inner)), each((length, double)),
            each((length, 128)), each((length, 128)), each((inner, double // 2)),
        ],
        [
            bf16(count, length, model), f32(count, length, inner), f32(count, length + EDGE, inner),
            f32(count, length + EDGE, double), f32(count, length, inner), f32(count, length, double),
            f32(count, length, 128), f32(count, length, 128), f32(count, inner, double // 2),
        ],
        micros=11,
    )(
        x, edge, gain, gate_w, value_w, state_w, step_w, value_taps, state_taps,
        value_bias, state_bias, step_shift, decay_rate,
    )


def decay_masks(decay, heads):
    length = decay.shape[0]
    causal = not_before(length)
    turned = decay.T
    return [
        jnp.exp(jnp.where(causal, decay[:, head : head + 1] - turned[head : head + 1], -1e30))
        for head in range(heads)
    ]


def mixer_within(pre_value, pre_state, step_raw, decay_sum, step_shift, skip, heads):
    count, length, inner = pre_value.shape
    double = pre_state.shape[2]

    def kernel(pv_ref, ps_ref, step_ref, decay_ref, shift_ref, skip_ref, within_out):
        values = jax.nn.silu(pv_ref[0])
        both = jax.nn.silu(ps_ref[0])
        b_matrix, c_matrix = both[:, : double // 2], both[:, double // 2 :]
        scaled = values * spread(softplus(step_ref[0] + shift_ref[...]), heads, inner)
        crossed = fine(c_matrix, b_matrix, TRANSPOSED)
        result = spread(skip_ref[...], heads, inner) * values
        for head, mask in enumerate(decay_masks(decay_ref[0], heads)):
            result = result + fine(crossed * mask, only_head(scaled, head, heads))
        within_out[0] = result

    return call(
        kernel,
        (count,),
        [
            each((length, inner)), each((length, double)), each((length, 128)), each((length, 128)),
            whole(step_shift.shape), whole(skip.shape),
        ],
        each((length, inner)),
        f32(count, length, inner),
        micros=6,
    )(pre_value, pre_state, step_raw, decay_sum, step_shift, skip)


def mixer_output(order, within, pre_state, decay_sum, entering, gate_raw, gain, out_w, heads, owners):
    count, length, inner = within.shape
    double, model = pre_state.shape[2], out_w.shape[1]
    rows = length // owners
    half = owners // 2

    def kernel(
        order_ref, within_ref, ps_ref, decay_ref, state_ref, gate_ref, gain_ref, out_ref,
        ssm_out, scaled_out, *outs,
    ):
        part_outs, mixed = outs[:-1], outs[-1]
        c_matrix = jax.nn.silu(ps_ref[0, :, double // 2 :])
        carried = fine(c_matrix, state_ref[0], TRANSPOSED)
        ssm = within_ref[0] + spread(jnp.exp(decay_ref[0]), heads, inner) * carried
        ssm_out[0] = ssm
        gated = ssm * jax.nn.silu(gate_ref[0])
        scaled = (gated * gain_ref[...]).astype(jnp.bfloat16)
        scaled_out[0] = scaled
        squares = jnp.sum(gated * gated, axis=-1, keepdims=True)
        mixed[:, :model] = product(scaled, out_ref[...]).astype(jnp.bfloat16)
        tail = jnp.zeros((length, 128), jnp.float32)
        mixed[:, model:] = two_parts(squares, tail).astype(jnp.bfloat16)
        for place in range(owners):
            start = pl.multiple_of(order_ref[place] * rows, rows)
            part_outs[place // half][place % half // 2, place % 2] = mixed[pl.ds(start, rows)]

    blocks = pl.BlockSpec((half // 2, 2, rows, model + 128), lambda b, *_: (0, 0, b, 0))
    return call(
        kernel,
        (count,),
        [
            each((length, inner)), each((length, double)), each((length, 128)),
            each((inner, double // 2)), each((length, inner)), whole(gain.shape), whole(out_w.shape),
        ],
        [each((length, inner)), each((length, inner))] + [blocks] * 2,
        [f32(count, length, inner), bf16(count, length, inner)]
        + [bf16(half // 2, 2, count * rows, model + 128)] * 2,
        [pltpu.VMEM((length, model + 128), jnp.bfloat16)],
        1,
        micros=7,
    )(order, within, pre_state, decay_sum, entering, gate_raw, gain, out_w)


def mixer_output_back(order, blocks, gate_raw, ssm, pre_state, decay_sum, gain, out_w, heads):
    count, length, inner = ssm.shape
    double, model = pre_state.shape[2], out_w.shape[1]
    owners, wide_model = len(blocks), blocks[0].shape[1]
    rows = length // owners

    def kernel(order_ref, *refs):
        blocks_ref = refs[:owners]
        gate_ref, ssm_ref, ps_ref, decay_ref, gain_ref, out_ref = refs[owners : owners + 6]
        mix_out, ssm_grad_out, gate_grad_out, state_out, gain_out, sums = refs[owners + 6 :]
        for place in range(owners):
            start = pl.multiple_of(order_ref[place] * rows, rows)
            mix_out[0, pl.ds(start, rows)] = blocks_ref[place][:, :model]
            sums[pl.ds(start, rows)] = blocks_ref[place][:, model:].astype(jnp.float32)
        sum_grad = sums[:, 0:1] + sums[:, 1:2]
        scaled_grad = product(mix_out[0], out_ref[...], TRANSPOSED)
        gate, value = gate_ref[0], ssm_ref[0]
        opened = jax.nn.silu(gate)
        gated = value * opened

        @pl.when(pl.program_id(0) == 0)
        def _():
            gain_out[...] = jnp.zeros_like(gain_out)

        gain_out[...] += jnp.sum(scaled_grad * gated, axis=0, keepdims=True)
        gated_grad = scaled_grad * gain_ref[...] + 2.0 * gated * sum_grad
        ssm_grad = gated_grad * opened
        ssm_grad_out[0] = ssm_grad
        gate_grad_out[0] = (gated_grad * value * silu_slope(gate)).astype(jnp.bfloat16)
        c_matrix = jax.nn.silu(ps_ref[0, :, double // 2 :])
        carried_grad = spread(jnp.exp(decay_ref[0]), heads, inner) * ssm_grad
        state_out[0] = fine(carried_grad, c_matrix, ROWS_SUMMED)

    return call(
        kernel,
        (count,),
        [pl.BlockSpec((rows, wide_model), lambda b, *_: (b, 0))] * owners
        + [
            each((length, inner)), each((length, inner)), each((length, double)), each((length, 128)),
            whole(gain.shape), whole(out_w.shape),
        ],
        [
            each((length, model)), each((length, inner)), each((length, inner)),
            each((inner, double // 2)), whole((8, inner)),
        ],
        [
            bf16(count, length, model), f32(count, length, inner), bf16(count, length, inner),
            f32(count, inner, double // 2), f32(8, inner),
        ],
        [pltpu.VMEM((length, wide_model - model), jnp.float32)],
        1,
        micros=8,
    )(order, *blocks, gate_raw, ssm, pre_state, decay_sum, gain, out_w)


def mixer_within_back(pre_value, pre_state, step_raw, decay_sum, step_shift, ssm_grad, entering, heads):
    count, length, inner = pre_value.shape
    double = pre_state.shape[2]

    def kernel(pv_ref, ps_ref, step_ref, decay_ref, shift_ref, grad_ref, state_ref, scaled_out, both_out):
        values = jax.nn.silu(pv_ref[0])
        both = jax.nn.silu(ps_ref[0])
        b_matrix, c_matrix = both[:, : double // 2], both[:, double // 2 :]
        scaled = values * spread(softplus(step_ref[0] + shift_ref[...]), heads, inner)
        crossed = fine(c_matrix, b_matrix, TRANSPOSED)
        grad = grad_ref[0]
        decay = decay_ref[0]
        scaled_grad = jnp.zeros((length, inner), jnp.float32)
        crossed_grad = jnp.zeros((length, length), jnp.float32)
        for head, mask in enumerate(decay_masks(decay, heads)):
            head_grad = only_head(grad, head, heads)
            scaled_grad = scaled_grad + fine(crossed * mask, head_grad, ROWS_SUMMED)
            crossed_grad = crossed_grad + fine(head_grad, scaled, TRANSPOSED) * mask
        scaled_out[0] = scaled_grad
        both_out[0, :, : double // 2] = fine(crossed_grad, c_matrix, ROWS_SUMMED)
        carried_grad = spread(jnp.exp(decay), heads, inner) * grad
        both_out[0, :, double // 2 :] = fine(crossed_grad, b_matrix) + fine(carried_grad, state_ref[0])

    return call(
        kernel,
        (count,),
        [
            each((length, inner)), each((length, double)), each((length, 128)), each((length, 128)),
            whole(step_shift.shape), each((length, inner)), each((inner, double // 2)),
        ],
        [each((length, inner)), each((length, double))],
        [f32(count, length, inner), f32(count, length, double)],
        micros=9,
    )(pre_value, pre_state, step_raw, decay_sum, step_shift, ssm_grad, entering)


def mixer_input_back(
    pre_value, pre_state, ext_value, ext_state, step_raw, decay_sum, ssm, ssm_grad, scaled_grad,
    state_part, entering, exit_grad, value_taps, state_taps, step_shift, decay_rate, skip, heads,
):
    count, length, inner = pre_value.shape
    double = pre_state.shape[2]
    window = value_taps.shape[0]

    def kernel(
        pv_ref, ps_ref, ev_ref, es_ref, step_ref, decay_ref, ssm_ref, grad_ref, scaled_ref, part_ref,
        state_ref, exit_ref, vt_ref, st_ref, shift_ref, rate_ref, skip_ref,
        value_out, state_out, edge_v_out, edge_s_out, step_out, taps_v_out, taps_s_out, head_out,
        room_v, room_s,
    ):
        pre_v, pre_s = pv_ref[0], ps_ref[0]
        values = jax.nn.silu(pre_v)
        b_matrix = jax.nn.silu(pre_s[:, : double // 2])
        grad, scaled = grad_ref[0], scaled_ref[0]
        step_pre = step_ref[0] + shift_ref[...]
        step = softplus(step_pre)
        rate = jnp.exp(rate_ref[...])
        decay = decay_ref[0]
        last = decay[length - 1 : length]
        remain = jnp.exp(last - decay)
        remain_wide = spread(remain, heads, inner)
        step_wide = spread(step, heads, inner)
        tail_wide = remain_wide * step_wide
        skip_wide = spread(skip_ref[...], heads, inner)
        leaving = exit_ref[0]
        passed = fine(b_matrix, leaving, TRANSPOSED)
        value_grad = scaled * step_wide + tail_wide * passed + skip_wide * grad
        b_grad = part_ref[0, :, : double // 2] + fine(tail_wide * values, leaving)
        summing = head_sum_matrix(inner, heads)
        crossing = values * passed
        left_part = exact_right(crossing * tail_wide, summing)
        decay_grad = (
            exact_right(grad * (ssm_ref[0] - skip_wide * values) - values * step_wide * scaled, summing)
            - left_part
        )
        total_grad = jnp.sum(left_part, axis=0, keepdims=True)
        state_dot = exact_left(jnp.ones((8, double // 2), jnp.bfloat16), leaving * state_ref[0], TRANSPOSED)
        total_grad = total_grad + jnp.exp(last) * exact_right(state_dot, summing)[:1]
        row = lax.broadcasted_iota(jnp.int32, decay_grad.shape, 0)
        decay_grad = decay_grad + jnp.where(row == length - 1, total_grad, 0.0)
        log_grad = exact_left(ones_of(not_before(length, True)), decay_grad)
        step_size_grad = exact_right(scaled * values + crossing * remain_wide, summing) - rate * log_grad
        step_raw_grad = step_size_grad * jax.nn.sigmoid(step_pre)
        step_out[0] = step_raw_grad.astype(jnp.bfloat16)
        skip_grad = exact_right(grad * values, summing)

        @pl.when(pl.program_id(0) == 0)
        def _():
            taps_v_out[...] = jnp.zeros_like(taps_v_out)
            taps_s_out[...] = jnp.zeros_like(taps_s_out)
            head_out[...] = jnp.zeros_like(head_out)
            for room in (room_v, room_s):
                room[:EDGE] = jnp.zeros((EDGE, room.shape[1]), jnp.float32)
                room[EDGE + length :] = jnp.zeros((EDGE, room.shape[1]), jnp.float32)

        head_out[0:1] += jnp.sum(step_raw_grad, axis=0, keepdims=True)
        head_out[1:2] += jnp.sum(-rate * step * log_grad, axis=0, keepdims=True)
        head_out[2:3] += jnp.sum(skip_grad, axis=0, keepdims=True)
        room_v[EDGE : EDGE + length] = value_grad * silu_slope(pre_v)
        room_s[EDGE : EDGE + length, : double // 2] = b_grad * silu_slope(pre_s[:, : double // 2])
        room_s[EDGE : EDGE + length, double // 2 :] = part_ref[0, :, double // 2 :] * silu_slope(
            pre_s[:, double // 2 :]
        )
        first = EDGE - window + 1
        for room, ext, taps, taps_out, out, edge_out in (
            (room_v, ev_ref, vt_ref, taps_v_out, value_out, edge_v_out),
            (room_s, es_ref, st_ref, taps_s_out, state_out, edge_s_out),
        ):
            pre_grad = room[EDGE : EDGE + length]
            taps_out[window : window + 1] += jnp.sum(pre_grad, axis=0, keepdims=True)
            inside = jnp.zeros(pre_grad.shape, jnp.float32)
            before = jnp.zeros((EDGE, pre_grad.shape[1]), jnp.float32)
            for tap in range(window):
                moved = ext[0, first + tap : first + tap + length]
                taps_out[tap : tap + 1] += jnp.sum(pre_grad * moved, axis=0, keepdims=True)
                ahead = window - 1 - tap
                weight = taps[tap : tap + 1]
                inside = inside + weight * room[EDGE + ahead : EDGE + ahead + length]
                before = before + weight * room[ahead : ahead + EDGE]
            out[0] = inside
            edge_out[0] = before

    return call(
        kernel,
        (count,),
        [
            each((length, inner)), each((length, double)), each((length + EDGE, inner)),
            each((length + EDGE, double)), each((length, 128)), each((length, 128)),
            each((length, inner)), each((length, inner)), each((length, inner)), each((length, double)),
            each((inner, double // 2)), each((inner, double // 2)), whole(value_taps.shape),
            whole(state_taps.shape), whole(step_shift.shape), whole(decay_rate.shape), whole(skip.shape),
        ],
        [
            each((length, inner)), each((length, double)), each((EDGE, inner)), each((EDGE, double)),
            each((length, 128)), whole((8, inner)), whole((8, double)), whole((8, 128)),
        ],
        [
            f32(count, length, inner), f32(count, length, double), f32(count, EDGE, inner),
            f32(count, EDGE, double), bf16(count, length, 128), f32(8, inner), f32(8, double), f32(8, 128),
        ],
        [
            pltpu.VMEM((length + 2 * EDGE, inner), jnp.float32),
            pltpu.VMEM((length + 2 * EDGE, double), jnp.float32),
        ],
        micros=13,
    )(
        pre_value, pre_state, ext_value, ext_state, step_raw, decay_sum, ssm, ssm_grad, scaled_grad,
        state_part, entering, exit_grad, value_taps, state_taps, step_shift, decay_rate, skip,
    )


def mixer_project_back(
    order, value_local, state_local, edge_value, edge_state, gate_grad, step_grad, x,
    gate_w, value_w, state_w, step_w, owners,
):
    count, length, inner = value_local.shape
    double, model = state_local.shape[2], x.shape[2]
    rows = length // owners
    half = owners // 2

    def kernel(
        order_ref, value_ref, state_ref, ev_ref, es_ref, gate_grad_ref, step_grad_ref, x_ref,
        gate_ref, vw_ref, sw_ref, step_ref,
        value_out, state_out, gain_out, *outs,
    ):
        part_outs, mixed = outs[:-1], outs[-1]
        body_rows = length - EDGE
        for part, edge, out in ((value_ref, ev_ref, value_out), (state_ref, es_ref, state_out)):
            out[0, :body_rows] = part[0, :body_rows].astype(jnp.bfloat16)
            out[0, body_rows:] = (part[0, body_rows:] + edge[0]).astype(jnp.bfloat16)
        grad = product(gate_grad_ref[0], gate_ref[...], TRANSPOSED)
        grad = grad + product(value_out[0], vw_ref[...], TRANSPOSED)
        grad = grad + product(state_out[0], sw_ref[...], TRANSPOSED)
        grad = grad + product(step_grad_ref[0], step_ref[...], TRANSPOSED)
        value = x_ref[0].astype(jnp.float32)
        scale = lax.rsqrt(jnp.mean(value * value, axis=-1, keepdims=True) + epsilon)

        @pl.when(pl.program_id(0) == 0)
        def _():
            gain_out[...] = jnp.zeros_like(gain_out)

        gain_out[...] += jnp.sum(grad * value * scale, axis=0, keepdims=True)
        mixed[...] = grad.astype(jnp.bfloat16)
        for place in range(owners):
            start = pl.multiple_of(order_ref[place] * rows, rows)
            part_outs[place // half][place % half // 2, place % 2] = mixed[pl.ds(start, rows)]

    blocks = pl.BlockSpec((half // 2, 2, rows, model), lambda b, *_: (0, 0, b, 0))
    return call(
        kernel,
        (count,),
        [
            each((length, inner)), each((length, double)), each((EDGE, inner)), each((EDGE, double)),
            each((length, inner)), each((length, 128)), each((length, model)), whole(gate_w.shape),
            whole(value_w.shape), whole(state_w.shape), whole(step_w.shape),
        ],
        [each((length, inner)), each((length, double)), whole((8, model))] + [blocks] * 2,
        [bf16(count, length, inner), bf16(count, length, double), f32(8, model)]
        + [bf16(half // 2, 2, count * rows, model)] * 2,
        [pltpu.VMEM((length, model), jnp.bfloat16)],
        1,
        micros=10,
    )(
        order, value_local, state_local, edge_value, edge_state, gate_grad, step_grad, x,
        gate_w, value_w, state_w, step_w,
    )


def total_of(refs):
    result = refs[0][...].astype(jnp.float32)
    for ref in refs[1:]:
        result = result + ref[...].astype(jnp.float32)
    return result


def two_parts(value, like):
    lane = lax.broadcasted_iota(jnp.int32, like.shape, len(like.shape) - 1)
    high = value.astype(jnp.bfloat16).astype(jnp.float32)
    return jnp.where(lane == 0, high, jnp.where(lane == 1, value - high, 0.0))


def store_sum(total, tail, out_refs):
    model = total.shape[-1] - tail
    for place, out in enumerate(out_refs):
        part = total[place] if len(out_refs) > 1 else total
        out[:, :model] = part[:, :model].astype(jnp.bfloat16)
        if tail:
            column = part[:, model : model + 1] + part[:, model + 1 : model + 2]
            out[:, model:] = two_parts(column, part[:, model:]).astype(jnp.bfloat16)


def add_pairs(left, right, tail):
    steps, _, rows, width = left.shape

    def kernel(left_ref, right_ref, *out_refs):
        for step in range(steps):
            total = left_ref[step].astype(jnp.float32) + right_ref[step].astype(jnp.float32)
            store_sum(total, tail, out_refs[2 * step : 2 * step + 2])

    sums = call(
        kernel,
        (1,),
        [whole(left.shape)] * 2,
        [whole((rows, width))] * (2 * steps),
        [bf16(rows, width)] * (2 * steps),
        micros=3,
    )(left, right)
    return list(sums[0::2]), list(sums[1::2])


def add_blocks(left, right, tail):
    def kernel(left_ref, right_ref, out_ref):
        store_sum(total_of((left_ref, right_ref)), tail, [out_ref])

    return call(
        kernel, (1,), [whole(left.shape)] * 2, whole(left.shape), bf16(*left.shape)
    )(left, right)


def after(value, *others):
    return lax.optimization_barrier((value, others))[0]


def distances():
    ring = lax.axis_size("mp") // 4
    return sorted(range(ring), key=lambda step: min(step, ring - step))


def gather_blocks(block, early=None, ties=()):
    ring = lax.axis_size("mp") // 4
    own, partner, result = [], [], None
    arrived = [block] + [ring_step(block, step) for step in distances()[1:]]
    for step, tie in enumerate(ties):
        arrived[step] = after(arrived[step], tie)
    for step, held in enumerate(arrived):
        both = [held, across_pair(held)]
        if early is not None and step == ring // 2:
            result = early(own + partner)
        if early is not None and step == ring - 1:
            partner += [across_core(value) for value in after(both, result[-1])]
        else:
            partner += [across_core(value) for value in both]
        own += both
    return own + partner, result


def scatter_core(own, partner, tail=0):
    return add_pairs(own, across_core(partner), tail)


def scatter_deep(kept, sent, tail=0):
    ring = len(kept)
    received = [across_pair(block) for block in sent]
    moving = [add_blocks(kept[step], received[step], tail) for step in range(1, ring)]
    result = [kept[0], received[0]]
    for step in range(1, ring):
        result.append(ring_step(moving[step - 1], ring - distances()[step]))
    return result, moving


def hidden_rows(parts, own_inputs, gain):
    rows, model = own_inputs.shape

    def kernel(*refs):
        part_refs, (x_ref, gain_ref, hidden_out, mix_out, inv_out, low_out) = refs[:-6], refs[-6:]
        total = total_of(part_refs)
        mixed = total[:, :model]
        squares = total[:, model : model + 1] + total[:, model + 1 : model + 2]
        inv_norm = lax.rsqrt(squares / INNER + epsilon)
        hidden = x_ref[...].astype(jnp.float32) + mixed * inv_norm
        hidden_out[...] = hidden
        mix_out[...] = mixed
        inv_out[...] = jnp.broadcast_to(inv_norm, inv_out.shape)
        low_out[...] = rms_scale(hidden, gain_ref[...]).astype(jnp.bfloat16)

    return call(
        kernel,
        (1,),
        [whole(part.shape) for part in parts] + [whole(own_inputs.shape), whole(gain.shape)],
        [whole((rows, model)), whole((rows, model)), whole((rows, 128)), whole((rows, model))],
        [f32(rows, model), f32(rows, model), f32(rows, 128), bf16(rows, model)],
    )(*parts, own_inputs, gain)


def output_rows(parts, hidden, target, valid):
    rows, model = hidden.shape

    def kernel(*refs):
        part_refs, (hidden_ref, target_ref, valid_ref, block_out, grad_out, low_out) = refs[:-6], refs[-6:]
        output = hidden_ref[...] + total_of(part_refs)
        block_out[...] = output.astype(jnp.bfloat16)
        grad = (output - target_ref[...].astype(jnp.float32)) * valid_ref[...]
        grad_out[...] = grad
        low_out[...] = grad.astype(jnp.bfloat16)

    return call(
        kernel,
        (1,),
        [whole(part.shape) for part in parts]
        + [whole(hidden.shape), whole(target.shape), whole(valid.shape)],
        [whole((rows, model))] * 3,
        [bf16(rows, model), f32(rows, model), bf16(rows, model)],
    )(*parts, hidden, target, valid)


def hidden_rows_back(parts, grad_out, hidden, mixed, inv_norm, gain):
    rows, model = hidden.shape

    def kernel(*refs):
        part_refs = refs[:-8]
        grad_ref, hidden_ref, mix_ref, inv_ref, gain_ref, hidden_out, send_out, gain_out = refs[-8:]
        input_grad = total_of(part_refs)
        value = hidden_ref[...]
        scale = lax.rsqrt(jnp.mean(value * value, axis=-1, keepdims=True) + epsilon)
        gained = input_grad * gain_ref[...]
        dot_sum = jnp.sum(gained * value, axis=-1, keepdims=True)
        grad = grad_ref[...] + scale * gained - value * (scale * scale * scale * dot_sum / model)
        hidden_out[...] = grad
        gain_out[...] = jnp.broadcast_to(
            jnp.sum(input_grad * value * scale, axis=0, keepdims=True), gain_out.shape
        )
        inv = inv_ref[:, 0:1]
        send_out[:, :model] = (grad * inv).astype(jnp.bfloat16)
        sum_grad = jnp.sum(grad * mix_ref[...], axis=-1, keepdims=True) * (-0.5 / INNER) * inv * inv * inv
        send_out[:, model:] = two_parts(sum_grad, inv_ref[...]).astype(jnp.bfloat16)

    return call(
        kernel,
        (1,),
        [whole(part.shape) for part in parts]
        + [whole(grad_out.shape), whole(hidden.shape), whole(mixed.shape), whole(inv_norm.shape), whole(gain.shape)],
        [whole((rows, model)), whole((rows, model + 128)), whole((8, model))],
        [f32(rows, model), bf16(rows, model + 128), f32(8, model)],
    )(*parts, grad_out, hidden, mixed, inv_norm, gain)


def token_rows_back(parts, hidden_grad, own_inputs, gain):
    rows, model = hidden_grad.shape

    def kernel(*refs):
        part_refs, (grad_ref, x_ref, gain_ref, out) = refs[:-4], refs[-4:]
        normed_grad = total_of(part_refs)
        value = x_ref[...].astype(jnp.float32)
        scale = lax.rsqrt(jnp.mean(value * value, axis=-1, keepdims=True) + epsilon)
        gained = normed_grad * gain_ref[...]
        dot_sum = jnp.sum(gained * value, axis=-1, keepdims=True)
        out[...] = grad_ref[...] + scale * gained - value * (scale * scale * scale * dot_sum / model)

    return call(
        kernel,
        (1,),
        [whole(part.shape) for part in parts]
        + [whole(hidden_grad.shape), whole(own_inputs.shape), whole(gain.shape)],
        whole((rows, model)),
        f32(rows, model),
    )(*parts, hidden_grad, own_inputs, gain)


def store_parts(value, out_refs):
    for place, out in enumerate(out_refs):
        size = value.shape[0] // len(out_refs)
        out[...] = value[place * size : (place + 1) * size].reshape(out.shape).astype(jnp.bfloat16)


def experts_forward(blocks, share, gate_w, up_w, down_w, pair_w, pair_down):
    rows, model = blocks[0].shape
    count, hidden = len(blocks), gate_w.shape[1]
    total, double = rows * count, pair_w.shape[1]

    def kernel(*refs):
        block_refs = refs[:count]
        share_ref, gate_ref, up_ref, down_ref, pair_ref, pd_ref = refs[count : count + 6]
        rows_out, gate_out, up_out, both_out, act_out, shared_out = refs[count + 6 : count + 12]
        part_refs = refs[count + 12 :]
        for place, block in enumerate(block_refs):
            rows_out[place * rows : (place + 1) * rows] = block[...]
        value = rows_out[...]
        gate = product(value, gate_ref[...])
        up = product(value, up_ref[...])
        gate_out[...] = gate
        up_out[...] = up
        act = (jax.nn.silu(gate) * up).astype(jnp.bfloat16)
        act_out[...] = act
        both = product(value, pair_ref[...])
        both_out[...] = both
        lane = lax.broadcasted_iota(jnp.int32, both.shape, 1)
        shared = jax.nn.silu(both) * pltpu.roll(both, double // 2, 1)
        shared = jnp.where(lane < double // 2, shared, 0.0).astype(jnp.bfloat16)
        shared_out[...] = shared
        result = product(act, down_ref[...]).astype(jnp.bfloat16).astype(jnp.float32)
        store_parts(share_ref[...] * result + product(shared, pd_ref[...]), part_refs)

    parts, steps = 2, count // 4
    return call(
        kernel,
        (1,),
        [whole(block.shape) for block in blocks]
        + [whole(w.shape) for w in (share, gate_w, up_w, down_w, pair_w, pair_down)],
        [whole((total, model)), whole((total, hidden)), whole((total, hidden)), whole((total, double))]
        + [whole((total, hidden)), whole((total, double))]
        + [whole((steps, 2, rows, model))] * parts,
        [bf16(total, model), f32(total, hidden), f32(total, hidden), f32(total, double)]
        + [bf16(total, hidden), bf16(total, double)]
        + [bf16(steps, 2, rows, model)] * parts,
        micros=8,
    )(*blocks, share, gate_w, up_w, down_w, pair_w, pair_down)


def experts_backward(blocks, share, gate, up, both, gate_w, up_w, down_w, pair_w, pair_down):
    rows, model = blocks[0].shape
    count, hidden = len(blocks), gate_w.shape[1]
    total, double = rows * count, pair_w.shape[1]

    def kernel(*refs):
        block_refs = refs[:count]
        share_ref, g_ref, u_ref, both_ref, gate_ref, up_ref, down_ref, pair_ref, pd_ref = refs[count : count + 9]
        grads_out, gate_out, up_out, shared_out = refs[count + 9 : count + 13]
        part_refs = refs[count + 13 :]
        for place, block in enumerate(block_refs):
            grads_out[place * rows : (place + 1) * rows] = block[...]
        grad = grads_out[...]
        routed = (share_ref[...] * grad.astype(jnp.float32)).astype(jnp.bfloat16)
        act_grad = product(routed, down_ref[...], TRANSPOSED)
        gate = g_ref[...]
        gate_out[...] = (act_grad * u_ref[...] * silu_slope(gate)).astype(jnp.bfloat16)
        up_out[...] = (act_grad * jax.nn.silu(gate)).astype(jnp.bfloat16)
        pair_value = both_ref[...]
        turned = pltpu.roll(pair_value, double // 2, 1)
        lane = lax.broadcasted_iota(jnp.int32, pair_value.shape, 1)
        factor = jnp.where(lane < double // 2, turned * silu_slope(pair_value), jax.nn.silu(turned))
        shared_out[...] = (product(grad, pd_ref[...], TRANSPOSED) * factor).astype(jnp.bfloat16)
        result = product(gate_out[...], gate_ref[...], TRANSPOSED)
        result = result + product(up_out[...], up_ref[...], TRANSPOSED)
        store_parts(result + product(shared_out[...], pair_ref[...], TRANSPOSED), part_refs)

    parts, steps = 2, count // 4
    return call(
        kernel,
        (1,),
        [whole(block.shape) for block in blocks]
        + [whole(w.shape) for w in (share, gate, up, both, gate_w, up_w, down_w, pair_w, pair_down)],
        [whole((total, model)), whole((total, hidden)), whole((total, hidden)), whole((total, double))]
        + [whole((steps, 2, rows, model))] * parts,
        [bf16(total, model), bf16(total, hidden), bf16(total, hidden), bf16(total, double)]
        + [bf16(steps, 2, rows, model)] * parts,
        micros=9,
    )(*blocks, share, gate, up, both, gate_w, up_w, down_w, pair_w, pair_down)


def experts_weights(groups):
    rows, grads, share, act, shared, gate_grad, up_grad, pair_grad = groups[0]
    model, hidden, double = rows.shape[1], act.shape[1], shared.shape[1]
    width = 256 if model % 256 == 0 else model
    each_group = len(groups[0])

    steps = model // width
    runs = [(2, 2, 2), (2, 2, 2), (2, 2, 2)] if steps == 6 else [(steps,)] * 3

    def kernel(*refs):
        *piece_outs, pair_out, pair_down_out = refs[len(groups) * each_group :]
        sums = [0.0] * 5
        for group in range(len(groups)):
            x, g, s, a, sa, gg, ug, pg = refs[group * each_group : (group + 1) * each_group]
            routed = (s[...] * g[...].astype(jnp.float32)).astype(jnp.bfloat16)
            sums[0] = sums[0] + product(a[...], routed, ROWS_SUMMED)
            sums[1] = sums[1] + product(x[...], gg[...], ROWS_SUMMED)
            sums[2] = sums[2] + product(x[...], ug[...], ROWS_SUMMED)
            sums[3] = sums[3] + product(x[...], pg[...], ROWS_SUMMED)
            sums[4] = sums[4] + product(sa[...], g[...], ROWS_SUMMED)
        pair_out[...] = sums[3].astype(jnp.bfloat16)
        pair_down_out[...] = sums[4].astype(jnp.bfloat16)
        number = 0
        for kind in range(3):
            first = 0
            for run in runs[kind]:
                store_piece(piece_outs[number], sums[kind], first, run)
                number, first = number + 1, first + run

    def store_piece(out, value, first, run):
        @pl.when((pl.program_id(0) >= first) & (pl.program_id(0) < first + run))
        def _():
            out[...] = value.astype(jnp.bfloat16)

    in_specs = []
    for group in groups:
        total = group[0].shape[0]
        columns = pl.BlockSpec((total, width), lambda d: (0, d))
        in_specs += [columns, columns] + [whole(value.shape) for value in group[2:]]

    def piece_spec(kind, first, run):
        if kind < 2:
            return pl.BlockSpec((width, hidden), lambda d: (jnp.clip(d - first, 0, run - 1), 0))
        return pl.BlockSpec((hidden, width), lambda d: (0, jnp.clip(d - first, 0, run - 1)))

    out_specs, shapes = [], []
    for place, kind in enumerate((2, 0, 1)):
        first = 0
        for run in runs[place]:
            out_specs.append(piece_spec(kind, first, run))
            shapes.append(bf16(width * run, hidden) if kind < 2 else bf16(hidden, width * run))
            first += run
    outs = call(
        kernel,
        (steps,),
        in_specs,
        out_specs
        + [
            pl.BlockSpec((width, double), lambda d: (d, 0)),
            pl.BlockSpec((double, width), lambda d: (0, d)),
        ],
        shapes + [bf16(model, double), bf16(double, model)],
        micros=11,
    )(*[value for group in groups for value in group])
    return outs[:-2], [len(run) for run in runs], outs[-2], outs[-1]


def mixer_weights(normed, gate_grad, value_grad, state_grad):
    count, length, model = normed.shape
    width = 256 if model % 256 == 0 else model
    inner = gate_grad.shape[2]

    def kernel(normed_ref, gate_ref, value_ref, state_ref, both_out, state_out):
        def summed(grad):
            total = 0.0
            for place in range(count):
                total = total + product(normed_ref[place], grad[place], ROWS_SUMMED)
            return total.astype(jnp.bfloat16)

        def shift(start):
            row = lax.broadcasted_iota(jnp.int32, (inner, 2 * inner), 0)
            lane = lax.broadcasted_iota(jnp.int32, (inner, 2 * inner), 1)
            return ones_of(row + start == lane)

        both = product(summed(gate_ref), shift(0)) + product(summed(value_ref), shift(inner))
        both_out[...] = both.astype(jnp.bfloat16)
        state_out[...] = summed(state_ref)

    grads = (gate_grad, value_grad, state_grad)
    return call(
        kernel,
        (model // width,),
        [pl.BlockSpec((count, length, width), lambda d: (0, 0, d))] + [whole(grad.shape) for grad in grads],
        [
            pl.BlockSpec((width, 2 * inner), lambda d: (d, 0)),
            pl.BlockSpec((width, state_grad.shape[2]), lambda d: (d, 0)),
        ],
        [bf16(model, 2 * inner), bf16(model, state_grad.shape[2])],
        micros=8,
    )(normed, *grads)


def body(
    tokens,
    target,
    lengths,
    routes,
    route_weight,
    in_gain,
    gate_proj,
    value_proj,
    state_proj,
    step_proj,
    conv_value,
    conv_value_bias,
    conv_state,
    conv_state_bias,
    step_bias,
    decay_log,
    skip_gain,
    mixer_gain,
    out_proj,
    ffn_gain,
    shared_gate,
    shared_up,
    shared_down,
    expert_gate,
    routed_up_weights,
    expert_down,
):
    mp_count = lax.axis_size("mp")
    slot_count, seq_count, model_width = tokens.shape
    seq_devices = lax.axis_size("seq")
    shared_expert_rows = slot_count // mp_count
    inner_width = gate_proj.shape[1]
    row_count = shared_expert_rows * seq_count
    window = conv_value.shape[0]
    gain_rows = in_gain.shape[0]
    state_rows = conv_state.shape[0]
    state_width = state_proj.shape[1]
    expert_count = expert_gate.shape[0] * mp_count

    packed = jnp.concatenate(
        [
            state_proj.reshape(-1),
            in_gain,
            ffn_gain,
            conv_state.reshape(-1),
            conv_state_bias,
        ]
    )
    route_rows = route_weight.transpose(1, 0, 2).reshape(row_count, -1)
    chosen = routes.transpose(1, 0, 2).reshape(row_count, -1, 1) == jnp.arange(expert_count, dtype=jnp.int32)
    coefficient = jnp.sum(jnp.where(chosen, route_rows[..., None], 0.0), axis=1)
    coefficient_high = rounded(coefficient)
    coefficient_low = coefficient - coefficient_high
    columns = shared_gate.shape[1] // (seq_devices * mp_count)
    hidden_own = seq_devices * columns
    pair_cut = jnp.stack([shared_gate, shared_up]).reshape(2, gain_rows, seq_devices, mp_count, columns)
    pair_cut = pair_cut.transpose(3, 1, 0, 2, 4).reshape(mp_count, -1)
    both_packed = seq_gather(packed)
    small = gather_small(
        jnp.concatenate(
            [
                both_packed.reshape(-1),
                bits(coefficient_high).reshape(-1),
                bits(coefficient_low).reshape(-1),
            ]
        )
    )
    width = packed.shape[0]
    weights_small = small[:, : seq_devices * width].reshape(mp_count, seq_devices, width)
    weights_small = jnp.moveaxis(weights_small, 1, 0).reshape(seq_devices * mp_count, width)
    cut = [gain_rows * state_width]
    for part in (gain_rows, gain_rows, conv_state.size):
        cut.append(cut[-1] + part)
    state_whole = weights_small[:, : cut[0]].reshape(-1, state_width)
    gain_first = weights_small[:, cut[0] : cut[1]].reshape(-1)
    gain_second = weights_small[:, cut[1] : cut[2]].reshape(-1)
    conv_state_whole = weights_small[:, cut[2] : cut[3]].reshape(-1, window)
    conv_bias_whole = weights_small[:, cut[3] :].reshape(-1)
    share = small[:, seq_devices * width :].reshape(mp_count, 2, row_count, expert_count)
    share = lax.dynamic_index_in_dim(share, lax.axis_index("mp"), 3, keepdims=False)
    share = wide(share[:, 0]) + wide(share[:, 1])
    ring = mp_count // 4
    order = relative_owner().reshape(-1).astype(jnp.int32)
    share = share[order].reshape(2, ring, 2 * row_count)
    ring_groups = [tuple(range(ring // 2)), tuple(range(ring // 2, ring))]
    shares = [share[:, group[0] : group[-1] + 1].reshape(-1, 1) for group in ring_groups]

    gate_weight, up_weight, down_weight = expert_gate[0], routed_up_weights[0], expert_down[0]

    head_count = step_proj.shape[1]
    start_row = lax.axis_index("mp") * shared_expert_rows
    sequences = tokens.transpose(1, 0, 2)
    own_inputs = lax.dynamic_slice_in_dim(sequences, start_row, shared_expert_rows, 1)
    own_inputs = own_inputs.reshape(row_count, model_width)
    edge_rows = shifted(tokens[slot_count - window + 1 :].transpose(1, 0, 2), "seq", 1)
    edge_rows = jnp.pad(edge_rows, ((0, 0), (EDGE - window + 1, 0), (0, 0)))
    lane_pad = ((0, 0), (0, 128 - head_count))
    step_weight = jnp.pad(step_proj, lane_pad)
    step_shift = jnp.pad(step_bias[None], lane_pad)
    decay_rate = jnp.pad(decay_log[None], lane_pad)
    skip_row = jnp.pad(skip_gain[None], lane_pad)
    state_taps = wide(conv_state_whole).T
    mixer = mixer_input(
        sequences,
        edge_rows,
        wide(gain_first)[None],
        gate_proj,
        value_proj,
        state_whole,
        step_weight,
        conv_value,
        state_taps,
        conv_value_bias[None],
        wide(conv_bias_whole)[None],
        step_shift,
        decay_rate,
        head_count,
    )
    normed, gate_raw, ext_value, ext_state, pre_value, pre_state, step_raw, decay_sum, local_state = mixer
    decay_total = jnp.exp(decay_sum[:, slot_count - 1, :head_count])
    state_shape = (seq_count, head_count, inner_width // head_count, STATE)

    def entering_of(state, backward):
        moved = seq_entering(decay_total, state.reshape(state_shape), backward)
        return moved.reshape(state.shape)

    entering = entering_of(local_state, False)
    within = mixer_within(pre_value, pre_state, step_raw, decay_sum, step_shift, skip_row, head_count)
    ssm, scaled_low, *mix_parts = mixer_output(
        order,
        within,
        pre_state,
        decay_sum,
        entering,
        gate_raw,
        mixer_gain[None],
        out_proj,
        head_count,
        mp_count,
    )
    first_gain, second_gain = wide(gain_first)[None], wide(gain_second)[None]
    kept, sent = scatter_core(*mix_parts, 128)
    pair_moved = mp_exchange(after(pair_cut, sent))
    pair_weight = seq_gather(pair_moved).reshape(model_width, 2 * hidden_own)
    down_shared = seq_gather(after(shared_down, sent)).reshape(hidden_own, model_width)
    pair_down = jnp.concatenate([down_shared, down_shared])
    mix_sums, _ = scatter_deep(kept, sent, 128)
    hidden, pre_mix, inv_norm, ffn_input = hidden_rows(
        after(mix_sums, pair_moved), own_inputs, second_gain
    )

    def of_group(blocks, group):
        half = 2 * ring
        picked = [2 * step + side for step in group for side in (0, 1)]
        return [blocks[core * half + place] for core in (0, 1) for place in picked]

    def of_groups(parts_of_groups):
        both = [scatter_core(*parts) for parts in parts_of_groups]
        return sum([kept for kept, _ in both], []), sum([sent for _, sent in both], [])

    expert_weights = (gate_weight, up_weight, down_weight, pair_weight, pair_down)
    row_blocks, first_forward = gather_blocks(
        ffn_input, lambda blocks: experts_forward(blocks, shares[0], *expert_weights)
    )
    forwards = [
        first_forward,
        experts_forward(of_group(row_blocks, ring_groups[1]), shares[1], *expert_weights),
    ]
    position = (
        lax.axis_index("seq") * slot_count
        + start_row
        + jnp.arange(shared_expert_rows, dtype=jnp.int32)
    )
    valid_mask = (position[None, :] < lengths[:, None]).astype(jnp.float32).reshape(row_count, 1)
    block_rows, grad_out, grad_low = output_rows(
        scatter_deep(*of_groups([result[6:] for result in forwards]))[0],
        hidden,
        target.transpose(1, 0, 2).reshape(row_count, model_width),
        valid_mask,
    )

    def slots_first(value):
        return value.reshape(seq_count, shared_expert_rows, model_width).transpose(1, 0, 2)

    block_out = slots_first(block_rows)
    grad_blocks, first_backward = gather_blocks(
        grad_low,
        lambda blocks: experts_backward(blocks, shares[0], *forwards[0][1:4], *expert_weights),
    )
    backwards = [
        first_backward,
        experts_backward(
            of_group(grad_blocks, ring_groups[1]), shares[1], *forwards[1][1:4], *expert_weights
        ),
    ]
    kept, sent = of_groups([result[4:] for result in backwards])
    expert_parts, part_counts, pair_grad, pair_down_grad = experts_weights(
        [
            (after(ahead[0], sent), back[0], share_rows, ahead[4], ahead[5], back[1], back[2], back[3])
            for ahead, back, share_rows in zip(forwards, backwards, shares)
        ]
    )
    row_sums, _ = scatter_deep(after(kept, pair_down_grad), sent)

    def seq_moved(value):
        return lax.ppermute(value, "seq", [(0, 1), (1, 0)])

    paired = seq_devices == 2
    chunks = len(expert_parts)
    expert_moved = [None] * chunks
    early_chunks, mix_ties = 5 if chunks == 9 else 0, ()
    if paired:
        for place in range(early_chunks):
            expert_moved[place] = seq_moved(expert_parts[place])
        row_sums = after(row_sums, expert_moved[: min(early_chunks, 1)])
        mix_ties = [(), *expert_moved[1 : max(early_chunks - 2, 1)]]
    hidden_grad, mix_grad_send, ffn_gain_grad = hidden_rows_back(
        row_sums,
        grad_out,
        hidden,
        pre_mix,
        inv_norm,
        second_gain,
    )
    mix_blocks, _ = gather_blocks(mix_grad_send, None, mix_ties)
    if paired and early_chunks:
        mix_blocks = after(mix_blocks, expert_moved[early_chunks - 2])
    mix_grad_all, ssm_grad, gate_grad, entering_grad, mixer_gain_grad = mixer_output_back(
        order,
        mix_blocks,
        gate_raw,
        ssm,
        pre_state,
        decay_sum,
        mixer_gain[None],
        out_proj,
        head_count,
    )
    exit_grad = entering_of(entering_grad, True)
    within_grad = ssm_grad
    if paired and early_chunks:
        within_grad = after(ssm_grad, expert_moved[early_chunks - 1])
    scaled_value_grad, state_part_grad = mixer_within_back(
        pre_value, pre_state, step_raw, decay_sum, step_shift, within_grad, entering, head_count
    )
    def by_rows(value):
        return value.reshape(slot_count * seq_count, -1)

    out_proj_grad = lax.dot_general(
        by_rows(scaled_low),
        by_rows(after(mix_grad_all, scaled_value_grad)),
        ROWS_SUMMED,
        preferred_element_type=jnp.float32,
    )
    out_proj_part = bits(out_proj_grad)
    scaled_value_grad = after(scaled_value_grad, out_proj_part)
    if paired:
        out_proj_moved = seq_moved(after(out_proj_part, scaled_value_grad))
    if paired and early_chunks:
        expert_moved[6] = seq_moved(expert_parts[6])
        expert_moved[5] = seq_moved(after(expert_parts[5], scaled_value_grad))
        exit_grad = after(exit_grad, expert_moved[6])
    shared_down_grad = seq_scatter(
        after(pair_down_grad, scaled_value_grad)[:hidden_own].reshape(seq_devices, columns, model_width)
    )
    value_local, state_local, edge_value, edge_state, step_grad, taps_value, taps_state, head_grads = (
        mixer_input_back(
            pre_value,
            pre_state,
            ext_value,
            ext_state,
            step_raw,
            decay_sum,
            ssm,
            ssm_grad,
            scaled_value_grad,
            state_part_grad,
            entering,
            exit_grad,
            conv_value,
            state_taps,
            step_shift,
            decay_rate,
            skip_row,
            head_count,
        )
    )
    exact = (
        taps_value[:window],
        taps_value[window],
        head_grads[0, :head_count],
        head_grads[1, :head_count],
        head_grads[2, :head_count],
        mixer_gain_grad[0],
        taps_state[:window].T,
        taps_state[window],
    )
    flat = jnp.concatenate([part.reshape(-1) for part in exact])
    step_proj_grad = lax.dot_general(
        by_rows(normed), by_rows(step_grad), ROWS_SUMMED, preferred_element_type=jnp.float32
    )[:, :head_count]
    step_flat = step_proj_grad.reshape(-1)
    edges = shifted(jnp.concatenate([edge_value, edge_state], axis=-1), "seq", -1)
    if paired:
        flat = flat + seq_moved(flat)
        edges = after(edges, flat, out_proj_moved, shared_down_grad, expert_moved[5:6] if early_chunks else ())
    else:
        flat = lax.psum(flat, "seq")
    value_grad, state_grad, in_gain_grad, *last_parts = mixer_project_back(
        order,
        value_local,
        state_local,
        edges[..., :inner_width],
        edges[..., inner_width:],
        gate_grad,
        step_grad,
        sequences,
        gate_proj,
        value_proj,
        state_whole,
        step_weight,
        mp_count,
    )

    if paired:
        step_flat = step_flat + seq_moved(step_flat)
        last_parts[0] = after(last_parts[0], step_flat)
        if early_chunks:
            expert_moved[7] = seq_moved(after(expert_parts[7], edges))
            last_parts[0] = after(last_parts[0], expert_moved[7])
    else:
        step_flat = lax.psum(step_flat, "seq")
    kept, sent = scatter_core(*last_parts)
    if paired and early_chunks == 0:
        expert_moved = [seq_moved(after(part, value_grad)) for part in expert_parts]
    both_proj_grad, state_proj_grad = mixer_weights(
        after(normed, sent), gate_grad, value_grad, state_grad
    )
    in_gain_grad, pair_grad = after((in_gain_grad, pair_grad), sent)
    in_gain_grad = in_gain_grad[0]
    pair_extra = pair_grad.reshape(seq_devices, mp_count, -1)

    def by_owner(value):
        return value.reshape(seq_devices, mp_count, -1)

    exact_out, at = [], 0
    for part in exact:
        exact_out.append(flat[at : at + part.size].reshape(part.shape))
        at += part.size
    mine = lax.axis_index("seq")
    conv_small = jnp.concatenate(
        [pick(by_owner(exact_out[6]), mine), pick(by_owner(exact_out[7]), mine)], axis=-1
    )
    conv_high = rounded(conv_small)
    extra = jnp.concatenate(
        [
            by_owner(state_proj_grad),
            bits(by_owner(in_gain_grad)),
            bits(by_owner(ffn_gain_grad[0])),
            pair_extra,
        ],
        axis=-1,
    )
    local_extra = extra
    if paired and early_chunks:
        expert_moved[-1] = seq_moved(after(expert_parts[-1], local_extra))
    last_sums, moving = scatter_deep(after(kept, extra), sent)
    extra_low = bits(seq_scatter(extra))
    extra = jnp.concatenate(
        [extra_low, bits(conv_high), bits(conv_small - conv_high)], axis=-1
    )
    extra = mp_exchange(after(extra, last_sums))
    tokens_grad = slots_first(
        token_rows_back(last_sums, hidden_grad, own_inputs, first_gain)
    )
    cuts = [gain_rows * state_width]
    for size in (gain_rows, gain_rows, pair_extra.shape[2], conv_small.shape[1]):
        cuts.append(cuts[-1] + size)
    pair_grad = wide(extra[:, cuts[2] : cuts[3]])
    extra_own = jnp.sum(wide(jnp.concatenate([extra[:, : cuts[2]], extra[:, cuts[3] :]], axis=1)), axis=0)
    cuts = cuts[:3] + [cuts[4] - cuts[3] + cuts[2]]
    state_proj_out = extra_own[: cuts[0]].reshape(gain_rows, state_width)
    in_gain_out = extra_own[cuts[0] : cuts[1]]
    ffn_gain_out = extra_own[cuts[1] : cuts[2]]
    conv_own = extra_own[cuts[2] : cuts[3]] + extra_own[cuts[3] :]
    conv_state_out = conv_own[: state_rows * window].reshape(state_rows, window)
    conv_state_bias_out = conv_own[state_rows * window :]
    pair_grad = pair_grad.reshape(mp_count, gain_rows, 2, seq_devices, columns)
    pair_grad = pair_grad.transpose(2, 1, 3, 0, 4).reshape(2, gain_rows, -1)
    shared_gate_grad, shared_up_grad = pair_grad[0], pair_grad[1]
    if paired:
        early_sums = sum(part_counts[:2])
        expert_moved[:early_sums] = after(expert_moved[:early_sums], last_sums[2:3])
        both_part = after(both_proj_grad, local_extra)
        both_moved = seq_moved(both_part)
        expert_moved[early_sums:], out_proj_moved, both_moved = after(
            (expert_moved[early_sums:], out_proj_moved, both_moved), tokens_grad
        )
        both_proj_grad = wide(both_part) + wide(both_moved)
        out_proj_grad = wide(out_proj_part) + wide(out_proj_moved)
        expert_sums = [wide(part) + wide(other) for part, other in zip(expert_parts, expert_moved)]
    else:
        both_proj_grad = seq_sum(both_proj_grad)
        out_proj_grad = seq_sum(out_proj_grad)
        expert_sums = [seq_sum(part) for part in expert_parts]
    gate_proj_grad, value_proj_grad = both_proj_grad[:, :inner_width], both_proj_grad[:, inner_width:]
    step_proj_grad = step_flat.reshape(step_proj_grad.shape)
    one, two = part_counts[0], part_counts[0] + part_counts[1]
    expert_down_grad = jnp.concatenate(expert_sums[:one], axis=1)[None]
    expert_gate_grad = jnp.concatenate(expert_sums[one:two])[None]
    expert_up_grad = jnp.concatenate(expert_sums[two:])[None]
    return (
        block_out,
        tokens_grad,
        in_gain_out,
        gate_proj_grad,
        value_proj_grad,
        state_proj_out,
        step_proj_grad,
        exact_out[0],
        exact_out[1],
        conv_state_out,
        conv_state_bias_out,
        exact_out[2],
        exact_out[3],
        exact_out[4],
        exact_out[5],
        out_proj_grad,
        ffn_gain_out,
        shared_gate_grad,
        shared_up_grad,
        shared_down_grad,
        expert_gate_grad,
        expert_up_grad,
        expert_down_grad,
    )


def solution(mesh):
    placed = (
        P("seq", None, None),
        P(("seq", "mp"), None, None),
        P(),
        P(("seq", "mp"), None, None),
        P(("seq", "mp"), None, None),
        P(("seq", "mp")),
        P(None, "mp"),
        P(None, "mp"),
        P(("seq", "mp"), None),
        P(None, "mp"),
        P(None, "mp"),
        P("mp"),
        P(("seq", "mp"), None),
        P(("seq", "mp")),
        P("mp"),
        P("mp"),
        P("mp"),
        P("mp"),
        P("mp", None),
        P(("seq", "mp")),
        P(("seq", "mp"), None),
        P(("seq", "mp"), None),
        P(("seq", "mp"), None),
        P("mp", None, None),
        P("mp", None, None),
        P("mp", None, None),
    )
    return jax.shard_map(
        body,
        mesh=mesh,
        in_specs=placed,
        out_specs=(
            P(("seq", "mp"), None, None),
            P(("seq", "mp"), None, None),
            P(("seq", "mp")),
            P(None, "mp"),
            P(None, "mp"),
            P(("seq", "mp"), None),
            P(None, "mp"),
            P(None, "mp"),
            P("mp"),
            P(("seq", "mp"), None),
            P(("seq", "mp")),
            P("mp"),
            P("mp"),
            P("mp"),
            P("mp"),
            P("mp", None),
            P(("seq", "mp")),
            P(("seq", "mp"), None),
            P(("seq", "mp"), None),
            P(("seq", "mp"), None),
            P("mp", None, None),
            P("mp", None, None),
            P("mp", None, None),
        ),
        check_vma=False,
    )
```

```python
import jax
import jax.numpy as jnp
from jax import lax
from jax.experimental import pallas as pl
from jax.experimental.pallas import tpu as pltpu
from jax.sharding import PartitionSpec as P

STATE = 128
INNER = 3072


epsilon = 1e-05
highest = lax.Precision.HIGHEST


def shifted(block, axis, distance):
    devices = range(lax.axis_size(axis))
    route = [(i - distance, i) for i in devices if i - distance in devices]
    return lax.ppermute(block, axis, route)


def entering_2(value, axis, join, neutral, backward):
    count, mine = (lax.axis_size(axis), lax.axis_index(axis))
    pieces = jax.tree.map(lambda part: lax.all_gather(part, axis), value)
    if backward:
        pieces = jax.tree.map(lambda part: part[::-1], pieces)
        mine = count - 1 - mine
    running = jax.tree.map(
        lambda part, zero: jnp.full_like(part, 0) + jnp.asarray(zero, part.dtype), value, neutral
    )

    def hop(position, running):
        longer = join(running, jax.tree.map(lambda part: part[position], pieces))
        return jax.tree.map(lambda new, old: jnp.where(position < mine, new, old), longer, running)

    return lax.fori_loop(0, count - 1, hop, running)


def rms_scale(values, gain):
    return values * lax.rsqrt(jnp.mean(values * values, axis=-1, keepdims=True) + epsilon) * gain


def silu_slope(values):
    sigmoid_val = jax.nn.sigmoid(values)
    return sigmoid_val * (1.0 + values * (1.0 - sigmoid_val))


def chain_combine(earlier, latter):
    return (earlier[0] * latter[0], latter[0][..., None, None] * earlier[1] + latter[1])


def bits(value):
    return value.astype(jnp.bfloat16)


def wide(value):
    return value.astype(jnp.float32)


def rounded(value):
    return lax.reduce_precision(value, 8, 7)


def mp_permute(value, target):
    count = lax.axis_size("mp")
    return lax.ppermute(value, "mp", [(i, target(i)) for i in range(count)])


def across_core(value):
    return mp_permute(value, lambda i: i ^ 1)


def across_pair(value):
    return mp_permute(value, lambda i: i ^ 2)


def ring_step(value, distance=1):
    count = lax.axis_size("mp")
    return mp_permute(value, lambda i: (i + 4 * distance) % count)


def coordinates():
    mine = lax.axis_index("mp")
    return mine // 4, (mine // 2) % 2, mine % 2


def pick(value, index, axis=0):
    return lax.dynamic_index_in_dim(value, index, axis, keepdims=False)


def relative_owner():
    ring = lax.axis_size("mp") // 4
    deep, pair, core = coordinates()
    cores = jnp.arange(2)[:, None, None]
    steps = jnp.array(distances())[None, :, None]
    pairs = jnp.arange(2)[None, None, :]
    return ((deep - steps) % ring) * 4 + (pair ^ pairs) * 2 + (core ^ cores)


def gather_small(block):
    count = lax.axis_size("mp")
    every = jnp.stack([block] + [ring_step(block, step) for step in distances()[1:]])
    every = jnp.stack([every, across_pair(every)], axis=1)
    every = jnp.stack([every, across_core(every)])
    order = relative_owner().reshape(-1)
    place = jnp.zeros((count,), jnp.int32).at[order].set(jnp.arange(count, dtype=jnp.int32))
    return every.reshape((count,) + block.shape)[place]


def seq_gather(value):
    if lax.axis_size("seq") != 2:
        return lax.all_gather(value, "seq")
    other = lax.ppermute(value, "seq", [(0, 1), (1, 0)])
    first = lax.axis_index("seq") == 0
    return jnp.stack([jnp.where(first, value, other), jnp.where(first, other, value)])


def seq_scatter(value):
    if lax.axis_size("seq") != 2:
        return lax.psum_scatter(wide(value), "seq", scatter_dimension=0, tiled=False)
    mine = lax.axis_index("seq")
    other = lax.ppermute(bits(pick(value, 1 - mine)), "seq", [(0, 1), (1, 0)])
    return wide(pick(value, mine)) + wide(other)


def seq_sum(value):
    if lax.axis_size("seq") != 2:
        return lax.psum(wide(value), "seq")
    low = bits(value)
    return wide(low) + wide(lax.ppermute(low, "seq", [(0, 1), (1, 0)]))


def seq_entering(decay, state, backward):
    if lax.axis_size("seq") == 2:
        route = [(1, 0)] if backward else [(0, 1)]
        return lax.ppermute(state, "seq", route)
    return entering_2(
        (decay, state),
        "seq",
        chain_combine,
        (jnp.ones_like(decay), jnp.zeros_like(state)),
        backward,
    )[1]


def mp_exchange(value):
    return lax.all_to_all(value, "mp", split_axis=0, concat_axis=0, tiled=True)


EDGE = 16
TRANSPOSED = (((1,), (1,)), ((), ()))
ROWS_SUMMED = (((0,), (0,)), ((), ()))
PLAIN = (((1,), (0,)), ((), ()))


def product(left, right, dims=PLAIN):
    return lax.dot_general(left, right, dims, preferred_element_type=jnp.float32)


def halves_of(value):
    high = value.astype(jnp.bfloat16)
    return high, (value - high.astype(jnp.float32)).astype(jnp.bfloat16)


def fine(left, right, dims=PLAIN):
    left_high, left_low = halves_of(left)
    right_high, right_low = halves_of(right)
    small = product(left_high, right_low, dims) + product(left_low, right_high, dims)
    return product(left_high, right_high, dims) + small


def exact_right(left, right, dims=PLAIN):
    high, low = halves_of(left)
    return product(high, right, dims) + product(low, right, dims)


def exact_left(left, right, dims=PLAIN):
    high = right.astype(jnp.bfloat16)
    rest = right - high.astype(jnp.float32)
    middle = rest.astype(jnp.bfloat16)
    last = (rest - middle.astype(jnp.float32)).astype(jnp.bfloat16)
    return product(left, high, dims) + (product(left, middle, dims) + product(left, last, dims))


def softplus(value):
    return jnp.maximum(value, 0.0) + jnp.log1p(jnp.exp(-jnp.abs(value)))


def spread(value, heads, width):
    channel = width // heads
    lane = lax.broadcasted_iota(jnp.int32, (value.shape[0], width), 1)
    result = jnp.broadcast_to(value[:, heads - 1 : heads], (value.shape[0], width))
    for head in range(heads - 2, -1, -1):
        result = jnp.where(lane < (head + 1) * channel, value[:, head : head + 1], result)
    return result


def only_head(value, head, heads):
    channel = value.shape[1] // heads
    lane = lax.broadcasted_iota(jnp.int32, value.shape, 1)
    inside = (lane >= head * channel) & (lane < (head + 1) * channel)
    return jnp.where(inside, value, 0.0)


def head_sum_matrix(width, heads):
    channel = width // heads
    row = lax.broadcasted_iota(jnp.int32, (width, 128), 0) // channel
    lane = lax.broadcasted_iota(jnp.int32, (width, 128), 1)
    return (row == lane).astype(jnp.float32).astype(jnp.bfloat16)


def not_before(length, reverse=False):
    row = lax.broadcasted_iota(jnp.int32, (length, length), 0)
    lane = lax.broadcasted_iota(jnp.int32, (length, length), 1)
    return (row <= lane) if reverse else (row >= lane)


def ones_of(mask):
    return mask.astype(jnp.float32).astype(jnp.bfloat16)


def whole(shape):
    return pl.BlockSpec(shape, lambda b, *_: (0,) * len(shape))


def each(shape):
    return pl.BlockSpec((1,) + shape, lambda b, *_: (b,) + (0,) * len(shape))


def f32(*shape):
    return jax.ShapeDtypeStruct(shape, jnp.float32)


def bf16(*shape):
    return jax.ShapeDtypeStruct(shape, jnp.bfloat16)


def call(kernel, grid, in_specs, out_specs, out_shape, scratch=(), prefetch=0, micros=2):
    return pl.pallas_call(
        kernel,
        grid_spec=pltpu.PrefetchScalarGridSpec(
            num_scalar_prefetch=prefetch,
            grid=grid,
            in_specs=in_specs,
            out_specs=out_specs,
            scratch_shapes=list(scratch),
        ),
        out_shape=out_shape,
        compiler_params=pltpu.CompilerParams(vmem_limit_bytes=56 * 1024 * 1024),
        cost_estimate=pl.CostEstimate(
            flops=int(micros * 9e+07), bytes_accessed=int(micros * 2.5e+05), transcendentals=0
        ),
    )


def mixer_input(
    x, edge, gain, gate_w, value_w, state_w, step_w, value_taps, state_taps,
    value_bias, state_bias, step_shift, decay_rate, heads,
):
    count, length, model = x.shape
    inner, double = value_w.shape[0], state_w.shape[1]
    window = value_taps.shape[0]

    def kernel(
        x_ref, edge_ref, gain_ref, gate_ref, value_ref, state_ref, step_ref, vt_ref, st_ref,
        vb_ref, sb_ref, shift_ref, rate_ref,
        normed_out, gate_out, ev_out, es_out, pv_out, ps_out, step_out, decay_out, local_out,
    ):
        def norm(value):
            value = value.astype(jnp.float32)
            scale = lax.rsqrt(jnp.mean(value * value, axis=-1, keepdims=True) + epsilon)
            return (value * scale * gain_ref[...]).astype(jnp.bfloat16)

        normed = norm(x_ref[0])
        normed_out[0] = normed
        ev_out[0, EDGE:] = product(normed, value_ref[...], TRANSPOSED)
        es_out[0, EDGE:] = product(normed, state_ref[...])
        step_raw = product(normed, step_ref[...])
        step_out[0] = step_raw
        gate_out[0] = product(normed, gate_ref[...], TRANSPOSED)
        edge_normed = norm(edge_ref[0])
        ev_out[0, :EDGE] = product(edge_normed, value_ref[...], TRANSPOSED)
        es_out[0, :EDGE] = product(edge_normed, state_ref[...])
        first = EDGE - window + 1
        pre_value = jnp.broadcast_to(vb_ref[...], (length, inner))
        pre_state = jnp.broadcast_to(sb_ref[...], (length, double))
        for tap in range(window):
            pre_value = pre_value + vt_ref[tap : tap + 1] * ev_out[0, first + tap : first + tap + length]
            pre_state = pre_state + st_ref[tap : tap + 1] * es_out[0, first + tap : first + tap + length]
        pv_out[0] = pre_value
        ps_out[0] = pre_state
        values = jax.nn.silu(pre_value)
        b_matrix = jax.nn.silu(pre_state[:, : double // 2])
        step = softplus(step_raw + shift_ref[...])
        decay = exact_left(ones_of(not_before(length)), -jnp.exp(rate_ref[...]) * step)
        decay_out[0] = decay
        tail = jnp.exp(decay[length - 1 : length] - decay) * step
        local_out[0] = fine(values * spread(tail, heads, inner), b_matrix, ROWS_SUMMED)

    return call(
        kernel,
        (count,),
        [
            each((length, model)), each((EDGE, model)), whole(gain.shape), whole(gate_w.shape),
            whole(value_w.shape), whole(state_w.shape), whole(step_w.shape), whole(value_taps.shape),
            whole(state_taps.shape), whole(value_bias.shape), whole(state_bias.shape),
            whole(step_shift.shape), whole(decay_rate.shape),
        ],
        [
            each((length, model)), each((length, inner)), each((length + EDGE, inner)),
            each((length + EDGE, double)), each((length, inner)), each((length, double)),
            each((length, 128)), each((length, 128)), each((inner, double // 2)),
        ],
        [
            bf16(count, length, model), f32(count, length, inner), f32(count, length + EDGE, inner),
            f32(count, length + EDGE, double), f32(count, length, inner), f32(count, length, double),
            f32(count, length, 128), f32(count, length, 128), f32(count, inner, double // 2),
        ],
        micros=11,
    )(
        x, edge, gain, gate_w, value_w, state_w, step_w, value_taps, state_taps,
        value_bias, state_bias, step_shift, decay_rate,
    )


def decay_masks(decay, heads):
    length = decay.shape[0]
    causal = not_before(length)
    turned = decay.T
    return [
        jnp.exp(jnp.where(causal, decay[:, head : head + 1] - turned[head : head + 1], -1e30))
        for head in range(heads)
    ]


def mixer_within(pre_value, pre_state, step_raw, decay_sum, step_shift, skip, heads):
    count, length, inner = pre_value.shape
    double = pre_state.shape[2]

    def kernel(pv_ref, ps_ref, step_ref, decay_ref, shift_ref, skip_ref, within_out):
        values = jax.nn.silu(pv_ref[0])
        both = jax.nn.silu(ps_ref[0])
        b_matrix, c_matrix = both[:, : double // 2], both[:, double // 2 :]
        scaled = values * spread(softplus(step_ref[0] + shift_ref[...]), heads, inner)
        crossed = fine(c_matrix, b_matrix, TRANSPOSED)
        result = spread(skip_ref[...], heads, inner) * values
        for head, mask in enumerate(decay_masks(decay_ref[0], heads)):
            result = result + fine(crossed * mask, only_head(scaled, head, heads))
        within_out[0] = result

    return call(
        kernel,
        (count,),
        [
            each((length, inner)), each((length, double)), each((length, 128)), each((length, 128)),
            whole(step_shift.shape), whole(skip.shape),
        ],
        each((length, inner)),
        f32(count, length, inner),
        micros=6,
    )(pre_value, pre_state, step_raw, decay_sum, step_shift, skip)


def mixer_output(order, within, pre_state, decay_sum, entering, gate_raw, gain, out_w, heads, owners):
    count, length, inner = within.shape
    double, model = pre_state.shape[2], out_w.shape[1]
    rows = length // owners
    half = owners // 2

    def kernel(
        order_ref, within_ref, ps_ref, decay_ref, state_ref, gate_ref, gain_ref, out_ref,
        ssm_out, scaled_out, *outs,
    ):
        part_outs, mixed = outs[:-1], outs[-1]
        c_matrix = jax.nn.silu(ps_ref[0, :, double // 2 :])
        carried = fine(c_matrix, state_ref[0], TRANSPOSED)
        ssm = within_ref[0] + spread(jnp.exp(decay_ref[0]), heads, inner) * carried
        ssm_out[0] = ssm
        gated = ssm * jax.nn.silu(gate_ref[0])
        scaled = (gated * gain_ref[...]).astype(jnp.bfloat16)
        scaled_out[0] = scaled
        squares = jnp.sum(gated * gated, axis=-1, keepdims=True)
        mixed[:, :model] = product(scaled, out_ref[...]).astype(jnp.bfloat16)
        tail = jnp.zeros((length, 128), jnp.float32)
        mixed[:, model:] = two_parts(squares, tail).astype(jnp.bfloat16)
        for place in range(owners):
            start = pl.multiple_of(order_ref[place] * rows, rows)
            part_outs[place // half][place % half // 2, place % 2] = mixed[pl.ds(start, rows)]

    blocks = pl.BlockSpec((half // 2, 2, rows, model + 128), lambda b, *_: (0, 0, b, 0))
    return call(
        kernel,
        (count,),
        [
            each((length, inner)), each((length, double)), each((length, 128)),
            each((inner, double // 2)), each((length, inner)), whole(gain.shape), whole(out_w.shape),
        ],
        [each((length, inner)), each((length, inner))] + [blocks] * 2,
        [f32(count, length, inner), bf16(count, length, inner)]
        + [bf16(half // 2, 2, count * rows, model + 128)] * 2,
        [pltpu.VMEM((length, model + 128), jnp.bfloat16)],
        1,
        micros=7,
    )(order, within, pre_state, decay_sum, entering, gate_raw, gain, out_w)


def mixer_output_back(order, blocks, gate_raw, ssm, pre_state, decay_sum, gain, out_w, heads):
    count, length, inner = ssm.shape
    double, model = pre_state.shape[2], out_w.shape[1]
    owners, wide_model = len(blocks), blocks[0].shape[1]
    rows = length // owners

    def kernel(order_ref, *refs):
        blocks_ref = refs[:owners]
        gate_ref, ssm_ref, ps_ref, decay_ref, gain_ref, out_ref = refs[owners : owners + 6]
        mix_out, ssm_grad_out, gate_grad_out, state_out, gain_out, sums = refs[owners + 6 :]
        for place in range(owners):
            start = pl.multiple_of(order_ref[place] * rows, rows)
            mix_out[0, pl.ds(start, rows)] = blocks_ref[place][:, :model]
            sums[pl.ds(start, rows)] = blocks_ref[place][:, model:].astype(jnp.float32)
        sum_grad = sums[:, 0:1] + sums[:, 1:2]
        scaled_grad = product(mix_out[0], out_ref[...], TRANSPOSED)
        gate, value = gate_ref[0], ssm_ref[0]
        opened = jax.nn.silu(gate)
        gated = value * opened

        @pl.when(pl.program_id(0) == 0)
        def _():
            gain_out[...] = jnp.zeros_like(gain_out)

        gain_out[...] += jnp.sum(scaled_grad * gated, axis=0, keepdims=True)
        gated_grad = scaled_grad * gain_ref[...] + 2.0 * gated * sum_grad
        ssm_grad = gated_grad * opened
        ssm_grad_out[0] = ssm_grad
        gate_grad_out[0] = (gated_grad * value * silu_slope(gate)).astype(jnp.bfloat16)
        c_matrix = jax.nn.silu(ps_ref[0, :, double // 2 :])
        carried_grad = spread(jnp.exp(decay_ref[0]), heads, inner) * ssm_grad
        state_out[0] = fine(carried_grad, c_matrix, ROWS_SUMMED)

    return call(
        kernel,
        (count,),
        [pl.BlockSpec((rows, wide_model), lambda b, *_: (b, 0))] * owners
        + [
            each((length, inner)), each((length, inner)), each((length, double)), each((length, 128)),
            whole(gain.shape), whole(out_w.shape),
        ],
        [
            each((length, model)), each((length, inner)), each((length, inner)),
            each((inner, double // 2)), whole((8, inner)),
        ],
        [
            bf16(count, length, model), f32(count, length, inner), bf16(count, length, inner),
            f32(count, inner, double // 2), f32(8, inner),
        ],
        [pltpu.VMEM((length, wide_model - model), jnp.float32)],
        1,
        micros=8,
    )(order, *blocks, gate_raw, ssm, pre_state, decay_sum, gain, out_w)


def mixer_within_back(pre_value, pre_state, step_raw, decay_sum, step_shift, ssm_grad, entering, heads):
    count, length, inner = pre_value.shape
    double = pre_state.shape[2]

    def kernel(pv_ref, ps_ref, step_ref, decay_ref, shift_ref, grad_ref, state_ref, scaled_out, both_out):
        values = jax.nn.silu(pv_ref[0])
        both = jax.nn.silu(ps_ref[0])
        b_matrix, c_matrix = both[:, : double // 2], both[:, double // 2 :]
        scaled = values * spread(softplus(step_ref[0] + shift_ref[...]), heads, inner)
        crossed = fine(c_matrix, b_matrix, TRANSPOSED)
        grad = grad_ref[0]
        decay = decay_ref[0]
        scaled_grad = jnp.zeros((length, inner), jnp.float32)
        crossed_grad = jnp.zeros((length, length), jnp.float32)
        for head, mask in enumerate(decay_masks(decay, heads)):
            head_grad = only_head(grad, head, heads)
            scaled_grad = scaled_grad + fine(crossed * mask, head_grad, ROWS_SUMMED)
            crossed_grad = crossed_grad + fine(head_grad, scaled, TRANSPOSED) * mask
        scaled_out[0] = scaled_grad
        both_out[0, :, : double // 2] = fine(crossed_grad, c_matrix, ROWS_SUMMED)
        carried_grad = spread(jnp.exp(decay), heads, inner) * grad
        both_out[0, :, double // 2 :] = fine(crossed_grad, b_matrix) + fine(carried_grad, state_ref[0])

    return call(
        kernel,
        (count,),
        [
            each((length, inner)), each((length, double)), each((length, 128)), each((length, 128)),
            whole(step_shift.shape), each((length, inner)), each((inner, double // 2)),
        ],
        [each((length, inner)), each((length, double))],
        [f32(count, length, inner), f32(count, length, double)],
        micros=9,
    )(pre_value, pre_state, step_raw, decay_sum, step_shift, ssm_grad, entering)


def mixer_input_back(
    pre_value, pre_state, ext_value, ext_state, step_raw, decay_sum, ssm, ssm_grad, scaled_grad,
    state_part, entering, exit_grad, value_taps, state_taps, step_shift, decay_rate, skip, heads,
):
    count, length, inner = pre_value.shape
    double = pre_state.shape[2]
    window = value_taps.shape[0]

    def kernel(
        pv_ref, ps_ref, ev_ref, es_ref, step_ref, decay_ref, ssm_ref, grad_ref, scaled_ref, part_ref,
        state_ref, exit_ref, vt_ref, st_ref, shift_ref, rate_ref, skip_ref,
        value_out, state_out, edge_v_out, edge_s_out, step_out, taps_v_out, taps_s_out, head_out,
        room_v, room_s,
    ):
        pre_v, pre_s = pv_ref[0], ps_ref[0]
        values = jax.nn.silu(pre_v)
        b_matrix = jax.nn.silu(pre_s[:, : double // 2])
        grad, scaled = grad_ref[0], scaled_ref[0]
        step_pre = step_ref[0] + shift_ref[...]
        step = softplus(step_pre)
        rate = jnp.exp(rate_ref[...])
        decay = decay_ref[0]
        last = decay[length - 1 : length]
        remain = jnp.exp(last - decay)
        remain_wide = spread(remain, heads, inner)
        step_wide = spread(step, heads, inner)
        tail_wide = remain_wide * step_wide
        skip_wide = spread(skip_ref[...], heads, inner)
        leaving = exit_ref[0]
        passed = fine(b_matrix, leaving, TRANSPOSED)
        value_grad = scaled * step_wide + tail_wide * passed + skip_wide * grad
        b_grad = part_ref[0, :, : double // 2] + fine(tail_wide * values, leaving)
        summing = head_sum_matrix(inner, heads)
        crossing = values * passed
        left_part = exact_right(crossing * tail_wide, summing)
        decay_grad = (
            exact_right(grad * (ssm_ref[0] - skip_wide * values) - values * step_wide * scaled, summing)
            - left_part
        )
        total_grad = jnp.sum(left_part, axis=0, keepdims=True)
        state_dot = exact_left(jnp.ones((8, double // 2), jnp.bfloat16), leaving * state_ref[0], TRANSPOSED)
        total_grad = total_grad + jnp.exp(last) * exact_right(state_dot, summing)[:1]
        row = lax.broadcasted_iota(jnp.int32, decay_grad.shape, 0)
        decay_grad = decay_grad + jnp.where(row == length - 1, total_grad, 0.0)
        log_grad = exact_left(ones_of(not_before(length, True)), decay_grad)
        step_size_grad = exact_right(scaled * values + crossing * remain_wide, summing) - rate * log_grad
        step_raw_grad = step_size_grad * jax.nn.sigmoid(step_pre)
        step_out[0] = step_raw_grad.astype(jnp.bfloat16)
        skip_grad = exact_right(grad * values, summing)

        @pl.when(pl.program_id(0) == 0)
        def _():
            taps_v_out[...] = jnp.zeros_like(taps_v_out)
            taps_s_out[...] = jnp.zeros_like(taps_s_out)
            head_out[...] = jnp.zeros_like(head_out)
            for room in (room_v, room_s):
                room[:EDGE] = jnp.zeros((EDGE, room.shape[1]), jnp.float32)
                room[EDGE + length :] = jnp.zeros((EDGE, room.shape[1]), jnp.float32)

        head_out[0:1] += jnp.sum(step_raw_grad, axis=0, keepdims=True)
        head_out[1:2] += jnp.sum(-rate * step * log_grad, axis=0, keepdims=True)
        head_out[2:3] += jnp.sum(skip_grad, axis=0, keepdims=True)
        room_v[EDGE : EDGE + length] = value_grad * silu_slope(pre_v)
        room_s[EDGE : EDGE + length, : double // 2] = b_grad * silu_slope(pre_s[:, : double // 2])
        room_s[EDGE : EDGE + length, double // 2 :] = part_ref[0, :, double // 2 :] * silu_slope(
            pre_s[:, double // 2 :]
        )
        first = EDGE - window + 1
        for room, ext, taps, taps_out, out, edge_out in (
            (room_v, ev_ref, vt_ref, taps_v_out, value_out, edge_v_out),
            (room_s, es_ref, st_ref, taps_s_out, state_out, edge_s_out),
        ):
            pre_grad = room[EDGE : EDGE + length]
            taps_out[window : window + 1] += jnp.sum(pre_grad, axis=0, keepdims=True)
            inside = jnp.zeros(pre_grad.shape, jnp.float32)
            before = jnp.zeros((EDGE, pre_grad.shape[1]), jnp.float32)
            for tap in range(window):
                moved = ext[0, first + tap : first + tap + length]
                taps_out[tap : tap + 1] += jnp.sum(pre_grad * moved, axis=0, keepdims=True)
                ahead = window - 1 - tap
                weight = taps[tap : tap + 1]
                inside = inside + weight * room[EDGE + ahead : EDGE + ahead + length]
                before = before + weight * room[ahead : ahead + EDGE]
            out[0] = inside
            edge_out[0] = before

    return call(
        kernel,
        (count,),
        [
            each((length, inner)), each((length, double)), each((length + EDGE, inner)),
            each((length + EDGE, double)), each((length, 128)), each((length, 128)),
            each((length, inner)), each((length, inner)), each((length, inner)), each((length, double)),
            each((inner, double // 2)), each((inner, double // 2)), whole(value_taps.shape),
            whole(state_taps.shape), whole(step_shift.shape), whole(decay_rate.shape), whole(skip.shape),
        ],
        [
            each((length, inner)), each((length, double)), each((EDGE, inner)), each((EDGE, double)),
            each((length, 128)), whole((8, inner)), whole((8, double)), whole((8, 128)),
        ],
        [
            f32(count, length, inner), f32(count, length, double), f32(count, EDGE, inner),
            f32(count, EDGE, double), bf16(count, length, 128), f32(8, inner), f32(8, double), f32(8, 128),
        ],
        [
            pltpu.VMEM((length + 2 * EDGE, inner), jnp.float32),
            pltpu.VMEM((length + 2 * EDGE, double), jnp.float32),
        ],
        micros=13,
    )(
        pre_value, pre_state, ext_value, ext_state, step_raw, decay_sum, ssm, ssm_grad, scaled_grad,
        state_part, entering, exit_grad, value_taps, state_taps, step_shift, decay_rate, skip,
    )


def mixer_project_back(
    order, value_local, state_local, edge_value, edge_state, gate_grad, step_grad, x,
    gate_w, value_w, state_w, step_w, owners,
):
    count, length, inner = value_local.shape
    double, model = state_local.shape[2], x.shape[2]
    rows = length // owners
    half = owners // 2

    def kernel(
        order_ref, value_ref, state_ref, ev_ref, es_ref, gate_grad_ref, step_grad_ref, x_ref,
        gate_ref, vw_ref, sw_ref, step_ref,
        value_out, state_out, gain_out, *outs,
    ):
        part_outs, mixed = outs[:-1], outs[-1]
        body_rows = length - EDGE
        for part, edge, out in ((value_ref, ev_ref, value_out), (state_ref, es_ref, state_out)):
            out[0, :body_rows] = part[0, :body_rows].astype(jnp.bfloat16)
            out[0, body_rows:] = (part[0, body_rows:] + edge[0]).astype(jnp.bfloat16)
        grad = product(gate_grad_ref[0], gate_ref[...])
        grad = grad + product(value_out[0], vw_ref[...])
        grad = grad + product(state_out[0], sw_ref[...], TRANSPOSED)
        grad = grad + product(step_grad_ref[0], step_ref[...], TRANSPOSED)
        value = x_ref[0].astype(jnp.float32)
        scale = lax.rsqrt(jnp.mean(value * value, axis=-1, keepdims=True) + epsilon)

        @pl.when(pl.program_id(0) == 0)
        def _():
            gain_out[...] = jnp.zeros_like(gain_out)

        gain_out[...] += jnp.sum(grad * value * scale, axis=0, keepdims=True)
        mixed[...] = grad.astype(jnp.bfloat16)
        for place in range(owners):
            start = pl.multiple_of(order_ref[place] * rows, rows)
            part_outs[place // half][place % half // 2, place % 2] = mixed[pl.ds(start, rows)]

    blocks = pl.BlockSpec((half // 2, 2, rows, model), lambda b, *_: (0, 0, b, 0))
    return call(
        kernel,
        (count,),
        [
            each((length, inner)), each((length, double)), each((EDGE, inner)), each((EDGE, double)),
            each((length, inner)), each((length, 128)), each((length, model)), whole(gate_w.shape),
            whole(value_w.shape), whole(state_w.shape), whole(step_w.shape),
        ],
        [each((length, inner)), each((length, double)), whole((8, model))] + [blocks] * 2,
        [bf16(count, length, inner), bf16(count, length, double), f32(8, model)]
        + [bf16(half // 2, 2, count * rows, model)] * 2,
        [pltpu.VMEM((length, model), jnp.bfloat16)],
        1,
        micros=10,
    )(
        order, value_local, state_local, edge_value, edge_state, gate_grad, step_grad, x,
        gate_w, value_w, state_w, step_w,
    )


def total_of(refs):
    result = refs[0][...].astype(jnp.float32)
    for ref in refs[1:]:
        result = result + ref[...].astype(jnp.float32)
    return result


def two_parts(value, like):
    lane = lax.broadcasted_iota(jnp.int32, like.shape, len(like.shape) - 1)
    high = value.astype(jnp.bfloat16).astype(jnp.float32)
    return jnp.where(lane == 0, high, jnp.where(lane == 1, value - high, 0.0))


def store_sum(total, tail, out_refs):
    model = total.shape[-1] - tail
    for place, out in enumerate(out_refs):
        part = total[place] if len(out_refs) > 1 else total
        out[:, :model] = part[:, :model].astype(jnp.bfloat16)
        if tail:
            column = part[:, model : model + 1] + part[:, model + 1 : model + 2]
            out[:, model:] = two_parts(column, part[:, model:]).astype(jnp.bfloat16)


def add_pairs(left, right, tail):
    steps, _, rows, width = left.shape

    def kernel(left_ref, right_ref, *out_refs):
        for step in range(steps):
            total = left_ref[step].astype(jnp.float32) + right_ref[step].astype(jnp.float32)
            store_sum(total, tail, out_refs[2 * step : 2 * step + 2])

    sums = call(
        kernel,
        (1,),
        [whole(left.shape)] * 2,
        [whole((rows, width))] * (2 * steps),
        [bf16(rows, width)] * (2 * steps),
        micros=3,
    )(left, right)
    return list(sums[0::2]), list(sums[1::2])


def add_blocks(left, right, tail):
    def kernel(left_ref, right_ref, out_ref):
        store_sum(total_of((left_ref, right_ref)), tail, [out_ref])

    return call(
        kernel, (1,), [whole(left.shape)] * 2, whole(left.shape), bf16(*left.shape)
    )(left, right)


def after(value, *others):
    return lax.optimization_barrier((value, others))[0]


def distances():
    ring = lax.axis_size("mp") // 4
    return sorted(range(ring), key=lambda step: min(step, ring - step))


def gather_blocks(block, early=None, ties=()):
    ring = lax.axis_size("mp") // 4
    own, partner, result = [], [], None
    arrived = [block] + [ring_step(block, step) for step in distances()[1:]]
    for step, tie in enumerate(ties):
        arrived[step] = after(arrived[step], tie)
    for step, held in enumerate(arrived):
        both = [held, across_pair(held)]
        if early is not None and step == ring // 2:
            result = early(own + partner)
        if early is not None and step == ring - 1:
            partner += [across_core(value) for value in after(both, result[-1])]
        else:
            partner += [across_core(value) for value in both]
        own += both
    return own + partner, result


def scatter_core(own, partner, tail=0):
    return add_pairs(own, across_core(partner), tail)


def scatter_deep(kept, sent, tail=0):
    ring = len(kept)
    received = [across_pair(block) for block in sent]
    moving = [add_blocks(kept[step], received[step], tail) for step in range(1, ring)]
    result = [kept[0], received[0]]
    for step in range(1, ring):
        result.append(ring_step(moving[step - 1], ring - distances()[step]))
    return result, moving


def hidden_rows(parts, own_inputs, gain):
    rows, model = own_inputs.shape

    def kernel(*refs):
        part_refs, (x_ref, gain_ref, hidden_out, mix_out, inv_out, low_out) = refs[:-6], refs[-6:]
        total = total_of(part_refs)
        mixed = total[:, :model]
        squares = total[:, model : model + 1] + total[:, model + 1 : model + 2]
        inv_norm = lax.rsqrt(squares / INNER + epsilon)
        hidden = x_ref[...].astype(jnp.float32) + mixed * inv_norm
        hidden_out[...] = hidden
        mix_out[...] = mixed
        inv_out[...] = jnp.broadcast_to(inv_norm, inv_out.shape)
        low_out[...] = rms_scale(hidden, gain_ref[...]).astype(jnp.bfloat16)

    return call(
        kernel,
        (1,),
        [whole(part.shape) for part in parts] + [whole(own_inputs.shape), whole(gain.shape)],
        [whole((rows, model)), whole((rows, model)), whole((rows, 128)), whole((rows, model))],
        [f32(rows, model), f32(rows, model), f32(rows, 128), bf16(rows, model)],
    )(*parts, own_inputs, gain)


def output_rows(parts, hidden, target, valid):
    rows, model = hidden.shape

    def kernel(*refs):
        part_refs, (hidden_ref, target_ref, valid_ref, block_out, grad_out, low_out) = refs[:-6], refs[-6:]
        output = hidden_ref[...] + total_of(part_refs)
        block_out[...] = output.astype(jnp.bfloat16)
        grad = (output - target_ref[...].astype(jnp.float32)) * valid_ref[...]
        grad_out[...] = grad
        low_out[...] = grad.astype(jnp.bfloat16)

    return call(
        kernel,
        (1,),
        [whole(part.shape) for part in parts]
        + [whole(hidden.shape), whole(target.shape), whole(valid.shape)],
        [whole((rows, model))] * 3,
        [bf16(rows, model), f32(rows, model), bf16(rows, model)],
    )(*parts, hidden, target, valid)


def hidden_rows_back(parts, grad_out, hidden, mixed, inv_norm, gain):
    rows, model = hidden.shape

    def kernel(*refs):
        part_refs = refs[:-8]
        grad_ref, hidden_ref, mix_ref, inv_ref, gain_ref, hidden_out, send_out, gain_out = refs[-8:]
        input_grad = total_of(part_refs)
        value = hidden_ref[...]
        scale = lax.rsqrt(jnp.mean(value * value, axis=-1, keepdims=True) + epsilon)
        gained = input_grad * gain_ref[...]
        dot_sum = jnp.sum(gained * value, axis=-1, keepdims=True)
        grad = grad_ref[...] + scale * gained - value * (scale * scale * scale * dot_sum / model)
        hidden_out[...] = grad
        gain_out[...] = jnp.broadcast_to(
            jnp.sum(input_grad * value * scale, axis=0, keepdims=True), gain_out.shape
        )
        inv = inv_ref[:, 0:1]
        send_out[:, :model] = (grad * inv).astype(jnp.bfloat16)
        sum_grad = jnp.sum(grad * mix_ref[...], axis=-1, keepdims=True) * (-0.5 / INNER) * inv * inv * inv
        send_out[:, model:] = two_parts(sum_grad, inv_ref[...]).astype(jnp.bfloat16)

    return call(
        kernel,
        (1,),
        [whole(part.shape) for part in parts]
        + [whole(grad_out.shape), whole(hidden.shape), whole(mixed.shape), whole(inv_norm.shape), whole(gain.shape)],
        [whole((rows, model)), whole((rows, model + 128)), whole((8, model))],
        [f32(rows, model), bf16(rows, model + 128), f32(8, model)],
    )(*parts, grad_out, hidden, mixed, inv_norm, gain)


def token_rows_back(parts, hidden_grad, own_inputs, gain):
    rows, model = hidden_grad.shape

    def kernel(*refs):
        part_refs, (grad_ref, x_ref, gain_ref, out) = refs[:-4], refs[-4:]
        normed_grad = total_of(part_refs)
        value = x_ref[...].astype(jnp.float32)
        scale = lax.rsqrt(jnp.mean(value * value, axis=-1, keepdims=True) + epsilon)
        gained = normed_grad * gain_ref[...]
        dot_sum = jnp.sum(gained * value, axis=-1, keepdims=True)
        out[...] = grad_ref[...] + scale * gained - value * (scale * scale * scale * dot_sum / model)

    return call(
        kernel,
        (1,),
        [whole(part.shape) for part in parts]
        + [whole(hidden_grad.shape), whole(own_inputs.shape), whole(gain.shape)],
        whole((rows, model)),
        f32(rows, model),
    )(*parts, hidden_grad, own_inputs, gain)


def store_parts(value, out_refs):
    for place, out in enumerate(out_refs):
        size = value.shape[0] // len(out_refs)
        out[...] = value[place * size : (place + 1) * size].reshape(out.shape).astype(jnp.bfloat16)


def experts_forward(blocks, share, gate_w, up_w, down_w, pair_w, pair_down):
    rows, model = blocks[0].shape
    count, hidden = len(blocks), gate_w.shape[1]
    total, double = rows * count, pair_w.shape[1]

    def kernel(*refs):
        block_refs = refs[:count]
        share_ref, gate_ref, up_ref, down_ref, pair_ref, pd_ref = refs[count : count + 6]
        rows_out, gate_out, up_out, both_out, act_out, shared_out = refs[count + 6 : count + 12]
        part_refs = refs[count + 12 :]
        for place, block in enumerate(block_refs):
            rows_out[place * rows : (place + 1) * rows] = block[...]
        value = rows_out[...]
        gate = product(value, gate_ref[...])
        up = product(value, up_ref[...])
        gate_out[...] = gate
        up_out[...] = up
        act = (jax.nn.silu(gate) * up).astype(jnp.bfloat16)
        act_out[...] = act
        both = product(value, pair_ref[...])
        both_out[...] = both
        lane = lax.broadcasted_iota(jnp.int32, both.shape, 1)
        shared = jax.nn.silu(both) * pltpu.roll(both, double // 2, 1)
        shared = jnp.where(lane < double // 2, shared, 0.0).astype(jnp.bfloat16)
        shared_out[...] = shared
        result = product(act, down_ref[...]).astype(jnp.bfloat16).astype(jnp.float32)
        store_parts(share_ref[...] * result + product(shared, pd_ref[...]), part_refs)

    parts, steps = 2, count // 4
    return call(
        kernel,
        (1,),
        [whole(block.shape) for block in blocks]
        + [whole(w.shape) for w in (share, gate_w, up_w, down_w, pair_w, pair_down)],
        [whole((total, model)), whole((total, hidden)), whole((total, hidden)), whole((total, double))]
        + [whole((total, hidden)), whole((total, double))]
        + [whole((steps, 2, rows, model))] * parts,
        [bf16(total, model), f32(total, hidden), f32(total, hidden), f32(total, double)]
        + [bf16(total, hidden), bf16(total, double)]
        + [bf16(steps, 2, rows, model)] * parts,
        micros=8,
    )(*blocks, share, gate_w, up_w, down_w, pair_w, pair_down)


def experts_backward(blocks, share, gate, up, both, act, before, last, gate_w, up_w, down_w, pair_w, pair_down):
    rows, model = blocks[0].shape
    count, hidden = len(blocks), gate_w.shape[1]
    total, double = rows * count, pair_w.shape[1]
    others = [share, gate, up, both, act, gate_w, up_w, down_w, pair_w, pair_down]
    others += [] if before is None else [before]

    def kernel(*refs):
        block_refs = refs[:count]
        share_ref, g_ref, u_ref, both_ref, act_ref, gate_ref, up_ref, down_ref, pair_ref, pd_ref = refs[
            count : count + 10
        ]
        before_ref = None if before is None else refs[count + 10]
        grads_out, gate_out, up_out, shared_out, *outs = refs[count + len(others) :]
        for place, block in enumerate(block_refs):
            grads_out[place * rows : (place + 1) * rows] = block[...]
        grad = grads_out[...]
        routed = (share_ref[...] * grad.astype(jnp.float32)).astype(jnp.bfloat16)
        act_grad = product(routed, down_ref[...], TRANSPOSED)
        gate = g_ref[...]
        gate_out[...] = (act_grad * u_ref[...] * silu_slope(gate)).astype(jnp.bfloat16)
        up_out[...] = (act_grad * jax.nn.silu(gate)).astype(jnp.bfloat16)
        pair_value = both_ref[...]
        turned = pltpu.roll(pair_value, double // 2, 1)
        lane = lax.broadcasted_iota(jnp.int32, pair_value.shape, 1)
        factor = jnp.where(lane < double // 2, turned * silu_slope(pair_value), jax.nn.silu(turned))
        shared_out[...] = (product(grad, pd_ref[...], TRANSPOSED) * factor).astype(jnp.bfloat16)
        result = product(gate_out[...], gate_ref[...], TRANSPOSED)
        result = result + product(up_out[...], up_ref[...], TRANSPOSED)
        store_parts(result + product(shared_out[...], pair_ref[...], TRANSPOSED), outs[:2])
        down_grad = product(act_ref[...], routed, ROWS_SUMMED)
        if before_ref is not None:
            down_grad = down_grad + before_ref[...]
        outs[2][...] = down_grad.astype(outs[2].dtype)

    steps = count // 4
    return call(
        kernel,
        (1,),
        [whole(block.shape) for block in blocks] + [whole(value.shape) for value in others],
        [whole((total, model)), whole((total, hidden)), whole((total, hidden)), whole((total, double))]
        + [whole((steps, 2, rows, model))] * 2
        + [whole((hidden, model))],
        [bf16(total, model), bf16(total, hidden), bf16(total, hidden), bf16(total, double)]
        + [bf16(steps, 2, rows, model)] * 2
        + [(bf16 if last else f32)(hidden, model)],
        micros=10,
    )(*blocks, *others)


def experts_weights(groups):
    rows, grads, shared, gate_grad, up_grad, pair_grad = groups[0]
    model, hidden, double = rows.shape[1], gate_grad.shape[1], shared.shape[1]
    width = 256 if model % 256 == 0 else model
    each_group = len(groups[0])
    steps = model // width
    runs = ((4, 2), (2, 2, 2)) if steps == 6 else ((steps,), (steps,))

    def kernel(*refs):
        *piece_outs, pair_out, pair_down_out = refs[len(groups) * each_group :]
        sums = [0.0] * 4
        for group in range(len(groups)):
            x, g, sa, gg, ug, pg = refs[group * each_group : (group + 1) * each_group]
            sums[0] = sums[0] + product(x[...], gg[...], ROWS_SUMMED)
            sums[1] = sums[1] + product(x[...], ug[...], ROWS_SUMMED)
            sums[2] = sums[2] + product(x[...], pg[...], ROWS_SUMMED)
            sums[3] = sums[3] + product(sa[...], g[...], ROWS_SUMMED)
        pair_out[...] = sums[2].astype(jnp.bfloat16)
        pair_down_out[...] = sums[3].astype(jnp.bfloat16)
        number = 0
        for kind in range(2):
            first = 0
            for run in runs[kind]:
                store_piece(piece_outs[number], sums[kind], first, run)
                number, first = number + 1, first + run

    def store_piece(out, value, first, run):
        @pl.when((pl.program_id(0) >= first) & (pl.program_id(0) < first + run))
        def _():
            out[...] = value.astype(jnp.bfloat16)

    def piece_spec(first, run):
        return pl.BlockSpec((width, hidden), lambda d: (jnp.clip(d - first, 0, run - 1), 0))

    in_specs = []
    for group in groups:
        total = group[0].shape[0]
        columns = pl.BlockSpec((total, width), lambda d: (0, d))
        in_specs += [columns, columns] + [whole(value.shape) for value in group[2:]]
    out_specs, shapes = [], []
    for kind in range(2):
        first = 0
        for run in runs[kind]:
            out_specs.append(piece_spec(first, run))
            shapes.append(bf16(width * run, hidden))
            first += run
    outs = call(
        kernel,
        (steps,),
        in_specs,
        out_specs
        + [
            pl.BlockSpec((width, double), lambda d: (d, 0)),
            pl.BlockSpec((double, width), lambda d: (0, d)),
        ],
        shapes + [bf16(model, double), bf16(double, model)],
        micros=11,
    )(*[value for group in groups for value in group])
    return outs[: len(runs[0])], outs[len(runs[0]) : -2], outs[-2], outs[-1]


def mixer_weights(normed, gate_grad, value_grad, state_grad):
    count, length, model = normed.shape
    width = 256 if model % 256 == 0 else model
    inner = gate_grad.shape[2]

    def kernel(normed_ref, gate_ref, value_ref, state_ref, both_out, state_out):
        def summed(grad):
            total = 0.0
            for place in range(count):
                total = total + product(normed_ref[place], grad[place], ROWS_SUMMED)
            return total.astype(jnp.bfloat16)

        def shift(start):
            row = lax.broadcasted_iota(jnp.int32, (inner, 2 * inner), 0)
            lane = lax.broadcasted_iota(jnp.int32, (inner, 2 * inner), 1)
            return ones_of(row + start == lane)

        both = product(summed(gate_ref), shift(0)) + product(summed(value_ref), shift(inner))
        both_out[...] = both.astype(jnp.bfloat16)
        state_out[...] = summed(state_ref)

    grads = (gate_grad, value_grad, state_grad)
    return call(
        kernel,
        (model // width,),
        [pl.BlockSpec((count, length, width), lambda d: (0, 0, d))] + [whole(grad.shape) for grad in grads],
        [
            pl.BlockSpec((width, 2 * inner), lambda d: (d, 0)),
            pl.BlockSpec((width, state_grad.shape[2]), lambda d: (d, 0)),
        ],
        [bf16(model, 2 * inner), bf16(model, state_grad.shape[2])],
        micros=8,
    )(normed, *grads)


def body(
    tokens,
    target,
    lengths,
    routes,
    route_weight,
    in_gain,
    gate_proj,
    value_proj,
    state_proj,
    step_proj,
    conv_value,
    conv_value_bias,
    conv_state,
    conv_state_bias,
    step_bias,
    decay_log,
    skip_gain,
    mixer_gain,
    out_proj,
    ffn_gain,
    shared_gate,
    shared_up,
    shared_down,
    expert_gate,
    routed_up_weights,
    expert_down,
):
    mp_count = lax.axis_size("mp")
    slot_count, seq_count, model_width = tokens.shape
    seq_devices = lax.axis_size("seq")
    shared_expert_rows = slot_count // mp_count
    inner_width = gate_proj.shape[1]
    row_count = shared_expert_rows * seq_count
    window = conv_value.shape[0]
    gain_rows = in_gain.shape[0]
    state_rows = conv_state.shape[0]
    state_width = state_proj.shape[1]
    expert_count = expert_gate.shape[0] * mp_count

    packed = jnp.concatenate(
        [
            state_proj.reshape(-1),
            in_gain,
            ffn_gain,
            conv_state.reshape(-1),
            conv_state_bias,
        ]
    )
    route_rows = route_weight.transpose(1, 0, 2).reshape(row_count, -1)
    chosen = routes.transpose(1, 0, 2).reshape(row_count, -1, 1) == jnp.arange(expert_count, dtype=jnp.int32)
    coefficient = jnp.sum(jnp.where(chosen, route_rows[..., None], 0.0), axis=1)
    coefficient_high = rounded(coefficient)
    coefficient_low = coefficient - coefficient_high
    columns = shared_gate.shape[1] // (seq_devices * mp_count)
    hidden_own = seq_devices * columns
    pair_cut = jnp.stack([shared_gate, shared_up]).reshape(2, gain_rows, seq_devices, mp_count, columns)
    pair_cut = pair_cut.transpose(3, 1, 0, 2, 4).reshape(mp_count, -1)
    head_count = step_proj.shape[1]
    lane_pad = ((0, 0), (0, 128 - head_count))
    step_weight = jnp.pad(step_proj, lane_pad)
    step_shift = jnp.pad(step_bias[None], lane_pad)
    decay_rate = jnp.pad(decay_log[None], lane_pad)
    skip_row = jnp.pad(skip_gain[None], lane_pad)
    both_packed = after(seq_gather(packed), step_weight, step_shift, decay_rate, skip_row)
    small = gather_small(
        jnp.concatenate(
            [
                both_packed.reshape(-1),
                bits(coefficient_high).reshape(-1),
                bits(coefficient_low).reshape(-1),
            ]
        )
    )
    width = packed.shape[0]
    weights_small = small[:, : seq_devices * width].reshape(mp_count, seq_devices, width)
    weights_small = jnp.moveaxis(weights_small, 1, 0).reshape(seq_devices * mp_count, width)
    cut = [gain_rows * state_width]
    for part in (gain_rows, gain_rows, conv_state.size):
        cut.append(cut[-1] + part)
    state_whole = weights_small[:, : cut[0]].reshape(-1, state_width)
    gain_first = weights_small[:, cut[0] : cut[1]].reshape(-1)
    gain_second = weights_small[:, cut[1] : cut[2]].reshape(-1)
    conv_state_whole = weights_small[:, cut[2] : cut[3]].reshape(-1, window)
    conv_bias_whole = weights_small[:, cut[3] :].reshape(-1)
    share = small[:, seq_devices * width :].reshape(mp_count, 2, row_count, expert_count)
    share = lax.dynamic_index_in_dim(share, lax.axis_index("mp"), 3, keepdims=False)
    share = wide(share[:, 0]) + wide(share[:, 1])
    ring = mp_count // 4
    order = relative_owner().reshape(-1).astype(jnp.int32)
    share = share[order].reshape(2, ring, 2 * row_count)
    ring_groups = [tuple(range(ring // 2)), tuple(range(ring // 2, ring))]
    shares = [share[:, group[0] : group[-1] + 1].reshape(-1, 1) for group in ring_groups]

    gate_weight, up_weight, down_weight = expert_gate[0], routed_up_weights[0], expert_down[0]

    head_count = step_proj.shape[1]
    start_row = lax.axis_index("mp") * shared_expert_rows
    sequences = tokens.transpose(1, 0, 2)
    own_inputs = lax.dynamic_slice_in_dim(sequences, start_row, shared_expert_rows, 1)
    own_inputs = own_inputs.reshape(row_count, model_width)
    edge_rows = shifted(tokens[slot_count - window + 1 :].transpose(1, 0, 2), "seq", 1)
    edge_rows = jnp.pad(edge_rows, ((0, 0), (EDGE - window + 1, 0), (0, 0)))
    state_taps = wide(conv_state_whole).T
    mixer = mixer_input(
        sequences,
        edge_rows,
        wide(gain_first)[None],
        gate_proj.T,
        value_proj.T,
        state_whole,
        step_weight,
        conv_value,
        state_taps,
        conv_value_bias[None],
        wide(conv_bias_whole)[None],
        step_shift,
        decay_rate,
        head_count,
    )
    normed, gate_raw, ext_value, ext_state, pre_value, pre_state, step_raw, decay_sum, local_state = mixer
    decay_total = jnp.exp(decay_sum[:, slot_count - 1, :head_count])
    state_shape = (seq_count, head_count, inner_width // head_count, STATE)

    def entering_of(state, backward):
        moved = seq_entering(decay_total, state.reshape(state_shape), backward)
        return moved.reshape(state.shape)

    entering = entering_of(local_state, False)
    within = mixer_within(pre_value, pre_state, step_raw, decay_sum, step_shift, skip_row, head_count)
    ssm, scaled_low, *mix_parts = mixer_output(
        order,
        within,
        pre_state,
        decay_sum,
        entering,
        gate_raw,
        mixer_gain[None],
        out_proj,
        head_count,
        mp_count,
    )
    first_gain, second_gain = wide(gain_first)[None], wide(gain_second)[None]
    kept, sent = scatter_core(*mix_parts, 128)
    pair_moved = mp_exchange(after(pair_cut, sent))
    pair_weight = seq_gather(pair_moved).reshape(model_width, 2 * hidden_own)
    down_shared = seq_gather(after(shared_down, sent)).reshape(hidden_own, model_width)
    pair_down = jnp.concatenate([down_shared, down_shared])
    mix_sums, _ = scatter_deep(kept, sent, 128)
    hidden, pre_mix, inv_norm, ffn_input = hidden_rows(
        after(mix_sums, pair_moved), own_inputs, second_gain
    )

    def of_group(blocks, group):
        half = 2 * ring
        picked = [2 * step + side for step in group for side in (0, 1)]
        return [blocks[core * half + place] for core in (0, 1) for place in picked]

    def of_groups(parts_of_groups):
        both = [scatter_core(*parts) for parts in parts_of_groups]
        return sum([kept for kept, _ in both], []), sum([sent for _, sent in both], [])

    expert_weights = (gate_weight, up_weight, down_weight, pair_weight, pair_down)
    row_blocks, first_forward = gather_blocks(
        ffn_input, lambda blocks: experts_forward(blocks, shares[0], *expert_weights)
    )
    forwards = [
        first_forward,
        experts_forward(of_group(row_blocks, ring_groups[1]), shares[1], *expert_weights),
    ]
    position = (
        lax.axis_index("seq") * slot_count
        + start_row
        + jnp.arange(shared_expert_rows, dtype=jnp.int32)
    )
    valid_mask = (position[None, :] < lengths[:, None]).astype(jnp.float32).reshape(row_count, 1)
    block_rows, grad_out, grad_low = output_rows(
        scatter_deep(*of_groups([result[6:] for result in forwards]))[0],
        hidden,
        target.transpose(1, 0, 2).reshape(row_count, model_width),
        valid_mask,
    )

    def slots_first(value):
        return value.reshape(seq_count, shared_expert_rows, model_width).transpose(1, 0, 2)

    block_out = slots_first(block_rows)
    grad_blocks, first_backward = gather_blocks(
        grad_low,
        lambda blocks: experts_backward(
            blocks, shares[0], *forwards[0][1:5], None, False, *expert_weights
        ),
    )
    backwards = [
        first_backward,
        experts_backward(
            of_group(grad_blocks, ring_groups[1]),
            shares[1],
            *forwards[1][1:5],
            first_backward[6],
            True,
            *expert_weights,
        ),
    ]
    def seq_moved(value):
        return lax.ppermute(value, "seq", [(0, 1), (1, 0)])

    paired = seq_devices == 2
    kept, sent = of_groups([result[4:6] for result in backwards])
    down_part = backwards[1][6]
    first_row = after(forwards[0][0], sent)
    gate_parts, up_parts, pair_grad, pair_down_grad = experts_weights(
        [
            (ahead_rows, back[0], ahead[5], back[1], back[2], back[3])
            for ahead_rows, ahead, back in zip((first_row, forwards[1][0]), forwards, backwards)
        ]
    )
    expert_parts = [down_part, *gate_parts, *up_parts]
    part_counts = [1, len(gate_parts)]
    ordered = paired and len(expert_parts) == 6
    expert_moved = [None] * len(expert_parts)
    row_sums, _ = scatter_deep(after(kept, pair_down_grad), sent)
    mix_ties = ()
    if ordered:
        expert_moved[:4] = [seq_moved(part) for part in expert_parts[:4]]
        row_sums = after(row_sums, expert_moved[0])
        mix_ties = [(), (), expert_moved[1]]
    hidden_grad, mix_grad_send, ffn_gain_grad = hidden_rows_back(
        row_sums,
        grad_out,
        hidden,
        pre_mix,
        inv_norm,
        second_gain,
    )
    mix_blocks, _ = gather_blocks(mix_grad_send, None, mix_ties)
    if ordered:
        mix_blocks = after(mix_blocks, expert_moved[2])
    mix_grad_all, ssm_grad, gate_grad, entering_grad, mixer_gain_grad = mixer_output_back(
        order,
        mix_blocks,
        gate_raw,
        ssm,
        pre_state,
        decay_sum,
        mixer_gain[None],
        out_proj,
        head_count,
    )
    exit_grad = entering_of(entering_grad, True)
    within_grad = ssm_grad
    if ordered:
        within_grad = after(ssm_grad, expert_moved[3])
    scaled_value_grad, state_part_grad = mixer_within_back(
        pre_value, pre_state, step_raw, decay_sum, step_shift, within_grad, entering, head_count
    )
    def by_rows(value):
        return value.reshape(slot_count * seq_count, -1)

    out_proj_grad = lax.dot_general(
        by_rows(scaled_low),
        by_rows(after(mix_grad_all, scaled_value_grad)),
        ROWS_SUMMED,
        preferred_element_type=jnp.float32,
    )
    out_proj_part = bits(out_proj_grad)
    scaled_value_grad = after(scaled_value_grad, out_proj_part)
    if paired:
        out_proj_moved = seq_moved(after(out_proj_part, scaled_value_grad))
    if ordered:
        expert_moved[4] = seq_moved(after(expert_parts[4], scaled_value_grad))
    value_local, state_local, edge_value, edge_state, step_grad, taps_value, taps_state, head_grads = (
        mixer_input_back(
            pre_value,
            pre_state,
            ext_value,
            ext_state,
            step_raw,
            decay_sum,
            ssm,
            ssm_grad,
            scaled_value_grad,
            state_part_grad,
            entering,
            exit_grad,
            conv_value,
            state_taps,
            step_shift,
            decay_rate,
            skip_row,
            head_count,
        )
    )
    exact = (
        taps_value[:window],
        taps_value[window],
        head_grads[0, :head_count],
        head_grads[1, :head_count],
        head_grads[2, :head_count],
        mixer_gain_grad[0],
        taps_state[:window].T,
        taps_state[window],
    )
    flat = jnp.concatenate([part.reshape(-1) for part in exact])
    step_proj_grad = lax.dot_general(
        by_rows(normed), by_rows(step_grad), ROWS_SUMMED, preferred_element_type=jnp.float32
    )[:, :head_count]
    step_flat = step_proj_grad.reshape(-1)
    edges = shifted(jnp.concatenate([edge_value, edge_state], axis=-1), "seq", -1)
    if paired:
        flat = flat + seq_moved(flat)
        edges = after(edges, flat, out_proj_moved)
        if ordered:
            edges = after(edges, expert_moved[4])
    else:
        flat = lax.psum(flat, "seq")
    value_grad, state_grad, in_gain_grad, *last_parts = mixer_project_back(
        order,
        value_local,
        state_local,
        edges[..., :inner_width],
        edges[..., inner_width:],
        gate_grad,
        step_grad,
        sequences,
        gate_proj.T,
        value_proj.T,
        state_whole,
        step_weight,
        mp_count,
    )

    if paired:
        step_flat = step_flat + seq_moved(step_flat)
        last_parts[0] = after(last_parts[0], step_flat)
    else:
        step_flat = lax.psum(step_flat, "seq")
    kept, sent = scatter_core(*last_parts)
    if ordered:
        expert_moved[5] = seq_moved(after(expert_parts[5], value_grad))
        kept = after(kept, expert_moved[5])
    elif paired:
        expert_moved = [seq_moved(after(part, value_grad)) for part in expert_parts]
    both_proj_grad, state_proj_grad = mixer_weights(
        after(normed, sent), gate_grad, value_grad, state_grad
    )
    in_gain_grad, pair_grad = after((in_gain_grad, pair_grad), sent)
    in_gain_grad = in_gain_grad[0]
    pair_extra = pair_grad.reshape(seq_devices, mp_count, -1)

    def by_owner(value):
        return value.reshape(seq_devices, mp_count, -1)

    exact_out, at = [], 0
    for part in exact:
        exact_out.append(flat[at : at + part.size].reshape(part.shape))
        at += part.size
    mine = lax.axis_index("seq")
    conv_small = jnp.concatenate(
        [pick(by_owner(exact_out[6]), mine), pick(by_owner(exact_out[7]), mine)], axis=-1
    )
    conv_high = rounded(conv_small)
    extra = jnp.concatenate(
        [
            by_owner(state_proj_grad),
            bits(by_owner(in_gain_grad)),
            bits(by_owner(ffn_gain_grad[0])),
            pair_extra,
        ],
        axis=-1,
    )
    local_extra = extra
    last_sums, moving = scatter_deep(after(kept, extra), sent)
    extra_low = bits(seq_scatter(extra))
    extra = jnp.concatenate(
        [extra_low, bits(conv_high), bits(conv_small - conv_high)], axis=-1
    )
    extra_sent = after(extra, last_sums)
    extra = mp_exchange(extra_sent)
    tokens_grad = slots_first(
        token_rows_back(last_sums, after(hidden_grad, extra_low), own_inputs, first_gain)
    )
    cuts = [gain_rows * state_width]
    for size in (gain_rows, gain_rows, pair_extra.shape[2], conv_small.shape[1]):
        cuts.append(cuts[-1] + size)
    pair_grad = wide(extra[:, cuts[2] : cuts[3]])
    extra_own = jnp.sum(wide(jnp.concatenate([extra[:, : cuts[2]], extra[:, cuts[3] :]], axis=1)), axis=0)
    cuts = cuts[:3] + [cuts[4] - cuts[3] + cuts[2]]
    state_proj_out = extra_own[: cuts[0]].reshape(gain_rows, state_width)
    in_gain_out = extra_own[cuts[0] : cuts[1]]
    ffn_gain_out = extra_own[cuts[1] : cuts[2]]
    conv_own = extra_own[cuts[2] : cuts[3]] + extra_own[cuts[3] :]
    conv_state_out = conv_own[: state_rows * window].reshape(state_rows, window)
    conv_state_bias_out = conv_own[state_rows * window :]
    pair_grad = pair_grad.reshape(mp_count, gain_rows, 2, seq_devices, columns)
    pair_grad = pair_grad.transpose(2, 1, 3, 0, 4).reshape(2, gain_rows, -1)
    shared_gate_grad, shared_up_grad = pair_grad[0], pair_grad[1]
    if paired:
        early_sums = part_counts[0] + part_counts[1]
        expert_moved[:early_sums] = after(expert_moved[:early_sums], extra_sent)
        both_part = after(both_proj_grad, local_extra)
        both_moved = seq_moved(both_part)
        expert_moved[early_sums:], out_proj_moved, both_moved = after(
            (expert_moved[early_sums:], out_proj_moved, both_moved), tokens_grad
        )
        both_proj_grad = wide(both_part) + wide(both_moved)
        out_proj_grad = wide(out_proj_part) + wide(out_proj_moved)
        expert_sums = [wide(part) + wide(other) for part, other in zip(expert_parts, expert_moved)]
    else:
        both_proj_grad = seq_sum(both_proj_grad)
        out_proj_grad = seq_sum(out_proj_grad)
        expert_sums = [seq_sum(part) for part in expert_parts]
    gate_proj_grad, value_proj_grad = both_proj_grad[:, :inner_width], both_proj_grad[:, inner_width:]
    step_proj_grad = step_flat.reshape(step_proj_grad.shape)
    down_low = pair_down_grad[:hidden_own].reshape(seq_devices, columns, model_width)
    if paired:
        own_down, other_down = pick(down_low, mine), pick(down_low, 1 - mine)
        shared_down_grad = wide(own_down) + wide(after(seq_moved(after(other_down, tokens_grad)), both_moved))
    else:
        shared_down_grad = seq_scatter(down_low)
    one, two = part_counts[0], part_counts[0] + part_counts[1]
    expert_down_grad = jnp.concatenate(expert_sums[:one], axis=1)[None]
    expert_gate_grad = jnp.concatenate(expert_sums[one:two])[None]
    expert_up_grad = jnp.concatenate(expert_sums[two:])[None]
    return (
        block_out,
        tokens_grad,
        in_gain_out,
        gate_proj_grad,
        value_proj_grad,
        state_proj_out,
        step_proj_grad,
        exact_out[0],
        exact_out[1],
        conv_state_out,
        conv_state_bias_out,
        exact_out[2],
        exact_out[3],
        exact_out[4],
        exact_out[5],
        out_proj_grad,
        ffn_gain_out,
        shared_gate_grad,
        shared_up_grad,
        shared_down_grad,
        expert_gate_grad,
        expert_up_grad,
        expert_down_grad,
    )


def solution(mesh):
    placed = (
        P("seq", None, None),
        P(("seq", "mp"), None, None),
        P(),
        P(("seq", "mp"), None, None),
        P(("seq", "mp"), None, None),
        P(("seq", "mp")),
        P(None, "mp"),
        P(None, "mp"),
        P(("seq", "mp"), None),
        P(None, "mp"),
        P(None, "mp"),
        P("mp"),
        P(("seq", "mp"), None),
        P(("seq", "mp")),
        P("mp"),
        P("mp"),
        P("mp"),
        P("mp"),
        P("mp", None),
        P(("seq", "mp")),
        P(("seq", "mp"), None),
        P(("seq", "mp"), None),
        P(("seq", "mp"), None),
        P("mp", None, None),
        P("mp", None, None),
        P("mp", None, None),
    )
    return jax.shard_map(
        body,
        mesh=mesh,
        in_specs=placed,
        out_specs=(
            P(("seq", "mp"), None, None),
            P(("seq", "mp"), None, None),
            P(("seq", "mp")),
            P(None, "mp"),
            P(None, "mp"),
            P(("seq", "mp"), None),
            P(None, "mp"),
            P(None, "mp"),
            P("mp"),
            P(("seq", "mp"), None),
            P(("seq", "mp")),
            P("mp"),
            P("mp"),
            P("mp"),
            P("mp"),
            P("mp", None),
            P(("seq", "mp")),
            P(("seq", "mp"), None),
            P(("seq", "mp"), None),
            P(("seq", "mp"), None),
            P("mp", None, None),
            P("mp", None, None),
            P("mp", None, None),
        ),
        check_vma=False,
    )
```

```python
import jax
import jax.numpy as jnp
from jax import lax
from jax.experimental import pallas as pl
from jax.experimental.pallas import tpu as pltpu
from jax.sharding import PartitionSpec as P

STATE = 128
INNER = 3072


epsilon = 1e-05
highest = lax.Precision.HIGHEST


def shifted(block, axis, distance):
    devices = range(lax.axis_size(axis))
    route = [(i - distance, i) for i in devices if i - distance in devices]
    return lax.ppermute(block, axis, route)


def entering_2(value, axis, join, neutral, backward):
    count, mine = (lax.axis_size(axis), lax.axis_index(axis))
    pieces = jax.tree.map(lambda part: lax.all_gather(part, axis), value)
    if backward:
        pieces = jax.tree.map(lambda part: part[::-1], pieces)
        mine = count - 1 - mine
    running = jax.tree.map(
        lambda part, zero: jnp.full_like(part, 0) + jnp.asarray(zero, part.dtype), value, neutral
    )

    def hop(position, running):
        longer = join(running, jax.tree.map(lambda part: part[position], pieces))
        return jax.tree.map(lambda new, old: jnp.where(position < mine, new, old), longer, running)

    return lax.fori_loop(0, count - 1, hop, running)


def rms_scale(values, gain):
    return values * lax.rsqrt(jnp.mean(values * values, axis=-1, keepdims=True) + epsilon) * gain


def silu_slope(values):
    sigmoid_val = jax.nn.sigmoid(values)
    return sigmoid_val * (1.0 + values * (1.0 - sigmoid_val))


def chain_combine(earlier, latter):
    return (earlier[0] * latter[0], latter[0][..., None, None] * earlier[1] + latter[1])


def bits(value):
    return value.astype(jnp.bfloat16)


def wide(value):
    return value.astype(jnp.float32)


def rounded(value):
    return lax.reduce_precision(value, 8, 7)


def mp_permute(value, target):
    count = lax.axis_size("mp")
    return lax.ppermute(value, "mp", [(i, target(i)) for i in range(count)])


def across_core(value):
    return mp_permute(value, lambda i: i ^ 1)


def across_pair(value):
    return mp_permute(value, lambda i: i ^ 2)


def ring_step(value, distance=1):
    count = lax.axis_size("mp")
    return mp_permute(value, lambda i: (i + 4 * distance) % count)


def coordinates():
    mine = lax.axis_index("mp")
    return mine // 4, (mine // 2) % 2, mine % 2


def pick(value, index, axis=0):
    return lax.dynamic_index_in_dim(value, index, axis, keepdims=False)


def relative_owner():
    ring = lax.axis_size("mp") // 4
    deep, pair, core = coordinates()
    cores = jnp.arange(2)[:, None, None]
    steps = jnp.array(distances())[None, :, None]
    pairs = jnp.arange(2)[None, None, :]
    return ((deep - steps) % ring) * 4 + (pair ^ pairs) * 2 + (core ^ cores)


def gather_small(block):
    count = lax.axis_size("mp")
    every = jnp.stack([block] + [ring_step(block, step) for step in distances()[1:]])
    every = jnp.stack([every, across_pair(every)], axis=1)
    every = jnp.stack([every, across_core(every)])
    order = relative_owner().reshape(-1)
    place = jnp.zeros((count,), jnp.int32).at[order].set(jnp.arange(count, dtype=jnp.int32))
    return every.reshape((count,) + block.shape)[place]


def seq_gather(value):
    if lax.axis_size("seq") != 2:
        return lax.all_gather(value, "seq")
    other = lax.ppermute(value, "seq", [(0, 1), (1, 0)])
    first = lax.axis_index("seq") == 0
    return jnp.stack([jnp.where(first, value, other), jnp.where(first, other, value)])


def seq_scatter(value):
    if lax.axis_size("seq") != 2:
        return lax.psum_scatter(wide(value), "seq", scatter_dimension=0, tiled=False)
    mine = lax.axis_index("seq")
    other = lax.ppermute(bits(pick(value, 1 - mine)), "seq", [(0, 1), (1, 0)])
    return wide(pick(value, mine)) + wide(other)


def seq_sum(value):
    if lax.axis_size("seq") != 2:
        return lax.psum(wide(value), "seq")
    low = bits(value)
    return wide(low) + wide(lax.ppermute(low, "seq", [(0, 1), (1, 0)]))


def seq_entering(decay, state, backward):
    if lax.axis_size("seq") == 2:
        route = [(1, 0)] if backward else [(0, 1)]
        return lax.ppermute(state, "seq", route)
    return entering_2(
        (decay, state),
        "seq",
        chain_combine,
        (jnp.ones_like(decay), jnp.zeros_like(state)),
        backward,
    )[1]


def mp_exchange(value):
    return lax.all_to_all(value, "mp", split_axis=0, concat_axis=0, tiled=True)


EDGE = 16
TRANSPOSED = (((1,), (1,)), ((), ()))
ROWS_SUMMED = (((0,), (0,)), ((), ()))
PLAIN = (((1,), (0,)), ((), ()))


def product(left, right, dims=PLAIN):
    return lax.dot_general(left, right, dims, preferred_element_type=jnp.float32)


def halves_of(value):
    high = value.astype(jnp.bfloat16)
    return high, (value - high.astype(jnp.float32)).astype(jnp.bfloat16)


def fine(left, right, dims=PLAIN):
    left_high, left_low = halves_of(left)
    right_high, right_low = halves_of(right)
    small = product(left_high, right_low, dims) + product(left_low, right_high, dims)
    return product(left_high, right_high, dims) + small


def exact_right(left, right, dims=PLAIN):
    high, low = halves_of(left)
    return product(high, right, dims) + product(low, right, dims)


def exact_left(left, right, dims=PLAIN):
    high = right.astype(jnp.bfloat16)
    rest = right - high.astype(jnp.float32)
    middle = rest.astype(jnp.bfloat16)
    last = (rest - middle.astype(jnp.float32)).astype(jnp.bfloat16)
    return product(left, high, dims) + (product(left, middle, dims) + product(left, last, dims))


def softplus(value):
    return jnp.maximum(value, 0.0) + jnp.log1p(jnp.exp(-jnp.abs(value)))


def spread(value, heads, width):
    channel = width // heads
    lane = lax.broadcasted_iota(jnp.int32, (value.shape[0], width), 1)
    result = jnp.broadcast_to(value[:, heads - 1 : heads], (value.shape[0], width))
    for head in range(heads - 2, -1, -1):
        result = jnp.where(lane < (head + 1) * channel, value[:, head : head + 1], result)
    return result


def only_head(value, head, heads):
    channel = value.shape[1] // heads
    lane = lax.broadcasted_iota(jnp.int32, value.shape, 1)
    inside = (lane >= head * channel) & (lane < (head + 1) * channel)
    return jnp.where(inside, value, 0.0)


def head_sum_matrix(width, heads):
    channel = width // heads
    row = lax.broadcasted_iota(jnp.int32, (width, 128), 0) // channel
    lane = lax.broadcasted_iota(jnp.int32, (width, 128), 1)
    return (row == lane).astype(jnp.float32).astype(jnp.bfloat16)


def not_before(length, reverse=False):
    row = lax.broadcasted_iota(jnp.int32, (length, length), 0)
    lane = lax.broadcasted_iota(jnp.int32, (length, length), 1)
    return (row <= lane) if reverse else (row >= lane)


def ones_of(mask):
    return mask.astype(jnp.float32).astype(jnp.bfloat16)


def whole(shape):
    return pl.BlockSpec(shape, lambda b, *_: (0,) * len(shape))


def each(shape):
    return pl.BlockSpec((1,) + shape, lambda b, *_: (b,) + (0,) * len(shape))


def f32(*shape):
    return jax.ShapeDtypeStruct(shape, jnp.float32)


def bf16(*shape):
    return jax.ShapeDtypeStruct(shape, jnp.bfloat16)


def call(kernel, grid, in_specs, out_specs, out_shape, scratch=(), prefetch=0, micros=2):
    return pl.pallas_call(
        kernel,
        grid_spec=pltpu.PrefetchScalarGridSpec(
            num_scalar_prefetch=prefetch,
            grid=grid,
            in_specs=in_specs,
            out_specs=out_specs,
            scratch_shapes=list(scratch),
        ),
        out_shape=out_shape,
        compiler_params=pltpu.CompilerParams(vmem_limit_bytes=56 * 1024 * 1024),
        cost_estimate=pl.CostEstimate(
            flops=int(micros * 3e+08), bytes_accessed=int(micros * 8e+05), transcendentals=0
        ),
    )


def mixer_input(
    x, edge, gain, gate_w, value_w, state_w, step_w, value_taps, state_taps,
    value_bias, state_bias, step_shift, decay_rate, heads,
):
    count, length, model = x.shape
    inner, double = value_w.shape[0], state_w.shape[1]
    window = value_taps.shape[0]

    def kernel(
        x_ref, edge_ref, gain_ref, gate_ref, value_ref, state_ref, step_ref, vt_ref, st_ref,
        vb_ref, sb_ref, shift_ref, rate_ref,
        normed_out, gate_out, ev_out, es_out, pv_out, ps_out, step_out, decay_out, local_out,
    ):
        def norm(value):
            value = value.astype(jnp.float32)
            scale = lax.rsqrt(jnp.mean(value * value, axis=-1, keepdims=True) + epsilon)
            return (value * scale * gain_ref[...]).astype(jnp.bfloat16)

        normed = norm(x_ref[0])
        normed_out[0] = normed
        ev_out[0, EDGE:] = product(normed, value_ref[...], TRANSPOSED)
        es_out[0, EDGE:] = product(normed, state_ref[...])
        step_raw = product(normed, step_ref[...])
        step_out[0] = step_raw
        gate_out[0] = product(normed, gate_ref[...], TRANSPOSED)
        edge_normed = norm(edge_ref[0])
        ev_out[0, :EDGE] = product(edge_normed, value_ref[...], TRANSPOSED)
        es_out[0, :EDGE] = product(edge_normed, state_ref[...])
        first = EDGE - window + 1
        pre_value = jnp.broadcast_to(vb_ref[...], (length, inner))
        pre_state = jnp.broadcast_to(sb_ref[...], (length, double))
        for tap in range(window):
            pre_value = pre_value + vt_ref[tap : tap + 1] * ev_out[0, first + tap : first + tap + length]
            pre_state = pre_state + st_ref[tap : tap + 1] * es_out[0, first + tap : first + tap + length]
        pv_out[0] = pre_value
        ps_out[0] = pre_state
        values = jax.nn.silu(pre_value)
        b_matrix = jax.nn.silu(pre_state[:, : double // 2])
        step = softplus(step_raw + shift_ref[...])
        decay = exact_left(ones_of(not_before(length)), -jnp.exp(rate_ref[...]) * step)
        decay_out[0] = decay
        tail = jnp.exp(decay[length - 1 : length] - decay) * step
        local_out[0] = fine(values * spread(tail, heads, inner), b_matrix, ROWS_SUMMED)

    return call(
        kernel,
        (count,),
        [
            each((length, model)), each((EDGE, model)), whole(gain.shape), whole(gate_w.shape),
            whole(value_w.shape), whole(state_w.shape), whole(step_w.shape), whole(value_taps.shape),
            whole(state_taps.shape), whole(value_bias.shape), whole(state_bias.shape),
            whole(step_shift.shape), whole(decay_rate.shape),
        ],
        [
            each((length, model)), each((length, inner)), each((length + EDGE, inner)),
            each((length + EDGE, double)), each((length, inner)), each((length, double)),
            each((length, 128)), each((length, 128)), each((inner, double // 2)),
        ],
        [
            bf16(count, length, model), f32(count, length, inner), f32(count, length + EDGE, inner),
            f32(count, length + EDGE, double), f32(count, length, inner), f32(count, length, double),
            f32(count, length, 128), f32(count, length, 128), f32(count, inner, double // 2),
        ],
        micros=11,
    )(
        x, edge, gain, gate_w, value_w, state_w, step_w, value_taps, state_taps,
        value_bias, state_bias, step_shift, decay_rate,
    )


def decay_masks(decay, heads):
    length = decay.shape[0]
    causal = not_before(length)
    turned = decay.T
    return [
        jnp.exp(jnp.where(causal, decay[:, head : head + 1] - turned[head : head + 1], -1e30))
        for head in range(heads)
    ]


def mixer_within(pre_value, pre_state, step_raw, decay_sum, step_shift, skip, heads):
    count, length, inner = pre_value.shape
    double = pre_state.shape[2]

    def kernel(pv_ref, ps_ref, step_ref, decay_ref, shift_ref, skip_ref, within_out):
        values = jax.nn.silu(pv_ref[0])
        both = jax.nn.silu(ps_ref[0])
        b_matrix, c_matrix = both[:, : double // 2], both[:, double // 2 :]
        scaled = values * spread(softplus(step_ref[0] + shift_ref[...]), heads, inner)
        crossed = fine(c_matrix, b_matrix, TRANSPOSED)
        result = spread(skip_ref[...], heads, inner) * values
        for head, mask in enumerate(decay_masks(decay_ref[0], heads)):
            result = result + fine(crossed * mask, only_head(scaled, head, heads))
        within_out[0] = result

    return call(
        kernel,
        (count,),
        [
            each((length, inner)), each((length, double)), each((length, 128)), each((length, 128)),
            whole(step_shift.shape), whole(skip.shape),
        ],
        each((length, inner)),
        f32(count, length, inner),
        micros=6,
    )(pre_value, pre_state, step_raw, decay_sum, step_shift, skip)


def mixer_output(order, within, pre_state, decay_sum, entering, gate_raw, gain, out_w, heads, owners):
    count, length, inner = within.shape
    double, model = pre_state.shape[2], out_w.shape[1]
    rows = length // owners
    half = owners // 2

    def kernel(
        order_ref, within_ref, ps_ref, decay_ref, state_ref, gate_ref, gain_ref, out_ref,
        ssm_out, scaled_out, *outs,
    ):
        part_outs, mixed = outs[:-1], outs[-1]
        c_matrix = jax.nn.silu(ps_ref[0, :, double // 2 :])
        carried = fine(c_matrix, state_ref[0], TRANSPOSED)
        ssm = within_ref[0] + spread(jnp.exp(decay_ref[0]), heads, inner) * carried
        ssm_out[0] = ssm
        gated = ssm * jax.nn.silu(gate_ref[0])
        scaled = (gated * gain_ref[...]).astype(jnp.bfloat16)
        scaled_out[0] = scaled
        squares = jnp.sum(gated * gated, axis=-1, keepdims=True)
        mixed[:, :model] = product(scaled, out_ref[...]).astype(jnp.bfloat16)
        tail = jnp.zeros((length, 128), jnp.float32)
        mixed[:, model:] = two_parts(squares, tail).astype(jnp.bfloat16)
        for place in range(owners):
            start = pl.multiple_of(order_ref[place] * rows, rows)
            part_outs[place // half][place % half // 2, place % 2] = mixed[pl.ds(start, rows)]

    blocks = pl.BlockSpec((half // 2, 2, rows, model + 128), lambda b, *_: (0, 0, b, 0))
    return call(
        kernel,
        (count,),
        [
            each((length, inner)), each((length, double)), each((length, 128)),
            each((inner, double // 2)), each((length, inner)), whole(gain.shape), whole(out_w.shape),
        ],
        [each((length, inner)), each((length, inner))] + [blocks] * 2,
        [f32(count, length, inner), bf16(count, length, inner)]
        + [bf16(half // 2, 2, count * rows, model + 128)] * 2,
        [pltpu.VMEM((length, model + 128), jnp.bfloat16)],
        1,
        micros=7,
    )(order, within, pre_state, decay_sum, entering, gate_raw, gain, out_w)


def mixer_output_back(order, blocks, gate_raw, ssm, pre_state, decay_sum, gain, out_w, heads):
    count, length, inner = ssm.shape
    double, model = pre_state.shape[2], out_w.shape[1]
    owners, wide_model = len(blocks), blocks[0].shape[1]
    rows = length // owners

    def kernel(order_ref, *refs):
        blocks_ref = refs[:owners]
        gate_ref, ssm_ref, ps_ref, decay_ref, gain_ref, out_ref = refs[owners : owners + 6]
        mix_out, ssm_grad_out, gate_grad_out, state_out, gain_out, sums = refs[owners + 6 :]
        for place in range(owners):
            start = pl.multiple_of(order_ref[place] * rows, rows)
            mix_out[0, pl.ds(start, rows)] = blocks_ref[place][:, :model]
            sums[pl.ds(start, rows)] = blocks_ref[place][:, model:].astype(jnp.float32)
        sum_grad = sums[:, 0:1] + sums[:, 1:2]
        scaled_grad = product(mix_out[0], out_ref[...], TRANSPOSED)
        gate, value = gate_ref[0], ssm_ref[0]
        opened = jax.nn.silu(gate)
        gated = value * opened

        @pl.when(pl.program_id(0) == 0)
        def _():
            gain_out[...] = jnp.zeros_like(gain_out)

        gain_out[...] += jnp.sum(scaled_grad * gated, axis=0, keepdims=True)
        gated_grad = scaled_grad * gain_ref[...] + 2.0 * gated * sum_grad
        ssm_grad = gated_grad * opened
        ssm_grad_out[0] = ssm_grad
        gate_grad_out[0] = (gated_grad * value * silu_slope(gate)).astype(jnp.bfloat16)
        c_matrix = jax.nn.silu(ps_ref[0, :, double // 2 :])
        carried_grad = spread(jnp.exp(decay_ref[0]), heads, inner) * ssm_grad
        state_out[0] = fine(carried_grad, c_matrix, ROWS_SUMMED)

    return call(
        kernel,
        (count,),
        [pl.BlockSpec((rows, wide_model), lambda b, *_: (b, 0))] * owners
        + [
            each((length, inner)), each((length, inner)), each((length, double)), each((length, 128)),
            whole(gain.shape), whole(out_w.shape),
        ],
        [
            each((length, model)), each((length, inner)), each((length, inner)),
            each((inner, double // 2)), whole((8, inner)),
        ],
        [
            bf16(count, length, model), f32(count, length, inner), bf16(count, length, inner),
            f32(count, inner, double // 2), f32(8, inner),
        ],
        [pltpu.VMEM((length, wide_model - model), jnp.float32)],
        1,
        micros=8,
    )(order, *blocks, gate_raw, ssm, pre_state, decay_sum, gain, out_w)


def mixer_within_back(pre_value, pre_state, step_raw, decay_sum, step_shift, ssm_grad, entering, heads):
    count, length, inner = pre_value.shape
    double = pre_state.shape[2]

    def kernel(pv_ref, ps_ref, step_ref, decay_ref, shift_ref, grad_ref, state_ref, scaled_out, both_out):
        values = jax.nn.silu(pv_ref[0])
        both = jax.nn.silu(ps_ref[0])
        b_matrix, c_matrix = both[:, : double // 2], both[:, double // 2 :]
        scaled = values * spread(softplus(step_ref[0] + shift_ref[...]), heads, inner)
        crossed = fine(c_matrix, b_matrix, TRANSPOSED)
        grad = grad_ref[0]
        decay = decay_ref[0]
        scaled_grad = jnp.zeros((length, inner), jnp.float32)
        crossed_grad = jnp.zeros((length, length), jnp.float32)
        for head, mask in enumerate(decay_masks(decay, heads)):
            head_grad = only_head(grad, head, heads)
            scaled_grad = scaled_grad + fine(crossed * mask, head_grad, ROWS_SUMMED)
            crossed_grad = crossed_grad + fine(head_grad, scaled, TRANSPOSED) * mask
        scaled_out[0] = scaled_grad
        both_out[0, :, : double // 2] = fine(crossed_grad, c_matrix, ROWS_SUMMED)
        carried_grad = spread(jnp.exp(decay), heads, inner) * grad
        both_out[0, :, double // 2 :] = fine(crossed_grad, b_matrix) + fine(carried_grad, state_ref[0])

    return call(
        kernel,
        (count,),
        [
            each((length, inner)), each((length, double)), each((length, 128)), each((length, 128)),
            whole(step_shift.shape), each((length, inner)), each((inner, double // 2)),
        ],
        [each((length, inner)), each((length, double))],
        [f32(count, length, inner), f32(count, length, double)],
        micros=9,
    )(pre_value, pre_state, step_raw, decay_sum, step_shift, ssm_grad, entering)


def mixer_input_back(
    pre_value, pre_state, ext_value, ext_state, step_raw, decay_sum, ssm, ssm_grad, scaled_grad,
    state_part, entering, exit_grad, value_taps, state_taps, step_shift, decay_rate, skip, heads,
):
    count, length, inner = pre_value.shape
    double = pre_state.shape[2]
    window = value_taps.shape[0]

    def kernel(
        pv_ref, ps_ref, ev_ref, es_ref, step_ref, decay_ref, ssm_ref, grad_ref, scaled_ref, part_ref,
        state_ref, exit_ref, vt_ref, st_ref, shift_ref, rate_ref, skip_ref,
        value_out, state_out, edge_v_out, edge_s_out, step_out, taps_v_out, taps_s_out, head_out,
        room_v, room_s,
    ):
        pre_v, pre_s = pv_ref[0], ps_ref[0]
        values = jax.nn.silu(pre_v)
        b_matrix = jax.nn.silu(pre_s[:, : double // 2])
        grad, scaled = grad_ref[0], scaled_ref[0]
        step_pre = step_ref[0] + shift_ref[...]
        step = softplus(step_pre)
        rate = jnp.exp(rate_ref[...])
        decay = decay_ref[0]
        last = decay[length - 1 : length]
        remain = jnp.exp(last - decay)
        remain_wide = spread(remain, heads, inner)
        step_wide = spread(step, heads, inner)
        tail_wide = remain_wide * step_wide
        skip_wide = spread(skip_ref[...], heads, inner)
        leaving = exit_ref[0]
        passed = fine(b_matrix, leaving, TRANSPOSED)
        value_grad = scaled * step_wide + tail_wide * passed + skip_wide * grad
        b_grad = part_ref[0, :, : double // 2] + fine(tail_wide * values, leaving)
        summing = head_sum_matrix(inner, heads)
        crossing = values * passed
        left_part = exact_right(crossing * tail_wide, summing)
        decay_grad = (
            exact_right(grad * (ssm_ref[0] - skip_wide * values) - values * step_wide * scaled, summing)
            - left_part
        )
        total_grad = jnp.sum(left_part, axis=0, keepdims=True)
        state_dot = exact_left(jnp.ones((8, double // 2), jnp.bfloat16), leaving * state_ref[0], TRANSPOSED)
        total_grad = total_grad + jnp.exp(last) * exact_right(state_dot, summing)[:1]
        row = lax.broadcasted_iota(jnp.int32, decay_grad.shape, 0)
        decay_grad = decay_grad + jnp.where(row == length - 1, total_grad, 0.0)
        log_grad = exact_left(ones_of(not_before(length, True)), decay_grad)
        step_size_grad = exact_right(scaled * values + crossing * remain_wide, summing) - rate * log_grad
        step_raw_grad = step_size_grad * jax.nn.sigmoid(step_pre)
        step_out[0] = step_raw_grad.astype(jnp.bfloat16)
        skip_grad = exact_right(grad * values, summing)

        @pl.when(pl.program_id(0) == 0)
        def _():
            taps_v_out[...] = jnp.zeros_like(taps_v_out)
            taps_s_out[...] = jnp.zeros_like(taps_s_out)
            head_out[...] = jnp.zeros_like(head_out)
            for room in (room_v, room_s):
                room[:EDGE] = jnp.zeros((EDGE, room.shape[1]), jnp.float32)
                room[EDGE + length :] = jnp.zeros((EDGE, room.shape[1]), jnp.float32)

        head_out[0:1] += jnp.sum(step_raw_grad, axis=0, keepdims=True)
        head_out[1:2] += jnp.sum(-rate * step * log_grad, axis=0, keepdims=True)
        head_out[2:3] += jnp.sum(skip_grad, axis=0, keepdims=True)
        room_v[EDGE : EDGE + length] = value_grad * silu_slope(pre_v)
        room_s[EDGE : EDGE + length, : double // 2] = b_grad * silu_slope(pre_s[:, : double // 2])
        room_s[EDGE : EDGE + length, double // 2 :] = part_ref[0, :, double // 2 :] * silu_slope(
            pre_s[:, double // 2 :]
        )
        first = EDGE - window + 1
        for room, ext, taps, taps_out, out, edge_out in (
            (room_v, ev_ref, vt_ref, taps_v_out, value_out, edge_v_out),
            (room_s, es_ref, st_ref, taps_s_out, state_out, edge_s_out),
        ):
            pre_grad = room[EDGE : EDGE + length]
            taps_out[window : window + 1] += jnp.sum(pre_grad, axis=0, keepdims=True)
            inside = jnp.zeros(pre_grad.shape, jnp.float32)
            before = jnp.zeros((EDGE, pre_grad.shape[1]), jnp.float32)
            for tap in range(window):
                moved = ext[0, first + tap : first + tap + length]
                taps_out[tap : tap + 1] += jnp.sum(pre_grad * moved, axis=0, keepdims=True)
                ahead = window - 1 - tap
                weight = taps[tap : tap + 1]
                inside = inside + weight * room[EDGE + ahead : EDGE + ahead + length]
                before = before + weight * room[ahead : ahead + EDGE]
            out[0] = inside
            edge_out[0] = before

    return call(
        kernel,
        (count,),
        [
            each((length, inner)), each((length, double)), each((length + EDGE, inner)),
            each((length + EDGE, double)), each((length, 128)), each((length, 128)),
            each((length, inner)), each((length, inner)), each((length, inner)), each((length, double)),
            each((inner, double // 2)), each((inner, double // 2)), whole(value_taps.shape),
            whole(state_taps.shape), whole(step_shift.shape), whole(decay_rate.shape), whole(skip.shape),
        ],
        [
            each((length, inner)), each((length, double)), each((EDGE, inner)), each((EDGE, double)),
            each((length, 128)), whole((8, inner)), whole((8, double)), whole((8, 128)),
        ],
        [
            f32(count, length, inner), f32(count, length, double), f32(count, EDGE, inner),
            f32(count, EDGE, double), bf16(count, length, 128), f32(8, inner), f32(8, double), f32(8, 128),
        ],
        [
            pltpu.VMEM((length + 2 * EDGE, inner), jnp.float32),
            pltpu.VMEM((length + 2 * EDGE, double), jnp.float32),
        ],
        micros=13,
    )(
        pre_value, pre_state, ext_value, ext_state, step_raw, decay_sum, ssm, ssm_grad, scaled_grad,
        state_part, entering, exit_grad, value_taps, state_taps, step_shift, decay_rate, skip,
    )


def mixer_project_back(
    order, value_local, state_local, edge_value, edge_state, gate_grad, step_grad, x,
    gate_w, value_w, state_w, step_w, owners,
):
    count, length, inner = value_local.shape
    double, model = state_local.shape[2], x.shape[2]
    rows = length // owners
    half = owners // 2

    def kernel(
        order_ref, value_ref, state_ref, ev_ref, es_ref, gate_grad_ref, step_grad_ref, x_ref,
        gate_ref, vw_ref, sw_ref, step_ref,
        value_out, state_out, gain_out, *outs,
    ):
        part_outs, mixed = outs[:-1], outs[-1]
        body_rows = length - EDGE
        for part, edge, out in ((value_ref, ev_ref, value_out), (state_ref, es_ref, state_out)):
            out[0, :body_rows] = part[0, :body_rows].astype(jnp.bfloat16)
            out[0, body_rows:] = (part[0, body_rows:] + edge[0]).astype(jnp.bfloat16)
        grad = product(gate_grad_ref[0], gate_ref[...])
        grad = grad + product(value_out[0], vw_ref[...])
        grad = grad + product(state_out[0], sw_ref[...], TRANSPOSED)
        grad = grad + product(step_grad_ref[0], step_ref[...], TRANSPOSED)
        value = x_ref[0].astype(jnp.float32)
        scale = lax.rsqrt(jnp.mean(value * value, axis=-1, keepdims=True) + epsilon)

        @pl.when(pl.program_id(0) == 0)
        def _():
            gain_out[...] = jnp.zeros_like(gain_out)

        gain_out[...] += jnp.sum(grad * value * scale, axis=0, keepdims=True)
        mixed[...] = grad.astype(jnp.bfloat16)
        for place in range(owners):
            start = pl.multiple_of(order_ref[place] * rows, rows)
            part_outs[place // half][place % half // 2, place % 2] = mixed[pl.ds(start, rows)]

    blocks = pl.BlockSpec((half // 2, 2, rows, model), lambda b, *_: (0, 0, b, 0))
    return call(
        kernel,
        (count,),
        [
            each((length, inner)), each((length, double)), each((EDGE, inner)), each((EDGE, double)),
            each((length, inner)), each((length, 128)), each((length, model)), whole(gate_w.shape),
            whole(value_w.shape), whole(state_w.shape), whole(step_w.shape),
        ],
        [each((length, inner)), each((length, double)), whole((8, model))] + [blocks] * 2,
        [bf16(count, length, inner), bf16(count, length, double), f32(8, model)]
        + [bf16(half // 2, 2, count * rows, model)] * 2,
        [pltpu.VMEM((length, model), jnp.bfloat16)],
        1,
        micros=10,
    )(
        order, value_local, state_local, edge_value, edge_state, gate_grad, step_grad, x,
        gate_w, value_w, state_w, step_w,
    )


def total_of(refs):
    result = refs[0][...].astype(jnp.float32)
    for ref in refs[1:]:
        result = result + ref[...].astype(jnp.float32)
    return result


def two_parts(value, like):
    lane = lax.broadcasted_iota(jnp.int32, like.shape, len(like.shape) - 1)
    high = value.astype(jnp.bfloat16).astype(jnp.float32)
    return jnp.where(lane == 0, high, jnp.where(lane == 1, value - high, 0.0))


def store_sum(total, tail, out_refs):
    model = total.shape[-1] - tail
    for place, out in enumerate(out_refs):
        part = total[place] if len(out_refs) > 1 else total
        out[:, :model] = part[:, :model].astype(jnp.bfloat16)
        if tail:
            column = part[:, model : model + 1] + part[:, model + 1 : model + 2]
            out[:, model:] = two_parts(column, part[:, model:]).astype(jnp.bfloat16)


def add_pairs(left, right, tail):
    steps, _, rows, width = left.shape

    def kernel(left_ref, right_ref, *out_refs):
        for step in range(steps):
            total = left_ref[step].astype(jnp.float32) + right_ref[step].astype(jnp.float32)
            store_sum(total, tail, out_refs[2 * step : 2 * step + 2])

    sums = call(
        kernel,
        (1,),
        [whole(left.shape)] * 2,
        [whole((rows, width))] * (2 * steps),
        [bf16(rows, width)] * (2 * steps),
        micros=3,
    )(left, right)
    return list(sums[0::2]), list(sums[1::2])


def add_blocks(left, right, tail):
    def kernel(left_ref, right_ref, out_ref):
        store_sum(total_of((left_ref, right_ref)), tail, [out_ref])

    return call(
        kernel, (1,), [whole(left.shape)] * 2, whole(left.shape), bf16(*left.shape)
    )(left, right)


def after(value, *others):
    return lax.optimization_barrier((value, others))[0]


def distances():
    ring = lax.axis_size("mp") // 4
    return sorted(range(ring), key=lambda step: min(step, ring - step))


def gather_blocks(block, early=None, ties=()):
    ring = lax.axis_size("mp") // 4
    own, partner, result = [], [], None
    arrived = [block] + [ring_step(block, step) for step in distances()[1:]]
    for step, tie in enumerate(ties):
        arrived[step] = after(arrived[step], tie)
    for step, held in enumerate(arrived):
        both = [held, across_pair(held)]
        if early is not None and step == ring // 2:
            result = early(own + partner)
        if early is not None and step == ring - 1:
            partner += [across_core(value) for value in after(both, result[-1])]
        else:
            partner += [across_core(value) for value in both]
        own += both
    return own + partner, result


def scatter_core(own, partner, tail=0):
    return add_pairs(own, across_core(partner), tail)


def scatter_deep(kept, sent, tail=0):
    ring = len(kept)
    received = [across_pair(block) for block in sent]
    moving = [add_blocks(kept[step], received[step], tail) for step in range(1, ring)]
    result = [kept[0], received[0]]
    for step in range(1, ring):
        result.append(ring_step(moving[step - 1], ring - distances()[step]))
    return result, moving


def hidden_rows(parts, own_inputs, gain):
    rows, model = own_inputs.shape

    def kernel(*refs):
        part_refs, (x_ref, gain_ref, hidden_out, mix_out, inv_out, low_out) = refs[:-6], refs[-6:]
        total = total_of(part_refs)
        mixed = total[:, :model]
        squares = total[:, model : model + 1] + total[:, model + 1 : model + 2]
        inv_norm = lax.rsqrt(squares / INNER + epsilon)
        hidden = x_ref[...].astype(jnp.float32) + mixed * inv_norm
        hidden_out[...] = hidden
        mix_out[...] = mixed
        inv_out[...] = jnp.broadcast_to(inv_norm, inv_out.shape)
        low_out[...] = rms_scale(hidden, gain_ref[...]).astype(jnp.bfloat16)

    return call(
        kernel,
        (1,),
        [whole(part.shape) for part in parts] + [whole(own_inputs.shape), whole(gain.shape)],
        [whole((rows, model)), whole((rows, model)), whole((rows, 128)), whole((rows, model))],
        [f32(rows, model), f32(rows, model), f32(rows, 128), bf16(rows, model)],
    )(*parts, own_inputs, gain)


def output_rows(parts, hidden, target, valid):
    rows, model = hidden.shape

    def kernel(*refs):
        part_refs, (hidden_ref, target_ref, valid_ref, block_out, grad_out, low_out) = refs[:-6], refs[-6:]
        output = hidden_ref[...] + total_of(part_refs)
        block_out[...] = output.astype(jnp.bfloat16)
        grad = (output - target_ref[...].astype(jnp.float32)) * valid_ref[...]
        grad_out[...] = grad
        low_out[...] = grad.astype(jnp.bfloat16)

    return call(
        kernel,
        (1,),
        [whole(part.shape) for part in parts]
        + [whole(hidden.shape), whole(target.shape), whole(valid.shape)],
        [whole((rows, model))] * 3,
        [bf16(rows, model), f32(rows, model), bf16(rows, model)],
    )(*parts, hidden, target, valid)


def hidden_rows_back(parts, grad_out, hidden, mixed, inv_norm, gain):
    rows, model = hidden.shape

    def kernel(*refs):
        part_refs = refs[:-8]
        grad_ref, hidden_ref, mix_ref, inv_ref, gain_ref, hidden_out, send_out, gain_out = refs[-8:]
        input_grad = total_of(part_refs)
        value = hidden_ref[...]
        scale = lax.rsqrt(jnp.mean(value * value, axis=-1, keepdims=True) + epsilon)
        gained = input_grad * gain_ref[...]
        dot_sum = jnp.sum(gained * value, axis=-1, keepdims=True)
        grad = grad_ref[...] + scale * gained - value * (scale * scale * scale * dot_sum / model)
        hidden_out[...] = grad
        gain_out[...] = jnp.broadcast_to(
            jnp.sum(input_grad * value * scale, axis=0, keepdims=True), gain_out.shape
        )
        inv = inv_ref[:, 0:1]
        send_out[:, :model] = (grad * inv).astype(jnp.bfloat16)
        sum_grad = jnp.sum(grad * mix_ref[...], axis=-1, keepdims=True) * (-0.5 / INNER) * inv * inv * inv
        send_out[:, model:] = two_parts(sum_grad, inv_ref[...]).astype(jnp.bfloat16)

    return call(
        kernel,
        (1,),
        [whole(part.shape) for part in parts]
        + [whole(grad_out.shape), whole(hidden.shape), whole(mixed.shape), whole(inv_norm.shape), whole(gain.shape)],
        [whole((rows, model)), whole((rows, model + 128)), whole((8, model))],
        [f32(rows, model), bf16(rows, model + 128), f32(8, model)],
    )(*parts, grad_out, hidden, mixed, inv_norm, gain)


def token_rows_back(parts, hidden_grad, own_inputs, gain):
    rows, model = hidden_grad.shape

    def kernel(*refs):
        part_refs, (grad_ref, x_ref, gain_ref, out) = refs[:-4], refs[-4:]
        normed_grad = total_of(part_refs)
        value = x_ref[...].astype(jnp.float32)
        scale = lax.rsqrt(jnp.mean(value * value, axis=-1, keepdims=True) + epsilon)
        gained = normed_grad * gain_ref[...]
        dot_sum = jnp.sum(gained * value, axis=-1, keepdims=True)
        out[...] = grad_ref[...] + scale * gained - value * (scale * scale * scale * dot_sum / model)

    return call(
        kernel,
        (1,),
        [whole(part.shape) for part in parts]
        + [whole(hidden_grad.shape), whole(own_inputs.shape), whole(gain.shape)],
        whole((rows, model)),
        f32(rows, model),
    )(*parts, hidden_grad, own_inputs, gain)


def store_parts(value, out_refs):
    for place, out in enumerate(out_refs):
        size = value.shape[0] // len(out_refs)
        out[...] = value[place * size : (place + 1) * size].reshape(out.shape).astype(jnp.bfloat16)


def experts_forward(blocks, share, gate_w, up_w, down_w, pair_w, pair_down):
    rows, model = blocks[0].shape
    count, hidden = len(blocks), gate_w.shape[1]
    total, double = rows * count, pair_w.shape[1]

    def kernel(*refs):
        block_refs = refs[:count]
        share_ref, gate_ref, up_ref, down_ref, pair_ref, pd_ref = refs[count : count + 6]
        rows_out, gate_out, up_out, both_out, act_out, shared_out = refs[count + 6 : count + 12]
        part_refs = refs[count + 12 :]
        for place, block in enumerate(block_refs):
            rows_out[place * rows : (place + 1) * rows] = block[...]
        value = rows_out[...]
        gate = product(value, gate_ref[...])
        up = product(value, up_ref[...])
        gate_out[...] = gate
        up_out[...] = up
        act = (jax.nn.silu(gate) * up).astype(jnp.bfloat16)
        act_out[...] = act
        both = product(value, pair_ref[...])
        both_out[...] = both
        lane = lax.broadcasted_iota(jnp.int32, both.shape, 1)
        shared = jax.nn.silu(both) * pltpu.roll(both, double // 2, 1)
        shared = jnp.where(lane < double // 2, shared, 0.0).astype(jnp.bfloat16)
        shared_out[...] = shared
        result = product(act, down_ref[...]).astype(jnp.bfloat16).astype(jnp.float32)
        store_parts(share_ref[...] * result + product(shared, pd_ref[...]), part_refs)

    parts, steps = 2, count // 4
    return call(
        kernel,
        (1,),
        [whole(block.shape) for block in blocks]
        + [whole(w.shape) for w in (share, gate_w, up_w, down_w, pair_w, pair_down)],
        [whole((total, model)), whole((total, hidden)), whole((total, hidden)), whole((total, double))]
        + [whole((total, hidden)), whole((total, double))]
        + [whole((steps, 2, rows, model))] * parts,
        [bf16(total, model), f32(total, hidden), f32(total, hidden), f32(total, double)]
        + [bf16(total, hidden), bf16(total, double)]
        + [bf16(steps, 2, rows, model)] * parts,
        micros=8,
    )(*blocks, share, gate_w, up_w, down_w, pair_w, pair_down)


def experts_backward(blocks, share, gate, up, both, act, before, last, gate_w, up_w, down_w, pair_w, pair_down):
    rows, model = blocks[0].shape
    count, hidden = len(blocks), gate_w.shape[1]
    total, double = rows * count, pair_w.shape[1]
    others = [share, gate, up, both, act, gate_w, up_w, down_w, pair_w, pair_down]
    others += [] if before is None else [before]

    def kernel(*refs):
        block_refs = refs[:count]
        share_ref, g_ref, u_ref, both_ref, act_ref, gate_ref, up_ref, down_ref, pair_ref, pd_ref = refs[
            count : count + 10
        ]
        before_ref = None if before is None else refs[count + 10]
        grads_out, gate_out, up_out, shared_out, *outs = refs[count + len(others) :]
        for place, block in enumerate(block_refs):
            grads_out[place * rows : (place + 1) * rows] = block[...]
        grad = grads_out[...]
        routed = (share_ref[...] * grad.astype(jnp.float32)).astype(jnp.bfloat16)
        act_grad = product(routed, down_ref[...], TRANSPOSED)
        gate = g_ref[...]
        gate_out[...] = (act_grad * u_ref[...] * silu_slope(gate)).astype(jnp.bfloat16)
        up_out[...] = (act_grad * jax.nn.silu(gate)).astype(jnp.bfloat16)
        pair_value = both_ref[...]
        turned = pltpu.roll(pair_value, double // 2, 1)
        lane = lax.broadcasted_iota(jnp.int32, pair_value.shape, 1)
        factor = jnp.where(lane < double // 2, turned * silu_slope(pair_value), jax.nn.silu(turned))
        shared_out[...] = (product(grad, pd_ref[...], TRANSPOSED) * factor).astype(jnp.bfloat16)
        result = product(gate_out[...], gate_ref[...], TRANSPOSED)
        result = result + product(up_out[...], up_ref[...], TRANSPOSED)
        store_parts(result + product(shared_out[...], pair_ref[...], TRANSPOSED), outs[:2])
        down_grad = product(act_ref[...], routed, ROWS_SUMMED)
        if before_ref is not None:
            down_grad = down_grad + before_ref[...]
        outs[2][...] = down_grad.astype(outs[2].dtype)

    steps = count // 4
    return call(
        kernel,
        (1,),
        [whole(block.shape) for block in blocks] + [whole(value.shape) for value in others],
        [whole((total, model)), whole((total, hidden)), whole((total, hidden)), whole((total, double))]
        + [whole((steps, 2, rows, model))] * 2
        + [whole((hidden, model))],
        [bf16(total, model), bf16(total, hidden), bf16(total, hidden), bf16(total, double)]
        + [bf16(steps, 2, rows, model)] * 2
        + [(bf16 if last else f32)(hidden, model)],
        micros=10,
    )(*blocks, *others)


def experts_weights(groups):
    rows, grads, shared, gate_grad, up_grad, pair_grad = groups[0]
    model, hidden, double = rows.shape[1], gate_grad.shape[1], shared.shape[1]
    width = 256 if model % 256 == 0 else model
    each_group = len(groups[0])
    steps = model // width
    runs = ((4, 2), (2, 2, 2)) if steps == 6 else ((steps,), (steps,))

    def kernel(*refs):
        *piece_outs, pair_out, pair_down_out = refs[len(groups) * each_group :]
        sums = [0.0] * 4
        for group in range(len(groups)):
            x, g, sa, gg, ug, pg = refs[group * each_group : (group + 1) * each_group]
            sums[0] = sums[0] + product(x[...], gg[...], ROWS_SUMMED)
            sums[1] = sums[1] + product(x[...], ug[...], ROWS_SUMMED)
            sums[2] = sums[2] + product(x[...], pg[...], ROWS_SUMMED)
            sums[3] = sums[3] + product(sa[...], g[...], ROWS_SUMMED)
        pair_out[...] = sums[2].astype(jnp.bfloat16)
        pair_down_out[...] = sums[3].astype(jnp.bfloat16)
        number = 0
        for kind in range(2):
            first = 0
            for run in runs[kind]:
                store_piece(piece_outs[number], sums[kind], first, run)
                number, first = number + 1, first + run

    def store_piece(out, value, first, run):
        @pl.when((pl.program_id(0) >= first) & (pl.program_id(0) < first + run))
        def _():
            out[...] = value.astype(jnp.bfloat16)

    def piece_spec(first, run):
        return pl.BlockSpec((width, hidden), lambda d: (jnp.clip(d - first, 0, run - 1), 0))

    in_specs = []
    for group in groups:
        total = group[0].shape[0]
        columns = pl.BlockSpec((total, width), lambda d: (0, d))
        in_specs += [columns, columns] + [whole(value.shape) for value in group[2:]]
    out_specs, shapes = [], []
    for kind in range(2):
        first = 0
        for run in runs[kind]:
            out_specs.append(piece_spec(first, run))
            shapes.append(bf16(width * run, hidden))
            first += run
    outs = call(
        kernel,
        (steps,),
        in_specs,
        out_specs
        + [
            pl.BlockSpec((width, double), lambda d: (d, 0)),
            pl.BlockSpec((double, width), lambda d: (0, d)),
        ],
        shapes + [bf16(model, double), bf16(double, model)],
        micros=11,
    )(*[value for group in groups for value in group])
    return outs[: len(runs[0])], outs[len(runs[0]) : -2], outs[-2], outs[-1]


def mixer_weights(normed, gate_grad, value_grad, state_grad):
    count, length, model = normed.shape
    width = 256 if model % 256 == 0 else model
    inner = gate_grad.shape[2]

    def kernel(normed_ref, gate_ref, value_ref, state_ref, both_out, state_out):
        def summed(grad):
            total = 0.0
            for place in range(count):
                total = total + product(normed_ref[place], grad[place], ROWS_SUMMED)
            return total.astype(jnp.bfloat16)

        def shift(start):
            row = lax.broadcasted_iota(jnp.int32, (inner, 2 * inner), 0)
            lane = lax.broadcasted_iota(jnp.int32, (inner, 2 * inner), 1)
            return ones_of(row + start == lane)

        both = product(summed(gate_ref), shift(0)) + product(summed(value_ref), shift(inner))
        both_out[...] = both.astype(jnp.bfloat16)
        state_out[...] = summed(state_ref)

    grads = (gate_grad, value_grad, state_grad)
    return call(
        kernel,
        (model // width,),
        [pl.BlockSpec((count, length, width), lambda d: (0, 0, d))] + [whole(grad.shape) for grad in grads],
        [
            pl.BlockSpec((width, 2 * inner), lambda d: (d, 0)),
            pl.BlockSpec((width, state_grad.shape[2]), lambda d: (d, 0)),
        ],
        [bf16(model, 2 * inner), bf16(model, state_grad.shape[2])],
        micros=8,
    )(normed, *grads)


def body(
    tokens,
    target,
    lengths,
    routes,
    route_weight,
    in_gain,
    gate_proj,
    value_proj,
    state_proj,
    step_proj,
    conv_value,
    conv_value_bias,
    conv_state,
    conv_state_bias,
    step_bias,
    decay_log,
    skip_gain,
    mixer_gain,
    out_proj,
    ffn_gain,
    shared_gate,
    shared_up,
    shared_down,
    expert_gate,
    routed_up_weights,
    expert_down,
):
    mp_count = lax.axis_size("mp")
    slot_count, seq_count, model_width = tokens.shape
    seq_devices = lax.axis_size("seq")
    shared_expert_rows = slot_count // mp_count
    inner_width = gate_proj.shape[1]
    row_count = shared_expert_rows * seq_count
    window = conv_value.shape[0]
    gain_rows = in_gain.shape[0]
    state_rows = conv_state.shape[0]
    state_width = state_proj.shape[1]
    expert_count = expert_gate.shape[0] * mp_count

    packed = jnp.concatenate(
        [
            state_proj.reshape(-1),
            in_gain,
            ffn_gain,
            conv_state.reshape(-1),
            conv_state_bias,
        ]
    )
    route_rows = route_weight.transpose(1, 0, 2).reshape(row_count, -1)
    chosen = routes.transpose(1, 0, 2).reshape(row_count, -1, 1) == jnp.arange(expert_count, dtype=jnp.int32)
    coefficient = jnp.sum(jnp.where(chosen, route_rows[..., None], 0.0), axis=1)
    coefficient_high = rounded(coefficient)
    coefficient_low = coefficient - coefficient_high
    columns = shared_gate.shape[1] // (seq_devices * mp_count)
    hidden_own = seq_devices * columns
    pair_cut = jnp.stack([shared_gate, shared_up]).reshape(2, gain_rows, seq_devices, mp_count, columns)
    pair_cut = pair_cut.transpose(3, 1, 0, 2, 4).reshape(mp_count, -1)
    head_count = step_proj.shape[1]
    lane_pad = ((0, 0), (0, 128 - head_count))
    step_weight = jnp.pad(step_proj, lane_pad)
    step_shift = jnp.pad(step_bias[None], lane_pad)
    decay_rate = jnp.pad(decay_log[None], lane_pad)
    skip_row = jnp.pad(skip_gain[None], lane_pad)
    both_packed = after(seq_gather(packed), step_weight, step_shift, decay_rate, skip_row)
    small = gather_small(
        jnp.concatenate(
            [
                both_packed.reshape(-1),
                bits(coefficient_high).reshape(-1),
                bits(coefficient_low).reshape(-1),
            ]
        )
    )
    width = packed.shape[0]
    weights_small = small[:, : seq_devices * width].reshape(mp_count, seq_devices, width)
    weights_small = jnp.moveaxis(weights_small, 1, 0).reshape(seq_devices * mp_count, width)
    cut = [gain_rows * state_width]
    for part in (gain_rows, gain_rows, conv_state.size):
        cut.append(cut[-1] + part)
    state_whole = weights_small[:, : cut[0]].reshape(-1, state_width)
    gain_first = weights_small[:, cut[0] : cut[1]].reshape(-1)
    gain_second = weights_small[:, cut[1] : cut[2]].reshape(-1)
    conv_state_whole = weights_small[:, cut[2] : cut[3]].reshape(-1, window)
    conv_bias_whole = weights_small[:, cut[3] :].reshape(-1)
    share = small[:, seq_devices * width :].reshape(mp_count, 2, row_count, expert_count)
    share = lax.dynamic_index_in_dim(share, lax.axis_index("mp"), 3, keepdims=False)
    share = wide(share[:, 0]) + wide(share[:, 1])
    ring = mp_count // 4
    order = relative_owner().reshape(-1).astype(jnp.int32)
    share = share[order].reshape(2, ring, 2 * row_count)
    ring_groups = [tuple(range(ring // 2)), tuple(range(ring // 2, ring))]
    shares = [share[:, group[0] : group[-1] + 1].reshape(-1, 1) for group in ring_groups]

    gate_weight, up_weight, down_weight = expert_gate[0], routed_up_weights[0], expert_down[0]

    head_count = step_proj.shape[1]
    start_row = lax.axis_index("mp") * shared_expert_rows
    sequences = tokens.transpose(1, 0, 2)
    own_inputs = lax.dynamic_slice_in_dim(sequences, start_row, shared_expert_rows, 1)
    own_inputs = own_inputs.reshape(row_count, model_width)
    edge_rows = shifted(tokens[slot_count - window + 1 :].transpose(1, 0, 2), "seq", 1)
    edge_rows = jnp.pad(edge_rows, ((0, 0), (EDGE - window + 1, 0), (0, 0)))
    state_taps = wide(conv_state_whole).T
    mixer = mixer_input(
        sequences,
        edge_rows,
        wide(gain_first)[None],
        gate_proj.T,
        value_proj.T,
        state_whole,
        step_weight,
        conv_value,
        state_taps,
        conv_value_bias[None],
        wide(conv_bias_whole)[None],
        step_shift,
        decay_rate,
        head_count,
    )
    normed, gate_raw, ext_value, ext_state, pre_value, pre_state, step_raw, decay_sum, local_state = mixer
    decay_total = jnp.exp(decay_sum[:, slot_count - 1, :head_count])
    state_shape = (seq_count, head_count, inner_width // head_count, STATE)

    def entering_of(state, backward):
        moved = seq_entering(decay_total, state.reshape(state_shape), backward)
        return moved.reshape(state.shape)

    entering = entering_of(local_state, False)
    within = mixer_within(pre_value, pre_state, step_raw, decay_sum, step_shift, skip_row, head_count)
    ssm, scaled_low, *mix_parts = mixer_output(
        order,
        within,
        pre_state,
        decay_sum,
        entering,
        gate_raw,
        mixer_gain[None],
        out_proj,
        head_count,
        mp_count,
    )
    first_gain, second_gain = wide(gain_first)[None], wide(gain_second)[None]
    kept, sent = scatter_core(*mix_parts, 128)
    pair_moved = mp_exchange(after(pair_cut, sent))
    pair_weight = seq_gather(pair_moved).reshape(model_width, 2 * hidden_own)
    down_shared = seq_gather(after(shared_down, sent)).reshape(hidden_own, model_width)
    pair_down = jnp.concatenate([down_shared, down_shared])
    mix_sums, _ = scatter_deep(kept, sent, 128)
    hidden, pre_mix, inv_norm, ffn_input = hidden_rows(
        after(mix_sums, pair_moved), own_inputs, second_gain
    )

    def of_group(blocks, group):
        half = 2 * ring
        picked = [2 * step + side for step in group for side in (0, 1)]
        return [blocks[core * half + place] for core in (0, 1) for place in picked]

    def of_groups(parts_of_groups):
        both = [scatter_core(*parts) for parts in parts_of_groups]
        return sum([kept for kept, _ in both], []), sum([sent for _, sent in both], [])

    expert_weights = (gate_weight, up_weight, down_weight, pair_weight, pair_down)
    row_blocks, first_forward = gather_blocks(
        ffn_input, lambda blocks: experts_forward(blocks, shares[0], *expert_weights)
    )
    forwards = [
        first_forward,
        experts_forward(of_group(row_blocks, ring_groups[1]), shares[1], *expert_weights),
    ]
    position = (
        lax.axis_index("seq") * slot_count
        + start_row
        + jnp.arange(shared_expert_rows, dtype=jnp.int32)
    )
    valid_mask = (position[None, :] < lengths[:, None]).astype(jnp.float32).reshape(row_count, 1)
    block_rows, grad_out, grad_low = output_rows(
        scatter_deep(*of_groups([result[6:] for result in forwards]))[0],
        hidden,
        target.transpose(1, 0, 2).reshape(row_count, model_width),
        valid_mask,
    )

    def slots_first(value):
        return value.reshape(seq_count, shared_expert_rows, model_width).transpose(1, 0, 2)

    block_out = slots_first(block_rows)
    grad_blocks, first_backward = gather_blocks(
        grad_low,
        lambda blocks: experts_backward(
            blocks, shares[0], *forwards[0][1:5], None, False, *expert_weights
        ),
    )
    backwards = [
        first_backward,
        experts_backward(
            of_group(grad_blocks, ring_groups[1]),
            shares[1],
            *forwards[1][1:5],
            first_backward[6],
            True,
            *expert_weights,
        ),
    ]
    def seq_moved(value):
        return lax.ppermute(value, "seq", [(0, 1), (1, 0)])

    paired = seq_devices == 2
    kept, sent = of_groups([result[4:6] for result in backwards])
    down_part = backwards[1][6]
    first_row = after(forwards[0][0], sent)
    gate_parts, up_parts, pair_grad, pair_down_grad = experts_weights(
        [
            (ahead_rows, back[0], ahead[5], back[1], back[2], back[3])
            for ahead_rows, ahead, back in zip((first_row, forwards[1][0]), forwards, backwards)
        ]
    )
    expert_parts = [down_part, *gate_parts, *up_parts]
    part_counts = [1, len(gate_parts)]
    ordered = paired and len(expert_parts) == 6
    expert_moved = [None] * len(expert_parts)
    row_sums, row_moving = scatter_deep(after(kept, pair_down_grad), sent)
    mix_ties = ()
    if ordered:
        expert_moved[0] = seq_moved(expert_parts[0])
        expert_moved[1:4] = [seq_moved(after(part, row_moving)) for part in expert_parts[1:4]]
        row_sums = after(row_sums, expert_moved[0])
        mix_ties = [(), (), expert_moved[1]]
    hidden_grad, mix_grad_send, ffn_gain_grad = hidden_rows_back(
        row_sums,
        grad_out,
        hidden,
        pre_mix,
        inv_norm,
        second_gain,
    )
    mix_blocks, _ = gather_blocks(mix_grad_send, None, mix_ties)
    if ordered:
        mix_blocks = after(mix_blocks, expert_moved[2])
    mix_grad_all, ssm_grad, gate_grad, entering_grad, mixer_gain_grad = mixer_output_back(
        order,
        mix_blocks,
        gate_raw,
        ssm,
        pre_state,
        decay_sum,
        mixer_gain[None],
        out_proj,
        head_count,
    )
    exit_grad = entering_of(entering_grad, True)
    within_grad = ssm_grad
    if ordered:
        within_grad = after(ssm_grad, expert_moved[3])
    scaled_value_grad, state_part_grad = mixer_within_back(
        pre_value, pre_state, step_raw, decay_sum, step_shift, within_grad, entering, head_count
    )
    def by_rows(value):
        return value.reshape(slot_count * seq_count, -1)

    out_proj_grad = lax.dot_general(
        by_rows(scaled_low),
        by_rows(after(mix_grad_all, scaled_value_grad)),
        ROWS_SUMMED,
        preferred_element_type=jnp.float32,
    )
    out_proj_part = bits(out_proj_grad)
    scaled_value_grad = after(scaled_value_grad, out_proj_part)
    if paired:
        out_proj_moved = seq_moved(after(out_proj_part, scaled_value_grad))
    if ordered:
        expert_moved[4] = seq_moved(after(expert_parts[4], scaled_value_grad))
    value_local, state_local, edge_value, edge_state, step_grad, taps_value, taps_state, head_grads = (
        mixer_input_back(
            pre_value,
            pre_state,
            ext_value,
            ext_state,
            step_raw,
            decay_sum,
            ssm,
            ssm_grad,
            scaled_value_grad,
            state_part_grad,
            entering,
            exit_grad,
            conv_value,
            state_taps,
            step_shift,
            decay_rate,
            skip_row,
            head_count,
        )
    )
    exact = (
        taps_value[:window],
        taps_value[window],
        head_grads[0, :head_count],
        head_grads[1, :head_count],
        head_grads[2, :head_count],
        mixer_gain_grad[0],
        taps_state[:window].T,
        taps_state[window],
    )
    flat = jnp.concatenate([part.reshape(-1) for part in exact])
    step_proj_grad = lax.dot_general(
        by_rows(normed), by_rows(step_grad), ROWS_SUMMED, preferred_element_type=jnp.float32
    )[:, :head_count]
    step_flat = step_proj_grad.reshape(-1)
    edges = shifted(jnp.concatenate([edge_value, edge_state], axis=-1), "seq", -1)
    if paired:
        flat = flat + seq_moved(flat)
        edges = after(edges, flat, out_proj_moved)
        if ordered:
            edges = after(edges, expert_moved[4])
    else:
        flat = lax.psum(flat, "seq")
    value_grad, state_grad, in_gain_grad, *last_parts = mixer_project_back(
        order,
        value_local,
        state_local,
        edges[..., :inner_width],
        edges[..., inner_width:],
        gate_grad,
        step_grad,
        sequences,
        gate_proj.T,
        value_proj.T,
        state_whole,
        step_weight,
        mp_count,
    )

    if paired:
        step_flat = step_flat + seq_moved(step_flat)
        last_parts[0] = after(last_parts[0], step_flat)
    else:
        step_flat = lax.psum(step_flat, "seq")
    kept, sent = scatter_core(*last_parts)
    if ordered:
        expert_moved[5] = seq_moved(after(expert_parts[5], value_grad))
        kept = after(kept, expert_moved[5])
    elif paired:
        expert_moved = [seq_moved(after(part, value_grad)) for part in expert_parts]
    both_proj_grad, state_proj_grad = mixer_weights(
        after(normed, sent), gate_grad, value_grad, state_grad
    )
    in_gain_grad, pair_grad = after((in_gain_grad, pair_grad), sent)
    in_gain_grad = in_gain_grad[0]
    pair_extra = pair_grad.reshape(seq_devices, mp_count, -1)

    def by_owner(value):
        return value.reshape(seq_devices, mp_count, -1)

    exact_out, at = [], 0
    for part in exact:
        exact_out.append(flat[at : at + part.size].reshape(part.shape))
        at += part.size
    mine = lax.axis_index("seq")
    conv_small = jnp.concatenate(
        [pick(by_owner(exact_out[6]), mine), pick(by_owner(exact_out[7]), mine)], axis=-1
    )
    conv_high = rounded(conv_small)
    extra = jnp.concatenate(
        [
            by_owner(state_proj_grad),
            bits(by_owner(in_gain_grad)),
            bits(by_owner(ffn_gain_grad[0])),
            pair_extra,
        ],
        axis=-1,
    )
    local_extra = extra
    last_sums, moving = scatter_deep(after(kept, extra), sent)
    extra_low = bits(seq_scatter(extra))
    extra = jnp.concatenate(
        [extra_low, bits(conv_high), bits(conv_small - conv_high)], axis=-1
    )
    extra_sent = after(extra, last_sums)
    extra = mp_exchange(extra_sent)
    tokens_grad = slots_first(
        token_rows_back(last_sums, after(hidden_grad, extra_low), own_inputs, first_gain)
    )
    cuts = [gain_rows * state_width]
    for size in (gain_rows, gain_rows, pair_extra.shape[2], conv_small.shape[1]):
        cuts.append(cuts[-1] + size)
    pair_grad = wide(extra[:, cuts[2] : cuts[3]])
    extra_own = jnp.sum(wide(jnp.concatenate([extra[:, : cuts[2]], extra[:, cuts[3] :]], axis=1)), axis=0)
    cuts = cuts[:3] + [cuts[4] - cuts[3] + cuts[2]]
    state_proj_out = extra_own[: cuts[0]].reshape(gain_rows, state_width)
    in_gain_out = extra_own[cuts[0] : cuts[1]]
    ffn_gain_out = extra_own[cuts[1] : cuts[2]]
    conv_own = extra_own[cuts[2] : cuts[3]] + extra_own[cuts[3] :]
    conv_state_out = conv_own[: state_rows * window].reshape(state_rows, window)
    conv_state_bias_out = conv_own[state_rows * window :]
    pair_grad = pair_grad.reshape(mp_count, gain_rows, 2, seq_devices, columns)
    pair_grad = pair_grad.transpose(2, 1, 3, 0, 4).reshape(2, gain_rows, -1)
    shared_gate_grad, shared_up_grad = pair_grad[0], pair_grad[1]
    if paired:
        early_sums = part_counts[0] + part_counts[1]
        expert_moved[:early_sums] = after(expert_moved[:early_sums], extra_sent)
        both_part = after(both_proj_grad, local_extra)
        both_moved = seq_moved(both_part)
        expert_moved[early_sums:], out_proj_moved, both_moved = after(
            (expert_moved[early_sums:], out_proj_moved, both_moved), tokens_grad
        )
        both_proj_grad = wide(both_part) + wide(both_moved)
        out_proj_grad = wide(out_proj_part) + wide(out_proj_moved)
        expert_sums = [wide(part) + wide(other) for part, other in zip(expert_parts, expert_moved)]
    else:
        both_proj_grad = seq_sum(both_proj_grad)
        out_proj_grad = seq_sum(out_proj_grad)
        expert_sums = [seq_sum(part) for part in expert_parts]
    gate_proj_grad, value_proj_grad = both_proj_grad[:, :inner_width], both_proj_grad[:, inner_width:]
    step_proj_grad = step_flat.reshape(step_proj_grad.shape)
    down_low = pair_down_grad[:hidden_own].reshape(seq_devices, columns, model_width)
    if paired:
        own_down, other_down = pick(down_low, mine), pick(down_low, 1 - mine)
        shared_down_grad = wide(own_down) + wide(after(seq_moved(after(other_down, tokens_grad)), both_moved))
    else:
        shared_down_grad = seq_scatter(down_low)
    one, two = part_counts[0], part_counts[0] + part_counts[1]
    expert_down_grad = jnp.concatenate(expert_sums[:one], axis=1)[None]
    expert_gate_grad = jnp.concatenate(expert_sums[one:two])[None]
    expert_up_grad = jnp.concatenate(expert_sums[two:])[None]
    return (
        block_out,
        tokens_grad,
        in_gain_out,
        gate_proj_grad,
        value_proj_grad,
        state_proj_out,
        step_proj_grad,
        exact_out[0],
        exact_out[1],
        conv_state_out,
        conv_state_bias_out,
        exact_out[2],
        exact_out[3],
        exact_out[4],
        exact_out[5],
        out_proj_grad,
        ffn_gain_out,
        shared_gate_grad,
        shared_up_grad,
        shared_down_grad,
        expert_gate_grad,
        expert_up_grad,
        expert_down_grad,
    )


def solution(mesh):
    placed = (
        P("seq", None, None),
        P(("seq", "mp"), None, None),
        P(),
        P(("seq", "mp"), None, None),
        P(("seq", "mp"), None, None),
        P(("seq", "mp")),
        P(None, "mp"),
        P(None, "mp"),
        P(("seq", "mp"), None),
        P(None, "mp"),
        P(None, "mp"),
        P("mp"),
        P(("seq", "mp"), None),
        P(("seq", "mp")),
        P("mp"),
        P("mp"),
        P("mp"),
        P("mp"),
        P("mp", None),
        P(("seq", "mp")),
        P(("seq", "mp"), None),
        P(("seq", "mp"), None),
        P(("seq", "mp"), None),
        P("mp", None, None),
        P("mp", None, None),
        P("mp", None, None),
    )
    return jax.shard_map(
        body,
        mesh=mesh,
        in_specs=placed,
        out_specs=(
            P(("seq", "mp"), None, None),
            P(("seq", "mp"), None, None),
            P(("seq", "mp")),
            P(None, "mp"),
            P(None, "mp"),
            P(("seq", "mp"), None),
            P(None, "mp"),
            P(None, "mp"),
            P("mp"),
            P(("seq", "mp"), None),
            P(("seq", "mp")),
            P("mp"),
            P("mp"),
            P("mp"),
            P("mp"),
            P("mp", None),
            P(("seq", "mp")),
            P(("seq", "mp"), None),
            P(("seq", "mp"), None),
            P(("seq", "mp"), None),
            P("mp", None, None),
            P("mp", None, None),
            P("mp", None, None),
        ),
        check_vma=False,
    )
```
